32 devices in a mesh: shard: 2 (over x), ctx: 4 (over z), tensor: 4 (over y, core).
Axes of the slice: x: 2, y: 2, z: 4, core: 2. Of those that a mesh axis runs over, the one named last changes fastest.
Arguments:
- inputs: bfloat16 [1024, 8, 1024], P('ctx', 'shard'), may hold values from -6 to 6
- time_features: bfloat16 [8, 256], P('shard'), may hold values from -1 to 1
- valid_mask: int32 [1024, 8], P('ctx', 'shard'), may hold values from 0 to 1, as said below
- teacher: bfloat16 [1024, 8, 1024], P('ctx', 'shard'), may hold values from -6 to 6
- w_time: bfloat16 [256, 1024], replicated, may hold values from -0.375 to 0.375
- b_time: float32 [1024], replicated, may hold values from -2 to 2
- w_query: bfloat16 [1024, 1024], P('shard', 'tensor'), may hold values from -0.1875 to 0.1875
- b_query: float32 [1024], P('tensor'), may hold values from -2 to 2
- w_key: bfloat16 [1024, 1024], P('shard', 'tensor'), may hold values from -0.1875 to 0.1875
- w_value: bfloat16 [1024, 1024], P('shard', 'tensor'), may hold values from -0.1875 to 0.1875
- b_value: float32 [1024], P('tensor'), may hold values from -0.3 to 0.3
- w_output: bfloat16 [1024, 1024], P('shard', 'tensor'), may hold values from -1.5 to 1.5
- b_output: float32 [1024], replicated, may hold values from -2 to 2
- gain_one: float32 [1024], replicated, may hold values from 0.5 to 1.5
- shift_one: float32 [1024], replicated, may hold values from -2 to 2
- w_hidden: bfloat16 [1024, 4096], P('shard', 'tensor'), may hold values from -0.1875 to 0.1875
- b_hidden: float32 [4096], P('tensor'), may hold values from -2 to 2
- w_down: bfloat16 [1024, 4096], P('shard', 'tensor'), may hold values from -0.09375 to 0.09375
- b_down: float32 [1024], replicated, may hold values from -2 to 2
- gain_two: float32 [1024], replicated, may hold values from 0.5 to 1.5
- shift_two: float32 [1024], replicated, may hold values from -2 to 2
Outputs:
- layer_out: bfloat16 [1024, 8, 1024], P('ctx', 'shard')
- loss: float32 [], replicated
- grad_inputs: float32 [1024, 8, 1024], P('ctx', 'shard')
- grad_w_time: float32 [256, 1024], replicated
- grad_b_time: float32 [1024], replicated
- grad_w_query: float32 [1024, 1024], P(('shard', 'ctx'), 'tensor')
- grad_b_query: float32 [1024], P('tensor')
- grad_w_key: float32 [1024, 1024], P(('shard', 'ctx'), 'tensor')
- grad_w_value: float32 [1024, 1024], P(('shard', 'ctx'), 'tensor')
- grad_b_value: float32 [1024], P('tensor')
- grad_w_output: float32 [1024, 1024], P(('shard', 'ctx'), 'tensor')
- grad_b_output: float32 [1024], replicated
- grad_gain_one: float32 [1024], replicated
- grad_shift_one: float32 [1024], replicated
- grad_w_hidden: float32 [1024, 4096], P(('shard', 'ctx'), 'tensor')
- grad_b_hidden: float32 [4096], P('tensor')
- grad_w_down: float32 [1024, 4096], P(('shard', 'ctx'), 'tensor')
- grad_b_down: float32 [1024], replicated
- grad_gain_two: float32 [1024], replicated
- grad_shift_two: float32 [1024], replicated
The draws below stay inside these ranges and needn't reach their ends.
Inputs may be any that keep to these rules, and one draw needn't show every extreme that they name: `valid_mask`: 0 or 1; the last token of every sequence is valid.
All inputs are finite; a program needn't handle non-finite values.
Results may differ from the reference program's by a relative error of at most 0.018.
Values may be sent and summed in bfloat16 or wider, within the bound.
No kernel may reach another device: no remote copies, remote signals or barrier semaphores. Data moves between devices by JAX's collectives and lax.ppermute only.
A program may use at most 256 MiB of HBM per device.

```python
import math
import jax
import jax.numpy as jnp
from jax import lax

D = 1024
HEADS = 16
FF = 4096
TF = 256
HD = 64
LENGTH = 1024
SEQS = 8
TOKENS = 8192


def draw_valid_mask(key, part):
    place = jnp.arange(LENGTH, dtype=jnp.int32)[:, None]
    sequence = jnp.arange(SEQS, dtype=jnp.int32)[None, :]
    order = (sequence * LENGTH + place) // SEQS
    ticket = jax.random.randint(key, (LENGTH, SEQS), 0, LENGTH, dtype=jnp.int32)
    chosen = ticket < (LENGTH + 9 * order) // 10 + 1
    return jnp.logical_or(chosen, place == LENGTH - 1).astype(jnp.int32)


def level_of(stream_key, extent, cuts, smallest, top_value):
    factor_of = 1.0
    for dim, shards_of in cuts:
        heights = jax.random.uniform(jax.random.fold_in(jax.random.fold_in(stream_key, 6), dim), (shards_of,), jnp.float32, smallest / len(cuts), top_value / len(cuts))
        factor_of = factor_of * jnp.repeat(jnp.exp(heights), extent[dim] // shards_of).reshape((-1,) + (1,) * (len(extent) - 1 - dim))
    return factor_of


def noise(stream_key, shape, width, reach, split=(), kind=jnp.bfloat16):
    factor_of = level_of(stream_key, shape, split, -0.22, 0.18) if split else 1.0
    entries = jax.random.normal(stream_key, shape, jnp.float32) * width * factor_of
    return jnp.minimum(jnp.maximum(entries, -reach), reach).astype(kind)


def setup_inputs(seed: int = 0) -> dict:
    arg_keys = jax.random.split(jax.random.key(seed), 22)
    return {
        "inputs": noise(arg_keys[0], (LENGTH, SEQS, D), 1.0, 6.0, ((0, 4), (1, 2))),
        "time_features": jnp.clip(jax.random.uniform(arg_keys[1], (SEQS, TF), jnp.float32, -1.0, 1.0) * level_of(arg_keys[1], (SEQS, TF), ((0, 2),), -0.4, 0.0), -1.0, 1.0).astype(jnp.bfloat16),
        "valid_mask": draw_valid_mask(jax.random.fold_in(arg_keys[21], 71), 0),
        "teacher": noise(arg_keys[3], (LENGTH, SEQS, D), 1.0, 6.0, ((0, 4), (1, 2))),
        "w_time": noise(arg_keys[4], (TF, D), TF ** -0.5, 0.375),
        "b_time": noise(arg_keys[5], (D,), 0.3, 2.0, (), jnp.float32),
        "w_query": noise(arg_keys[6], (D, D), D ** -0.5, 0.1875, ((0, 2), (1, 4))),
        "b_query": noise(arg_keys[7], (D,), 0.3, 2.0, ((0, 4),), jnp.float32),
        "w_key": noise(arg_keys[8], (D, D), D ** -0.5, 0.1875, ((0, 2), (1, 4))),
        "w_value": noise(arg_keys[9], (D, D), D ** -0.5, 0.1875, ((0, 2), (1, 4))),
        "b_value": noise(arg_keys[10], (D,), 0.05, 0.3, ((0, 4),), jnp.float32),
        "w_output": noise(arg_keys[11], (D, D), (16 * D // LENGTH) ** -0.5, 1.5, ((0, 2), (1, 4))),
        "b_output": noise(arg_keys[12], (D,), 0.3, 2.0, (), jnp.float32),
        "gain_one": jnp.clip(1.0 + 0.1 * jax.random.normal(arg_keys[13], (D,), jnp.float32), 0.5, 1.5),
        "shift_one": noise(arg_keys[14], (D,), 0.3, 2.0, (), jnp.float32),
        "w_hidden": noise(arg_keys[15], (D, FF), D ** -0.5, 0.1875, ((0, 2), (1, 4))),
        "b_hidden": noise(arg_keys[16], (FF,), 0.3, 2.0, ((0, 4),), jnp.float32),
        "w_down": noise(arg_keys[17], (D, FF), FF ** -0.5, 0.09375, ((0, 2), (1, 4))),
        "b_down": noise(arg_keys[18], (D,), 0.3, 2.0, (), jnp.float32),
        "gain_two": jnp.clip(1.0 + 0.1 * jax.random.normal(arg_keys[19], (D,), jnp.float32), 0.5, 1.5),
        "shift_two": noise(arg_keys[20], (D,), 0.3, 2.0, (), jnp.float32),
    }


@jax.custom_vjp
def low(v):
    return lax.optimization_barrier(v.astype(jnp.bfloat16)).astype(jnp.float32)

@jax.custom_vjp
def low_back(v):
    return v

def low_keep(v):
    return (low(v), None)

def low_pass(kept, grad):
    return (grad,)

def back_keep(v):
    return (v, None)

def back_low(kept, grad):
    return (low(grad),)
low.defvjp(low_keep, low_pass)
low_back.defvjp(back_keep, back_low)
exact = lax.Precision.HIGHEST

def rounded_both(value):
    return low(low_back(value))

def layer_norm(value, gain, shift):
    center = lax.optimization_barrier(jnp.mean(value, axis=-1, keepdims=True))
    offset = value - center
    spread = lax.optimization_barrier(jnp.mean(offset * offset, axis=-1, keepdims=True))
    return offset * lax.rsqrt(spread + 1e-05) * gain + shift

def attend(query, key, value):
    groups = query.shape[0]
    block = math.gcd(LENGTH, 512)
    blocks = query.reshape(groups, LENGTH // block, block, HEADS, HD).transpose(1, 0, 2, 3, 4)
    scale = 1.0 / math.sqrt(HD)

    def one_block(rows_in):
        scores = low_back(jnp.einsum('gqhd,gkhd->ghqk', rows_in, key, precision=exact) * scale)
        weights = jax.nn.softmax(scores, axis=-1)
        return jnp.einsum('ghqk,gkhd->gqhd', low(weights), value, precision=exact)
    result = lax.map(jax.checkpoint(one_block), blocks)
    return result.transpose(1, 0, 2, 3, 4).reshape(groups, LENGTH, HEADS * HD)

def forward(params, inputs, features, valid, target, count):
    w_time, b_time, w_query, b_query, w_key, w_value, b_value, w_output, b_output, gain_one, shift_one, w_hidden, b_hidden, w_down, b_down, gain_two, shift_two = params
    groups = inputs.shape[0]
    embed = jnp.dot(features, w_time, precision=exact) + b_time
    start = inputs + embed[:, None, :]
    start_low = low(start)
    query = rounded_both(jnp.dot(start_low, w_query, precision=exact) + b_query)
    key = rounded_both(jnp.dot(start_low, w_key, precision=exact))
    value = rounded_both(jnp.dot(start_low, w_value, precision=exact) + b_value)
    mixed = attend(query.reshape(groups, LENGTH, HEADS, HD), key.reshape(groups, LENGTH, HEADS, HD), value.reshape(groups, LENGTH, HEADS, HD))
    mixed = rounded_both(mixed)
    branch = low_back(jnp.dot(mixed, w_output.T, precision=exact) + b_output)
    normed = layer_norm(start + branch, gain_one, shift_one)
    normed_low = low(normed)
    pre_act = low_back(jnp.dot(normed_low, w_hidden, precision=exact) + b_hidden)
    hidden = low(jax.nn.gelu(pre_act, approximate=False))
    feed = low_back(jnp.dot(hidden, w_down.T, precision=exact) + b_down)
    result = layer_norm(normed + feed, gain_two, shift_two)
    error = result - target
    squares = jnp.sum(valid[..., None] * error * error)
    return (squares * (TOKENS / count), (result, squares))

def reference(inputs, time_features, valid_mask, teacher, w_time, b_time, w_query, b_query, w_key, w_value, b_value, w_output, b_output, gain_one, shift_one, w_hidden, b_hidden, w_down, b_down, gain_two, shift_two):
    count = jnp.sum(valid_mask).astype(jnp.float32)
    params = tuple((item.astype(jnp.float32) for item in (w_time, b_time, w_query, b_query, w_key, w_value, b_value, w_output, b_output, gain_one, shift_one, w_hidden, b_hidden, w_down, b_down, gain_two, shift_two)))
    group = math.gcd(SEQS, max(1, 4096 // LENGTH))
    steps_count = SEQS // group
    states = inputs.astype(jnp.float32).transpose(1, 0, 2).reshape(steps_count, group, LENGTH, D)
    targets = teacher.astype(jnp.float32).transpose(1, 0, 2).reshape(steps_count, group, LENGTH, D)
    valids = valid_mask.astype(jnp.float32).transpose(1, 0).reshape(steps_count, group, LENGTH)
    feats = time_features.astype(jnp.float32).reshape(steps_count, group, TF)
    zeros = tuple((jnp.zeros_like(item) for item in params))

    def step(carry, item):
        grads, total = carry
        state, feat, valid, target = item

        def local_fn(weights, state_in):
            return forward(weights, state_in, feat, valid, target, count)
        scaled, back_fn, extra = jax.vjp(local_fn, params, state, has_aux=True)
        grad_params, grad_state = back_fn(jnp.ones_like(scaled))
        grads = jax.tree.map(lambda left, right: left + right, grads, grad_params)
        return ((grads, total + extra[1]), (extra[0], grad_state))
    (grads, total), (results, grad_states) = lax.scan(step, (zeros, jnp.zeros((), jnp.float32)), (states, feats, valids, targets))
    layer_out = results.reshape(SEQS, LENGTH, D).transpose(1, 0, 2).astype(jnp.bfloat16)
    grad_inputs = grad_states.reshape(SEQS, LENGTH, D).transpose(1, 0, 2)
    loss = total / (D * count)
    return (layer_out, loss, grad_inputs, grads[0], grads[1], grads[2], grads[3], grads[4], grads[5], grads[6], grads[7], grads[8], grads[9], grads[10], grads[11], grads[12], grads[13], grads[14], grads[15], grads[16])
```

```python
from functools import partial
import math

import jax
import jax.numpy as jnp
from jax import lax
from jax.experimental import pallas as pl
from jax.experimental.pallas import tpu as pltpu
from jax.sharding import PartitionSpec as P

D = 1024
HEADS = 16
BF = jnp.bfloat16
F32 = jnp.float32
PAIR = 128
EPS = 1e-05


def contract(left, right, left_dim, right_dim):
    return lax.dot_general(
        left, right, (((left_dim,), (right_dim,)), ((), ())), preferred_element_type=F32
    )


def params(**kwargs):
    return pltpu.CompilerParams(vmem_limit_bytes=48 << 20, **kwargs)


def cost(flops, nbytes, exps=0):
    return pl.CostEstimate(flops=flops, bytes_accessed=nbytes, transcendentals=exps)


def swap(value, axis, bit):
    size = lax.axis_size(axis)
    return lax.ppermute(value, axis, [(i, i ^ bit) for i in range(size)])


def swap_core(value):
    return swap(value, "tensor", 1)


def swap_outer(value):
    return swap(value, "tensor", 2)


def swap_shard(value):
    return swap(value, "shard", 1)


def sum_ctx(value):
    size = lax.axis_size("ctx")
    if size & (size - 1):
        return lax.psum(value, "ctx")
    bit = 1
    while bit < size:
        value = value + swap(value, "ctx", bit)
        bit *= 2
    return value


def sum_tokens(value):
    return sum_ctx(value + swap_shard(value))


def turned(value, flip):
    half = value.shape[1] // 2
    return jnp.where(flip == 0, value, jnp.concatenate([value[:, half:], value[:, :half]], axis=1))


def entry_kernel(chunks, place, x_ref, embed_ref, low_ref, start_ref):
    core, flip = place[0], place[1]
    x = x_ref[...].astype(F32)
    rows = [x[:, s, :] + embed_ref[s : s + 1, :] for s in range(2 * chunks)]
    for c in range(chunks):
        first, second = rows[2 * c], rows[2 * c + 1]
        own = turned(jnp.where(core == 0, first, second), flip)
        other = turned(jnp.where(core == 0, second, first), flip)
        low_ref[c, 0] = own.astype(BF)
        low_ref[c, 1] = other.astype(BF)
        start_ref[c] = own


def entry(place, x, embed):
    positions, seqs, width = x.shape
    chunks = seqs // 2
    block = min(64, positions)
    return pl.pallas_call(
        partial(entry_kernel, chunks),
        grid_spec=pltpu.PrefetchScalarGridSpec(
            num_scalar_prefetch=1,
            grid=(positions // block,),
            in_specs=[
                pl.BlockSpec((block, seqs, width), lambda i, s: (i, 0, 0)),
                pl.BlockSpec((seqs, width), lambda i, s: (0, 0)),
            ],
            out_specs=[
                pl.BlockSpec((chunks, 2, block, width), lambda i, s: (0, 0, i, 0)),
                pl.BlockSpec((chunks, block, width), lambda i, s: (0, i, 0)),
            ],
        ),
        out_shape=[
            jax.ShapeDtypeStruct((chunks, 2, positions, width), BF),
            jax.ShapeDtypeStruct((chunks, positions, width), F32),
        ],
        cost_estimate=cost(4 * x.size, 6 * x.size),
        compiler_params=params(),
        name="entry",
    )(place, x, embed)


def own_kernel(chunks, place, x_ref, out_ref):
    core, flip = place[0], place[1]
    x = x_ref[...].astype(F32)
    for c in range(chunks):
        own = jnp.where(core == 0, x[:, 2 * c, :], x[:, 2 * c + 1, :])
        out_ref[c] = turned(own, flip).astype(BF)


def own_rows(place, x):
    positions, seqs, width = x.shape
    chunks = seqs // 2
    block = min(64, positions)
    return pl.pallas_call(
        partial(own_kernel, chunks),
        grid_spec=pltpu.PrefetchScalarGridSpec(
            num_scalar_prefetch=1,
            grid=(positions // block,),
            in_specs=[pl.BlockSpec((block, seqs, width), lambda i, s: (i, 0, 0))],
            out_specs=pl.BlockSpec((chunks, block, width), lambda i, s: (0, i, 0)),
        ),
        out_shape=jax.ShapeDtypeStruct((chunks, positions, width), BF),
        cost_estimate=cost(2 * x.size, 3 * x.size),
        compiler_params=params(),
        name="own_rows",
    )(place, x)


def leave_kernel(chunks, dtype, place, own_ref, other_ref, out_ref):
    core, flip = place[0], place[1]
    rows = []
    for c in range(chunks):
        own = turned(own_ref[c].astype(F32), flip)
        other = turned(other_ref[c].astype(F32), flip)
        rows += [jnp.where(core == 0, own, other), jnp.where(core == 0, other, own)]
    out_ref[...] = jnp.stack(rows, axis=1).astype(dtype)


def leave(place, own, other):
    chunks, positions, width = own.shape
    block = min(64, positions)
    spec = pl.BlockSpec((chunks, block, width), lambda i, s: (0, i, 0))
    return pl.pallas_call(
        partial(leave_kernel, chunks, own.dtype),
        grid_spec=pltpu.PrefetchScalarGridSpec(
            num_scalar_prefetch=1,
            grid=(positions // block,),
            in_specs=[spec, spec],
            out_specs=pl.BlockSpec((block, 2 * chunks, width), lambda i, s: (i, 0, 0)),
        ),
        out_shape=jax.ShapeDtypeStruct((positions, 2 * chunks, width), own.dtype),
        cost_estimate=cost(2 * own.size, 4 * own.size * own.dtype.itemsize),
        compiler_params=params(),
        name="leave",
    )(place, own, other)


def lanes_of(part):
    lane = lax.broadcasted_iota(jnp.int32, (1, PAIR), 1)
    return lane < PAIR // 2 if part == 0 else lane >= PAIR // 2


def attend_kernel(scale, q_ref, kv_ref, out_ref, log_ref):
    q = q_ref[:, 0:PAIR] * BF(scale)
    k, v = kv_ref[:, PAIR : 2 * PAIR], kv_ref[:, 2 * PAIR : 3 * PAIR]
    mixed = None
    for part in range(2):
        lanes = lanes_of(part)
        k_head, v_head = jnp.where(lanes, k, BF(0)), jnp.where(lanes, v, BF(0))
        scores = contract(k_head, q, 1, 1)
        peak = jnp.max(scores, axis=0, keepdims=True)
        weights = jnp.exp(scores - peak)
        total = jnp.sum(weights, axis=0, keepdims=True)
        term = contract(v_head, weights.astype(BF), 0, 0) * (1.0 / total)
        mixed = term if mixed is None else mixed + term
        log_ref[part : part + 1, :] = peak + jnp.log(total)
    out_ref[...] = mixed.T.astype(BF)


def attend(qkv, scale):
    length = qkv.shape[0]
    block = math.gcd(length, 1024)
    return pl.pallas_call(
        partial(attend_kernel, scale),
        grid=(length // block,),
        in_specs=[
            pl.BlockSpec((block, 3 * PAIR), lambda i: (i, 0)),
            pl.BlockSpec((length, 3 * PAIR), lambda i: (0, 0)),
        ],
        out_specs=[
            pl.BlockSpec((block, PAIR), lambda i: (i, 0)),
            pl.BlockSpec((2, block), lambda i: (0, i)),
        ],
        out_shape=[
            jax.ShapeDtypeStruct((length, PAIR), BF),
            jax.ShapeDtypeStruct((2, length), F32),
        ],
        cost_estimate=cost(8 * length * length * PAIR, 8 * length * PAIR, 2 * length * length),
        compiler_params=params(),
        name="attend",
    )(qkv, qkv)


def attend_back_kernel(scale, block, blocks, q_ref, kv_ref, grad_ref, log_ref, out_ref, k_sum, v_sum):
    step = pl.program_id(0)

    @pl.when(step == 0)
    def _():
        k_sum[...] = jnp.zeros_like(k_sum)
        v_sum[...] = jnp.zeros_like(v_sum)

    q = q_ref[:, 0:PAIR] * BF(scale)
    k, v = kv_ref[:, PAIR : 2 * PAIR], kv_ref[:, 2 * PAIR : 3 * PAIR]
    grad = grad_ref[...]
    q_grad = None
    for part in range(2):
        lanes = lanes_of(part)
        k_head, v_head = jnp.where(lanes, k, BF(0)), jnp.where(lanes, v, BF(0))
        q_head, grad_head = jnp.where(lanes, q, BF(0)), jnp.where(lanes, grad, BF(0))
        probs = jnp.exp(contract(k_head, q, 1, 1) - log_ref[part : part + 1, :])
        probs_grad = contract(v_head, grad, 1, 1)
        delta = jnp.sum(probs * probs_grad, axis=0, keepdims=True)
        scores_grad = (probs * (probs_grad - delta)).astype(BF)
        v_sum[...] += contract(probs.astype(BF), grad_head, 1, 0)
        k_sum[...] += contract(scores_grad, q_head, 1, 0)
        term = contract(k_head, scores_grad, 0, 0)
        q_grad = term if q_grad is None else q_grad + term
    rows = pl.ds(pl.multiple_of(step * block, block), block)
    out_ref[rows, 0:PAIR] = (q_grad * scale).T.astype(BF)

    @pl.when(step == blocks - 1)
    def _():
        out_ref[:, PAIR : 2 * PAIR] = k_sum[...].astype(BF)
        out_ref[:, 2 * PAIR : 3 * PAIR] = v_sum[...].astype(BF)


def attend_back(qkv, grad, logs, scale):
    length = qkv.shape[0]
    block = math.gcd(length, 512)
    return pl.pallas_call(
        partial(attend_back_kernel, scale, block, length // block),
        grid=(length // block,),
        in_specs=[
            pl.BlockSpec((block, 3 * PAIR), lambda i: (i, 0)),
            pl.BlockSpec((length, 3 * PAIR), lambda i: (0, 0)),
            pl.BlockSpec((block, PAIR), lambda i: (i, 0)),
            pl.BlockSpec((2, block), lambda i: (0, i)),
        ],
        out_specs=pl.BlockSpec((length, 3 * PAIR), lambda i: (0, 0)),
        out_shape=jax.ShapeDtypeStruct((length, 3 * PAIR), BF),
        scratch_shapes=[pltpu.VMEM((length, PAIR), F32)] * 2,
        cost_estimate=cost(20 * length * length * PAIR, 18 * length * PAIR, 2 * length * length),
        compiler_params=params(),
        name="attend_back",
    )(qkv, qkv, grad, logs)


def normal(value):
    center = jnp.mean(value, axis=-1, keepdims=True)
    offset = value - center
    spread = jnp.mean(offset * offset, axis=-1, keepdims=True)
    inverse = lax.rsqrt(spread + EPS)
    return offset * inverse, inverse


def normal_back(grad, unit, inverse):
    return inverse * (
        grad
        - jnp.mean(grad, axis=-1, keepdims=True)
        - unit * jnp.mean(grad * unit, axis=-1, keepdims=True)
    )


def add_sums(sums_ref, rows):
    @pl.when(pl.program_id(0) == 0)
    def _():
        sums_ref[...] = jnp.zeros_like(sums_ref)

    for i, value in enumerate(rows):
        sums_ref[i : i + 1, :] += jnp.sum(value, axis=0, keepdims=True)


def first_norm_kernel(start_ref, mine_ref, theirs_ref, vec_ref, sum_ref, low_ref):
    total = start_ref[...] + mine_ref[...].astype(F32) + theirs_ref[...].astype(F32) + vec_ref[0:1, :]
    sum_ref[...] = total
    unit, inverse = normal(total)
    low_ref[...] = (unit * vec_ref[1:2, :] + vec_ref[2:3, :]).astype(BF)


def second_norm_kernel(first_ref, mine_ref, theirs_ref, vec_ref, teacher_ref, valid_ref, out_ref, grad_ref, low_ref, sums_ref):
    unit, inverse = normal(first_ref[...])
    normed = unit * vec_ref[1:2, :] + vec_ref[2:3, :]
    total = normed + mine_ref[...].astype(F32) + theirs_ref[...].astype(F32) + vec_ref[3:4, :]
    unit, inverse = normal(total)
    result = unit * vec_ref[4:5, :] + vec_ref[5:6, :]
    out_ref[...] = result.astype(BF)
    error = result - teacher_ref[...].astype(F32)
    result_grad = valid_ref[:, 0:1] * error
    grad = normal_back(result_grad * vec_ref[4:5, :], unit, inverse)
    grad_ref[...] = grad
    low = grad.astype(BF)
    low_ref[...] = low
    add_sums(
        sums_ref,
        (result_grad * unit, result_grad, low.astype(F32), valid_ref[:, 1:2] * error * error),
    )


def first_back_kernel(grad_ref, mine_ref, theirs_ref, first_ref, vec_ref, out_ref, low_ref, sums_ref):
    grad = grad_ref[...] + mine_ref[...].astype(F32) + theirs_ref[...].astype(F32)
    unit, inverse = normal(first_ref[...])
    out = normal_back(grad * vec_ref[1:2, :], unit, inverse)
    out_ref[...] = out
    low = out.astype(BF)
    low_ref[...] = low
    add_sums(sums_ref, (grad * unit, grad, low.astype(F32)))


def last_kernel(grad_ref, mine_ref, theirs_ref, out_ref, sums_ref):
    grad = grad_ref[...] + mine_ref[...].astype(F32) + theirs_ref[...].astype(F32)
    out_ref[...] = grad
    add_sums(sums_ref, (grad,))


def row_call(kernel, name, args, out_dtypes, sums):
    rows, width = args[0].shape
    block = math.gcd(rows, 128)
    full = lambda a: pl.BlockSpec(a.shape, lambda i: (0, 0))
    tall = lambda a: pl.BlockSpec((block, a.shape[1]), lambda i: (i, 0))
    out_specs = [pl.BlockSpec((block, width), lambda i: (i, 0)) for _ in out_dtypes]
    out_shape = [jax.ShapeDtypeStruct((rows, width), d) for d in out_dtypes]
    if sums:
        out_specs.append(pl.BlockSpec((8, width), lambda i: (0, 0)))
        out_shape.append(jax.ShapeDtypeStruct((8, width), F32))
    return pl.pallas_call(
        kernel,
        grid=(rows // block,),
        in_specs=[full(a) if a.shape[0] == 8 else tall(a) for a in args],
        out_specs=out_specs,
        out_shape=out_shape,
        cost_estimate=cost(40 * rows * width, 16 * rows * width),
        compiler_params=params(),
        name=name,
    )(*args)


def spread_units(value):
    pairs, seqs, positions, columns = value.shape
    units = value.reshape(pairs * seqs, positions, columns)
    out = lax.all_to_all(units, "ctx", 0, 0)
    return out.reshape(pairs * seqs * positions, columns)


def collect_units(value, pairs, seqs):
    units = pairs * seqs
    out = lax.all_to_all(value.reshape(units, value.shape[0] // units, -1), "ctx", 0, 0)
    return out.reshape(pairs, seqs, out.shape[1], out.shape[2])


def heads_of(value):
    return value.reshape(value.shape[:-1] + (2, PAIR // 2))


def gathered_forward(qkv, scale):
    queries = heads_of(qkv[..., :PAIR])
    both = lax.all_gather(qkv[..., PAIR:], "ctx", axis=2, tiled=True)
    length = both.shape[2]
    block = math.gcd(length, 512)
    blocks = jnp.moveaxis(both.reshape(both.shape[:2] + (length // block, block, 2 * PAIR)), 2, 0)
    shape = queries.shape[:-1]

    def step(carry, piece):
        peak, total, summed = carry
        keys, values = heads_of(piece[..., :PAIR]), heads_of(piece[..., PAIR:])
        scores = jnp.einsum("gsqhd,gskhd->gsqhk", queries, keys, preferred_element_type=F32) * scale
        new_peak = jnp.maximum(peak, jnp.max(scores, axis=-1))
        fade = jnp.exp(peak - new_peak)
        weights = jnp.exp(scores - new_peak[..., None])
        total = total * fade + jnp.sum(weights, axis=-1)
        summed = summed * fade[..., None] + jnp.einsum(
            "gsqhk,gskhd->gsqhd", weights.astype(BF), values, preferred_element_type=F32
        )
        return (new_peak, total, summed), None

    first = (
        jnp.full(shape, -1e30, F32),
        jnp.zeros(shape, F32),
        jnp.zeros(queries.shape, F32),
    )
    (peak, total, summed), _ = lax.scan(step, first, blocks)
    attended = summed / total[..., None]
    mixed = attended.reshape(qkv.shape[:-1] + (PAIR,)).astype(BF)
    return mixed, (queries, blocks, peak + jnp.log(total), attended)


def gathered_backward(saved, grad, scale):
    queries, blocks, logs, attended = saved
    out_grad = heads_of(grad)
    delta = jnp.sum(out_grad.astype(F32) * attended, axis=-1)

    def step(q_grad, piece):
        keys, values = heads_of(piece[..., :PAIR]), heads_of(piece[..., PAIR:])
        scores = jnp.einsum("gsqhd,gskhd->gsqhk", queries, keys, preferred_element_type=F32) * scale
        weights = jnp.exp(scores - logs[..., None])
        weight_grad = jnp.einsum(
            "gsqhd,gskhd->gsqhk", out_grad, values, preferred_element_type=F32
        )
        score_grad = (weights * (weight_grad - delta[..., None])).astype(BF)
        v_grad = jnp.einsum(
            "gsqhk,gsqhd->gskhd", weights.astype(BF), out_grad, preferred_element_type=F32
        )
        k_grad = jnp.einsum("gsqhk,gsqhd->gskhd", score_grad, queries, preferred_element_type=F32)
        q_grad = q_grad + scale * jnp.einsum(
            "gsqhk,gskhd->gsqhd", score_grad, keys, preferred_element_type=F32
        )
        flat = lambda a: a.reshape(a.shape[:-2] + (PAIR,))
        return q_grad, jnp.concatenate([flat(k_grad) * scale, flat(v_grad)], axis=-1).astype(BF)

    q_grad, joined = lax.scan(step, jnp.zeros(queries.shape, F32), blocks)
    joined = jnp.moveaxis(joined, 0, 2)
    joined = joined.reshape(joined.shape[:2] + (-1, 2 * PAIR))
    owned = lax.psum_scatter(joined, "ctx", scatter_dimension=2, tiled=True)
    return jnp.concatenate([q_grad.reshape(grad.shape).astype(BF), owned], axis=-1)


def body(
    inputs,
    time_features,
    valid_mask,
    teacher,
    w_time,
    b_time,
    w_query,
    b_query,
    w_key,
    w_value,
    b_value,
    w_output,
    b_output,
    gain_one,
    shift_one,
    w_hidden,
    b_hidden,
    w_down,
    b_down,
    gain_two,
    shift_two,
):
    positions, seqs, width = inputs.shape
    half = width // 2
    chunks = seqs // 2
    columns = w_query.shape[1]
    pairs = columns // PAIR
    scale = 1.0 / math.sqrt(D // HEADS)
    ctx = lax.axis_size("ctx")
    shards = lax.axis_size("shard")
    by_units = 2 * pairs == ctx
    shard = lax.axis_index("shard")
    core = lax.axis_index("tensor") % 2
    place = jnp.stack([core, shard]).astype(jnp.int32)

    def turn(value):
        return jnp.where(
            shard == 0, value, jnp.concatenate([value[..., half:], value[..., :half]], axis=-1)
        )

    qkv_mine = jnp.concatenate(
        [w[:, g * PAIR : (g + 1) * PAIR] for g in range(pairs) for w in (w_query, w_key, w_value)],
        axis=1,
    )
    qkv_bias = jnp.concatenate(
        [
            b
            for g in range(pairs)
            for b in (
                b_query[g * PAIR : (g + 1) * PAIR],
                jnp.zeros((PAIR,), F32),
                b_value[g * PAIR : (g + 1) * PAIR],
            )
        ]
    )
    qkv_theirs = swap_shard(qkv_mine)
    out_mine, after = lax.optimization_barrier((w_output, qkv_theirs))
    out_theirs = swap_shard(out_mine)
    hidden_mine, after = lax.optimization_barrier((w_hidden, out_theirs))
    hidden_theirs = swap_shard(hidden_mine)
    down_mine, after = lax.optimization_barrier((w_down, hidden_theirs))
    down_theirs = swap_shard(down_mine)
    full_qkv = jnp.concatenate([qkv_mine, qkv_theirs], axis=0)
    full_out = jnp.concatenate([w_output, out_theirs], axis=0)
    full_hidden = jnp.concatenate([w_hidden, hidden_theirs], axis=0)
    full_down = jnp.concatenate([w_down, down_theirs], axis=0)

    vec = turn(
        jnp.stack([b_output, gain_one, shift_one, b_down, gain_two, shift_two, b_down, b_down])
    )
    valid = valid_mask.astype(F32)
    count = sum_tokens(jnp.full((8, 128), jnp.sum(valid), F32))[0, 0]
    tokens_all = positions * seqs * ctx * shards
    own_valid = valid.reshape(positions, chunks, 2)
    own_valid = jnp.where(core == 0, own_valid[:, :, 0], own_valid[:, :, 1])
    features_other = swap_shard(time_features)
    features = jnp.where(
        shard == 0,
        jnp.concatenate([time_features, features_other], axis=0),
        jnp.concatenate([features_other, time_features], axis=0),
    ).astype(F32)

    embed = jnp.dot(time_features, w_time, preferred_element_type=F32) + b_time
    low, start = entry(place, inputs, embed)
    teacher_own = own_rows(place, teacher)

    saved = []
    outs = []
    for c in range(chunks):
        rows = low[c].reshape(2 * positions, width)
        qkv = (jnp.dot(rows, full_qkv, preferred_element_type=F32) + qkv_bias).astype(BF)
        qkv = jnp.stack(
            [
                qkv[:, g * 3 * PAIR : (g + 1) * 3 * PAIR].reshape(2, positions, 3 * PAIR)
                for g in range(pairs)
            ]
        )
        if by_units:
            units = spread_units(qkv)
            unit_mixed, logs = attend(units, scale)
            mixed = collect_units(unit_mixed, pairs, 2)
            kept = (units, logs)
        else:
            mixed, kept = gathered_forward(qkv, scale)
        mixed = jnp.concatenate([mixed[g] for g in range(pairs)], axis=-1)
        sent = swap_core(contract(mixed[1], full_out, 1, 1).astype(BF))
        mine = (contract(mixed[0], full_out, 1, 1) + sent.astype(F32)).astype(BF)
        theirs = swap_outer(mine)
        first, normed = row_call(
            first_norm_kernel, "first_norm", (start[c], mine, theirs, vec), (F32, BF), False
        )
        normed = jnp.concatenate([normed, swap_core(normed)], axis=0)
        pre = jnp.dot(normed, full_hidden, preferred_element_type=F32) + b_hidden
        phi = 0.5 * (1.0 + lax.erf(pre * math.sqrt(0.5)))
        hidden = (pre * phi).astype(BF)
        slope = (phi + pre * jnp.exp(-0.5 * pre * pre) * (1.0 / math.sqrt(2.0 * math.pi))).astype(BF)
        sent = swap_core(contract(hidden[positions:], full_down, 1, 1).astype(BF))
        mine = (contract(hidden[:positions], full_down, 1, 1) + sent.astype(F32)).astype(BF)
        theirs = swap_outer(mine)
        weight = own_valid[:, c : c + 1]
        weights = jnp.concatenate([weight * (2.0 * tokens_all / count), weight], axis=1)
        out, sum_grad, feed_low, sums_two = row_call(
            second_norm_kernel,
            "second_norm",
            (first, mine, theirs, vec, teacher_own[c], weights),
            (BF, F32, BF),
            True,
        )
        outs.append(out)
        saved.append((rows, kept, mixed, first, normed, hidden, slope, sum_grad, feed_low, sums_two))
    layer_own = jnp.stack(outs)
    layer_out = leave(place, layer_own, swap_core(layer_own))

    grads = []
    for c in range(chunks):
        rows, kept, mixed, first, normed, hidden, slope, sum_grad, feed_low, sums_two = saved[c]
        feed_low = jnp.concatenate([feed_low, swap_core(feed_low)], axis=0)
        pre_grad = (
            jnp.dot(feed_low, full_down, preferred_element_type=F32) * slope.astype(F32)
        ).astype(BF)
        sent = swap_core(contract(pre_grad[positions:], full_hidden, 1, 1).astype(BF))
        mine = (contract(pre_grad[:positions], full_hidden, 1, 1) + sent.astype(F32)).astype(BF)
        theirs = swap_outer(mine)
        first_grad, branch_low, sums_one = row_call(
            first_back_kernel,
            "first_back",
            (sum_grad, mine, theirs, first, vec),
            (F32, BF),
            True,
        )
        branch_low = jnp.concatenate([branch_low, swap_core(branch_low)], axis=0)
        mixed_grad = jnp.dot(branch_low, full_out, preferred_element_type=F32).astype(BF)
        mixed_grad = jnp.stack(
            [
                mixed_grad[:, g * PAIR : (g + 1) * PAIR].reshape(2, positions, PAIR)
                for g in range(pairs)
            ]
        )
        if by_units:
            units, logs = kept
            unit_grad = attend_back(units, spread_units(mixed_grad), logs, scale)
            qkv_grad = collect_units(unit_grad, pairs, 2)
        else:
            qkv_grad = gathered_backward(kept, mixed_grad, scale)
        qkv_grad = jnp.concatenate([qkv_grad[g] for g in range(pairs)], axis=-1)
        sent = swap_core(contract(qkv_grad[1], full_qkv, 1, 1).astype(BF))
        mine = (contract(qkv_grad[0], full_qkv, 1, 1) + sent.astype(F32)).astype(BF)
        theirs = swap_outer(mine)
        start_grad, sums_zero = row_call(
            last_kernel, "last", (first_grad, mine, theirs), (F32,), True
        )
        grads.append(
            (
                feed_low,
                pre_grad,
                branch_low,
                qkv_grad.reshape(2 * positions, -1),
                start_grad,
                sums_one,
                sums_zero,
            )
        )
    grad_own = jnp.stack([g[4] for g in grads])
    grad_inputs = leave(place, grad_own, swap_core(grad_own))

    def reduced(lefts, rights):
        left = jnp.concatenate(lefts, axis=0)
        right = jnp.concatenate(rights, axis=0)
        sent = swap_shard(contract(left[:, half:], right, 0, 0).astype(BF))
        mine = (contract(left[:, :half], right, 0, 0) + sent.astype(F32)).astype(BF)
        pieces = lax.all_to_all(mine.reshape(ctx, half // ctx, -1), "ctx", 0, 0)
        return jnp.sum(pieces.astype(F32), axis=0)

    grad_w_down = reduced([g[0] for g in grads], [s[5] for s in saved])
    grad_w_hidden = reduced([s[4] for s in saved], [g[1] for g in grads])
    grad_w_output = reduced(
        [g[2] for g in grads], [s[2].reshape(2 * positions, columns) for s in saved]
    )
    grad_w_qkv = reduced([s[0] for s in saved], [g[3] for g in grads])
    grad_w_query, grad_w_key, grad_w_value = (
        jnp.concatenate(
            [
                grad_w_qkv[:, (3 * g + j) * PAIR : (3 * g + j + 1) * PAIR]
                for g in range(pairs)
            ],
            axis=1,
        )
        for j in range(3)
    )

    two = sum(s[9] for s in saved)
    one = sum(g[5] for g in grads)
    columns_sum = lambda arrays: sum(jnp.sum(a.astype(F32), axis=0) for a in arrays)
    hidden_sum = columns_sum([g[1] for g in grads])
    qkv_sum = columns_sum([g[3] for g in grads])
    here = jnp.concatenate(
        [hidden_sum, qkv_sum, jnp.zeros((-(hidden_sum.size + qkv_sum.size) % width,), F32)]
    ).reshape(-1, width)
    slots = here.shape[0]
    here = jnp.concatenate(
        [jnp.where(core == 0, here, 0.0), jnp.where(core == 1, here, 0.0)], axis=0
    )
    which = jnp.arange(shards * seqs)[:, None]
    embed_rows = sum(
        jnp.where(which == shard * seqs + 2 * c + core, turn(grads[c][6][0:1]), 0.0)
        for c in range(chunks)
    )
    packed = jnp.concatenate([turn(two[:4]), turn(one[:3]), here, embed_rows], axis=0)
    packed = packed + swap_core(packed)
    packed = sum_tokens(packed)
    here = jnp.where(core == 0, packed[7 : 7 + slots], packed[7 + slots : 7 + 2 * slots]).reshape(-1)
    embed_grad = packed[7 + 2 * slots :]
    hidden_units = hidden_sum.size
    qkv_sum = here[hidden_units : hidden_units + qkv_sum.size].reshape(pairs, 3, PAIR)
    grad_w_time = lax.dot_general(
        features, embed_grad, (((0,), (0,)), ((), ())), precision=lax.Precision.HIGHEST
    )
    return (
        layer_out,
        jnp.sum(packed[3]) / (D * count),
        grad_inputs,
        grad_w_time,
        jnp.sum(embed_grad, axis=0),
        grad_w_query,
        qkv_sum[:, 0].reshape(-1),
        grad_w_key,
        grad_w_value,
        qkv_sum[:, 2].reshape(-1),
        grad_w_output,
        packed[6],
        packed[4],
        packed[5],
        grad_w_hidden,
        here[:hidden_units],
        grad_w_down,
        packed[2],
        packed[0],
        packed[1],
    )


def solution(mesh):
    placed = (
        P("ctx", "shard", None),
        P("shard", None),
        P("ctx", "shard"),
        P("ctx", "shard", None),
        P(),
        P(),
        P("shard", "tensor"),
        P("tensor"),
        P("shard", "tensor"),
        P("shard", "tensor"),
        P("tensor"),
        P("shard", "tensor"),
        P(),
        P(),
        P(),
        P("shard", "tensor"),
        P("tensor"),
        P("shard", "tensor"),
        P(),
        P(),
        P(),
    )
    return jax.shard_map(
        body,
        mesh=mesh,
        in_specs=placed,
        out_specs=(
            P("ctx", "shard", None),
            P(),
            P("ctx", "shard", None),
            P(),
            P(),
            P(("shard", "ctx"), "tensor"),
            P("tensor"),
            P(("shard", "ctx"), "tensor"),
            P(("shard", "ctx"), "tensor"),
            P("tensor"),
            P(("shard", "ctx"), "tensor"),
            P(),
            P(),
            P(),
            P(("shard", "ctx"), "tensor"),
            P("tensor"),
            P(("shard", "ctx"), "tensor"),
            P(),
            P(),
            P(),
        ),
        check_vma=False,
    )
```

```python
from functools import partial
import math

import jax
import jax.numpy as jnp
from jax import lax
from jax.experimental import pallas as pl
from jax.experimental.pallas import tpu as pltpu
from jax.sharding import PartitionSpec as P

D = 1024
HEADS = 16
BF = jnp.bfloat16
F32 = jnp.float32
PAIR = 128
EPS = 1e-05


def contract(left, right, left_dim, right_dim):
    return lax.dot_general(
        left, right, (((left_dim,), (right_dim,)), ((), ())), preferred_element_type=F32
    )


PINNED = False
WEIGHT = 0.01


def cost(flops, nbytes):
    return pl.CostEstimate(flops=int(flops * WEIGHT), bytes_accessed=int(nbytes * WEIGHT), transcendentals=0)


def swap(value, axis, bit):
    size = lax.axis_size(axis)
    return lax.ppermute(value, axis, [(i, i ^ bit) for i in range(size)])


def swap_core(value):
    return swap(value, "tensor", 1)


def swap_outer(value):
    return swap(value, "tensor", 2)


def swap_shard(value):
    return swap(value, "shard", 1)


def swap_ctx(pieces):
    moved = {d: swap(pieces[d], "ctx", d) for d in reversed(range(1, len(pieces)))}
    return [pieces[0]] + [moved[d] for d in range(1, len(pieces))]


def sum_ctx(value):
    size = lax.axis_size("ctx")
    if size & (size - 1):
        return lax.psum(value, "ctx")
    bit = 1
    while bit < size:
        value = value + swap(value, "ctx", bit)
        bit *= 2
    return value


def sum_tokens(value):
    return sum_ctx(value + swap_shard(value))


def grid_call(kernel, name, grid, ins, outs, work, place, pinned=True):
    args = [a for a, _, _ in ins]
    nbytes = sum(a.size * a.dtype.itemsize for a in args)
    nbytes += sum(math.prod(s) * jnp.dtype(d).itemsize for s, d, _, _ in outs)
    without = lambda f: (lambda *i: f(*i[: len(grid)]))
    if pinned:
        args = [pltpu.with_memory_space_constraint(a, pltpu.HBM) for a in args]
    return pl.pallas_call(
        kernel,
        grid_spec=pltpu.PrefetchScalarGridSpec(
            num_scalar_prefetch=1,
            grid=grid,
            in_specs=[pl.BlockSpec(b, without(f)) for _, b, f in ins],
            out_specs=[pl.BlockSpec(b, without(f)) for _, _, b, f in outs],
        ),
        out_shape=[jax.ShapeDtypeStruct(s, d) for s, d, _, _ in outs],
        cost_estimate=cost(work, nbytes),
        compiler_params=pltpu.CompilerParams(vmem_limit_bytes=16 << 20),
        name=name,
    )(place, *args)


def call(kernel, name, args, outs, work, scratch=(), place=None, room=12, pinned=PINNED):
    nbytes = sum(a.size * a.dtype.itemsize for a in args)
    nbytes += sum(math.prod(s) * jnp.dtype(d).itemsize for s, d in outs)
    first = [] if place is None else [place]
    if pinned:
        args = [pltpu.with_memory_space_constraint(a, pltpu.VMEM) for a in args]
    return pl.pallas_call(
        kernel,
        in_specs=[pl.BlockSpec(memory_space=pltpu.SMEM)] * len(first)
        + [pl.BlockSpec(memory_space=pltpu.VMEM)] * len(args),
        out_specs=[pl.BlockSpec(memory_space=pltpu.VMEM)] * len(outs),
        out_shape=[jax.ShapeDtypeStruct(s, d) for s, d in outs],
        scratch_shapes=scratch,
        cost_estimate=cost(work, nbytes),
        compiler_params=pltpu.CompilerParams(vmem_limit_bytes=room << 20),
        name=name,
    )(*first, *args)


def whole(array):
    rank = array.ndim
    return (array, array.shape, lambda *i: (0,) * rank)


def turned(value, flip):
    half = value.shape[1] // 2
    return jnp.where(flip == 0, value, jnp.concatenate([value[:, half:], value[:, :half]], axis=1))


def entry_kernel(chunks, place, x_ref, embed_ref, *out_refs):
    core, flip = place[0], place[1]
    x = x_ref[...].astype(F32)
    rows = [x[:, s, :] + embed_ref[s : s + 1, :] for s in range(2 * chunks)]
    for c in range(chunks):
        own = turned(jnp.where(core == 0, rows[c], rows[chunks + c]), flip)
        out_refs[c][...] = own.astype(BF)
        out_refs[chunks + c][...] = own


def entry(place, x, embed):
    positions, seqs, width = x.shape
    chunks = seqs // 2
    block = math.gcd(64, positions)
    return grid_call(
        partial(entry_kernel, chunks),
        "entry",
        (positions // block,),
        [(x, (block, seqs, width), lambda i: (i, 0, 0)), whole(embed)],
        [
            ((positions, width), dtype, (block, width), lambda i: (i, 0))
            for dtype in (BF, F32)
            for _ in range(chunks)
        ],
        4 * x.size,
        place=place,
    )


def own_kernel(chunks, place, x_ref, *out_refs):
    core, flip = place[0], place[1]
    x = x_ref[...].astype(F32)
    for c in range(chunks):
        own = jnp.where(core == 0, x[:, c, :], x[:, chunks + c, :])
        out_refs[c][...] = turned(own, flip).astype(BF)


def own_rows(place, x):
    positions, seqs, width = x.shape
    chunks = seqs // 2
    block = math.gcd(64, positions)
    return grid_call(
        partial(own_kernel, chunks),
        "own_rows",
        (positions // block,),
        [(x, (block, seqs, width), lambda i: (i, 0, 0))],
        [((positions, width), BF, (block, width), lambda i: (i, 0))] * chunks,
        2 * x.size,
        place=place,
    )


def leave_kernel(chunks, dtype, place, *refs):
    core, flip = place[0], place[1]
    *ins, out_ref = refs
    own = [turned(ref[...].astype(F32), flip) for ref in ins[:chunks]]
    other = [turned(ref[...].astype(F32), flip) for ref in ins[chunks:]]
    rows = [jnp.where(core == 0, a, b) for a, b in zip(own, other)]
    rows += [jnp.where(core == 0, b, a) for a, b in zip(own, other)]
    out_ref[...] = jnp.stack(rows, axis=1).astype(dtype)


def leave(place, own):
    chunks = len(own)
    positions, width = own[0].shape
    dtype = own[0].dtype
    block = math.gcd(64, positions)
    arrays = [*own, *(swap_core(a) for a in own)]
    return grid_call(
        partial(leave_kernel, chunks, dtype),
        "leave",
        (positions // block,),
        [(a, (block, width), lambda i: (i, 0)) for a in arrays],
        [
            (
                (positions, 2 * chunks, width),
                dtype,
                (block, 2 * chunks, width),
                lambda i: (i, 0, 0),
            )
        ],
        2 * positions * width,
        place=place,
        pinned=False,
    )[0]


def pack_kernel(place, q_ref, k_ref, v_ref, out_ref):
    for g in range(q_ref.shape[1] // PAIR):
        for j, ref in enumerate((q_ref, k_ref, v_ref)):
            at = (3 * g + j) * PAIR
            out_ref[:, at : at + PAIR] = ref[:, g * PAIR : (g + 1) * PAIR]


def pack(place, q, k, v):
    rows, columns = q.shape
    return grid_call(
        pack_kernel,
        "pack",
        (1,),
        [whole(q), whole(k), whole(v)],
        [((rows, 3 * columns), BF, (rows, 3 * columns), lambda i: (0, 0))],
        0,
        place,
    )[0]


def pack_feed_kernel(place, out_ref, up_ref, down_ref, copy_ref, both_ref):
    each = up_ref.shape[1]
    copy_ref[...] = out_ref[...]
    both_ref[:, :each] = up_ref[...]
    both_ref[:, each:] = down_ref[...]


def pack_feed(place, out, up, down):
    rows, each = up.shape
    block = math.gcd(128, rows)
    tall = lambda a: (a, (block, a.shape[1]), lambda i: (i, 0))
    return grid_call(
        pack_feed_kernel,
        "pack_feed",
        (rows // block,),
        [tall(out), tall(up), tall(down)],
        [
            (out.shape, BF, (block, out.shape[1]), lambda i: (i, 0)),
            ((rows, 2 * each), BF, (block, 2 * each), lambda i: (i, 0)),
        ],
        0,
        place,
    )


def project_kernel(shift, place, x_ref, a_ref, b_ref, c_ref, d_ref, bias_ref, more_ref, *outs_and_all):
    *outs, pairs_ref = outs_and_all
    half = x_ref.shape[1] // 2
    per_core = len(outs) // 2
    wide = 3 * PAIR
    for core, (top, bottom) in enumerate(((a_ref, b_ref), (c_ref, d_ref))):

        def step(g, carry, core=core, top=top, bottom=bottom):
            at = pl.ds(pl.multiple_of(g * wide, wide), wide)
            value = contract(x_ref[:, :half], top[:, at], 1, 0)
            value += contract(x_ref[:, half:], bottom[:, at], 1, 0)
            pair = core * per_core + g
            bias = (bias_ref, more_ref)[core]
            for j, first in enumerate((shift, None, shift + per_core * PAIR)):
                part = value[:, j * PAIR : (j + 1) * PAIR]
                if first is not None:
                    part += bias[:, pl.ds(pl.multiple_of(first + g * PAIR, PAIR), PAIR)]
                pairs_ref[pair, :, j * PAIR : (j + 1) * PAIR] = part.astype(BF)
            return carry

        lax.fori_loop(0, per_core, step, 0)
    for d, out in enumerate(outs):
        out[...] = pairs_ref[place[2] ^ d]


def project(place, shift, x, weights, biases):
    rows, width = x.shape
    pairs = 2 * weights[0].shape[1] // (3 * PAIR)
    return call(
        partial(project_kernel, shift),
        "project",
        (x, *weights, *biases),
        [((rows, 3 * PAIR), BF)] * pairs,
        2 * rows * width * pairs * 3 * PAIR,
        scratch=[pltpu.VMEM((pairs, rows, 3 * PAIR), BF)],
        place=place,
    )


def project_back_kernel(pairs, place, *refs):
    pieces, (a_ref, b_ref, c_ref, d_ref, flat_ref, out_ref, sums_ref, pairs_ref) = (
        refs[:pairs],
        refs[pairs:],
    )
    for d, piece in enumerate(pieces):
        pairs_ref[place[2] ^ d] = piece[...]
    wide = 3 * PAIR
    for p in range(pairs):
        flat_ref[:, p * wide : (p + 1) * wide] = pairs_ref[p]
    half = a_ref.shape[0]
    middle = a_ref.shape[1]
    for at, first, second in ((0, a_ref, c_ref), (half, b_ref, d_ref)):
        value = contract(flat_ref[:, :middle], first[...], 1, 1)
        value += contract(flat_ref[:, middle:], second[...], 1, 1)
        out_ref[:, at : at + half] = value.astype(BF)
    sums_ref[...] = sum_rows(flat_ref[...].astype(F32))


def project_back(place, pieces, weights):
    rows, columns = pieces[0].shape
    pairs = len(pieces)
    width = 2 * weights[0].shape[0]
    return call(
        partial(project_back_kernel, pairs),
        "project_back",
        (*pieces, *weights),
        [((rows, pairs * columns), BF), ((rows, width), BF), ((1, pairs * columns), F32)],
        2 * rows * width * pairs * columns,
        scratch=[pltpu.VMEM((pairs, rows, columns), BF)],
        place=place,
    )


def merge_kernel(pairs, place, *refs):
    pieces, (a_ref, b_ref, c_ref, d_ref, flat_ref, out_ref, pairs_ref) = refs[:pairs], refs[pairs:]
    for d, piece in enumerate(pieces):
        pairs_ref[place[2] ^ d] = piece[...]
    for p in range(pairs):
        flat_ref[:, p * PAIR : (p + 1) * PAIR] = pairs_ref[p]
    half = a_ref.shape[0]
    middle = a_ref.shape[1]
    for at, first, second in ((0, a_ref, c_ref), (half, b_ref, d_ref)):
        value = contract(flat_ref[:, :middle], first[...], 1, 1)
        value += contract(flat_ref[:, middle:], second[...], 1, 1)
        out_ref[:, at : at + half] = value.astype(BF)


def merge(place, pieces, weights):
    rows, columns = pieces[0].shape
    pairs = len(pieces)
    width = 2 * weights[0].shape[0]
    return call(
        partial(merge_kernel, pairs),
        "merge",
        (*pieces, *weights),
        [((rows, pairs * columns), BF), ((rows, width), BF)],
        2 * rows * width * pairs * columns,
        scratch=[pltpu.VMEM((pairs, rows, columns), BF)],
        place=place,
    )


def lanes_of(part):
    lane = lax.broadcasted_iota(jnp.int32, (1, PAIR), 1)
    return lane < PAIR // 2 if part == 0 else lane >= PAIR // 2


def attend_kernel(scale, pieces, *refs):
    ins, outs, (log_ref, mixed_ref) = refs[:pieces], refs[pieces : 2 * pieces], refs[2 * pieces :]
    rows = ins[0].shape[0]
    join = lambda at: jnp.concatenate([ref[:, at : at + PAIR] for ref in ins], axis=0)
    q, k, v = join(0) * BF(scale), join(PAIR), join(2 * PAIR)
    lane = lax.broadcasted_iota(jnp.int32, (1, PAIR), 1)
    mixed_ref[...] = jnp.zeros_like(mixed_ref)

    def head(part, carry):
        lanes = (lane >= PAIR // 2) == (part == 1)
        k_head, v_head = jnp.where(lanes, k, BF(0)), jnp.where(lanes, v, BF(0))
        scores = contract(k_head, q, 1, 1)
        peak = jnp.max(scores, axis=0, keepdims=True)
        weights = jnp.exp(scores - peak)
        total = jnp.sum(weights, axis=0, keepdims=True)
        mixed_ref[...] += contract(v_head, weights.astype(BF), 0, 0) * (1.0 / total)
        log_ref[pl.ds(part, 1), :] = peak + jnp.log(total)
        return carry

    lax.fori_loop(0, 2, head, 0)
    mixed = mixed_ref[...].T.astype(BF)
    for d, out in enumerate(outs):
        out[...] = mixed[d * rows : (d + 1) * rows]


def attend(pieces, scale):
    rows = pieces[0].shape[0]
    length = rows * len(pieces)
    return call(
        partial(attend_kernel, scale, len(pieces)),
        "attend",
        pieces,
        [((rows, PAIR), BF)] * len(pieces) + [((2, length), F32)],
        16 * length * length * PAIR,
        scratch=[pltpu.VMEM((PAIR, length), F32)],
        room=24,
    )


def attend_back_kernel(scale, pieces, *refs):
    ins, grads = refs[:pieces], refs[pieces : 2 * pieces]
    log_ref, outs = refs[2 * pieces], refs[2 * pieces + 1 : 3 * pieces + 1]
    k_sum, v_sum, q_sum, q_ref, grad_ref = refs[3 * pieces + 1 :]
    rows = ins[0].shape[0]
    length = rows * pieces
    join = lambda refs, at: jnp.concatenate([ref[:, at : at + PAIR] for ref in refs], axis=0)
    k, v = join(ins, PAIR), join(ins, 2 * PAIR)
    q_ref[...] = join(ins, 0) * BF(scale)
    grad_ref[...] = join(grads, 0)
    k_sum[...] = jnp.zeros_like(k_sum)
    v_sum[...] = jnp.zeros_like(v_sum)
    q_sum[...] = jnp.zeros_like(q_sum)
    lane = lax.broadcasted_iota(jnp.int32, (1, PAIR), 1)
    block = math.gcd(512, length)

    def step(i, carry):
        part = i % 2
        at = pl.ds(pl.multiple_of(i // 2 * block, block), block)
        lanes = (lane >= PAIR // 2) == (part == 1)
        q, grad = q_ref[at, :], grad_ref[at, :]
        k_head, v_head = jnp.where(lanes, k, BF(0)), jnp.where(lanes, v, BF(0))
        q_head, grad_head = jnp.where(lanes, q, BF(0)), jnp.where(lanes, grad, BF(0))
        probs = jnp.exp(contract(k_head, q, 1, 1) - log_ref[pl.ds(part, 1), at])
        probs_grad = contract(v_head, grad, 1, 1)
        delta = jnp.sum(probs * probs_grad, axis=0, keepdims=True)
        scores_grad = (probs * (probs_grad - delta)).astype(BF)
        v_sum[...] += contract(probs.astype(BF), grad_head, 1, 0)
        k_sum[...] += contract(scores_grad, q_head, 1, 0)
        q_sum[:, at] += contract(k_head, scores_grad, 0, 0)
        return carry

    lax.fori_loop(0, 2 * length // block, step, 0)
    q_grad = (q_sum[...] * scale).T.astype(BF)
    for d, out in enumerate(outs):
        at = slice(d * rows, (d + 1) * rows)
        out[:, 0:PAIR] = q_grad[at, :]
        out[:, PAIR : 2 * PAIR] = k_sum[at, :].astype(BF)
        out[:, 2 * PAIR : 3 * PAIR] = v_sum[at, :].astype(BF)


def attend_back(pieces, grads, logs, scale):
    rows = pieces[0].shape[0]
    length = rows * len(pieces)
    return call(
        partial(attend_back_kernel, scale, len(pieces)),
        "attend_back",
        (*pieces, *grads, logs),
        [((rows, 3 * PAIR), BF)] * len(pieces),
        40 * length * length * PAIR,
        scratch=[pltpu.VMEM((length, PAIR), F32)] * 2
        + [pltpu.VMEM((PAIR, length), F32)]
        + [pltpu.VMEM((length, PAIR), BF)] * 2,
        room=24,
    )


def sum_rows(value):
    return jnp.sum(value, axis=0, keepdims=True)


def normal(value):
    center = jnp.mean(value, axis=-1, keepdims=True)
    offset = value - center
    spread = jnp.mean(offset * offset, axis=-1, keepdims=True)
    inverse = lax.rsqrt(spread + EPS)
    return offset * inverse, inverse


def normal_back(grad, unit, inverse):
    return inverse * (
        grad
        - jnp.mean(grad, axis=-1, keepdims=True)
        - unit * jnp.mean(grad * unit, axis=-1, keepdims=True)
    )


def by_rows(rows, run):
    size = math.gcd(64, rows)

    def step(i, carry):
        run(pl.ds(pl.multiple_of(i * size, size), size))
        return carry

    lax.fori_loop(0, rows // size, step, 0)


def feed_kernel(
    start_ref, mine_ref, theirs_ref, vec_ref, bias_ref, more_ref, a_ref, b_ref, c_ref, d_ref,
    first_ref, low_ref, hidden_ref, slope_ref, out_ref, acc,
):
    def norm(at):
        total = start_ref[at, :] + mine_ref[at, :].astype(F32) + theirs_ref[at, :].astype(F32)
        total += vec_ref[0:1, :]
        first_ref[at, :] = total
        unit, _ = normal(total)
        low_ref[at, :] = (unit * vec_ref[1:2, :] + vec_ref[2:3, :]).astype(BF)

    by_rows(start_ref.shape[0], norm)
    half, each = a_ref.shape[0], a_ref.shape[1] // 2
    size = math.gcd(512, each)
    acc[...] = jnp.zeros_like(acc)
    for core, (top, bottom) in enumerate(((a_ref, b_ref), (c_ref, d_ref))):

        def step(i, carry, core=core, top=top, bottom=bottom):
            here = pl.ds(pl.multiple_of(i * size, size), size)
            at = pl.ds(pl.multiple_of(core * each + i * size, size), size)
            down = pl.ds(pl.multiple_of(each + i * size, size), size)
            pre = contract(low_ref[:, :half], top[:, here], 1, 0)
            pre += contract(low_ref[:, half:], bottom[:, here], 1, 0)
            pre += (bias_ref, more_ref)[core][:, here]
            phi = 0.5 + 0.5 * lax.erf(pre * math.sqrt(0.5))
            hidden = (pre * phi).astype(BF)
            hidden_ref[:, at] = hidden
            bell = jnp.exp(-0.5 * (pre * pre)) * (1.0 / math.sqrt(2.0 * math.pi))
            slope_ref[:, at] = (phi + pre * bell).astype(BF)
            for k, weight in ((0, top), (half, bottom)):
                acc[:, k : k + half] += contract(hidden, weight[:, down], 1, 1)
            return carry

        lax.fori_loop(0, each // size, step, 0)
    out_ref[...] = acc[...].astype(BF)


def feed(start, mine, theirs, vec, biases, weights):
    rows, width = start.shape
    units = weights[0].shape[1]
    return call(
        feed_kernel,
        "feed",
        (start, mine, theirs, vec, *biases, *weights),
        [
            ((rows, width), F32),
            ((rows, width), BF),
            ((rows, units), BF),
            ((rows, units), BF),
            ((rows, width), BF),
        ],
        4 * rows * width * units,
        scratch=[pltpu.VMEM((rows, width), F32)],
    )


def feed_back_kernel(
    valid_row, tokens, place, first_ref, mine_ref, theirs_ref, vec_ref, teacher_ref, valid_ref, count_ref, slope_ref,
    a_ref, b_ref, c_ref, d_ref, result_ref, grad_ref, low_ref, pre_ref, out_ref, sums_ref, pre_sums_ref, acc, valid_sums,
):
    second = valid_ref.shape[0] // 2 + valid_row
    valid = jnp.where(
        place[0] == 0, valid_ref[valid_row : valid_row + 1, :], valid_ref[second : second + 1, :]
    )
    valid_sums[...] = jnp.broadcast_to(valid, (PAIR, valid.shape[1])).T
    sums_ref[...] = jnp.zeros_like(sums_ref)
    factor = 2.0 * tokens / count_ref[0:1, 0:1]

    def norm(at):
        valid = valid_sums[at, 0:1]
        unit, _ = normal(first_ref[at, :])
        normed = unit * vec_ref[1:2, :] + vec_ref[2:3, :]
        total = normed + mine_ref[at, :].astype(F32) + theirs_ref[at, :].astype(F32) + vec_ref[3:4, :]
        unit, inverse = normal(total)
        result = unit * vec_ref[4:5, :] + vec_ref[5:6, :]
        result_ref[at, :] = result.astype(BF)
        error = result - teacher_ref[at, :].astype(F32)
        result_grad = valid * factor * error
        grad = normal_back(result_grad * vec_ref[4:5, :], unit, inverse)
        grad_ref[at, :] = grad
        low = grad.astype(BF)
        low_ref[at, :] = low
        sums_ref[0:1, :] += sum_rows(result_grad * unit)
        sums_ref[1:2, :] += sum_rows(result_grad)
        sums_ref[2:3, :] += sum_rows(low.astype(F32))
        sums_ref[3:4, :] += sum_rows(valid * error * error)

    by_rows(first_ref.shape[0], norm)
    half, each = a_ref.shape[0], a_ref.shape[1] // 2
    size = math.gcd(512, each)
    acc[...] = jnp.zeros_like(acc)
    for core, (top, bottom) in enumerate(((a_ref, b_ref), (c_ref, d_ref))):

        def step(i, carry, core=core, top=top, bottom=bottom):
            here = pl.ds(pl.multiple_of(i * size, size), size)
            at = pl.ds(pl.multiple_of(core * each + i * size, size), size)
            down = pl.ds(pl.multiple_of(each + i * size, size), size)
            value = contract(low_ref[:, :half], top[:, down], 1, 0)
            value += contract(low_ref[:, half:], bottom[:, down], 1, 0)
            pre_grad = (value * slope_ref[:, at].astype(F32)).astype(BF)
            pre_ref[:, at] = pre_grad
            pre_sums_ref[:, at] = sum_rows(pre_grad.astype(F32))
            for k, weight in ((0, top), (half, bottom)):
                acc[:, k : k + half] += contract(pre_grad, weight[:, here], 1, 1)
            return carry

        lax.fori_loop(0, each // size, step, 0)
    out_ref[...] = acc[...].astype(BF)


def feed_back(place, row, tokens, first, mine, theirs, vec, teacher, valid, count, slope, weights):
    rows, width = first.shape
    units = slope.shape[1]
    return call(
        partial(feed_back_kernel, row, tokens),
        "feed_back",
        (first, mine, theirs, vec, teacher, valid, count, slope, *weights),
        [
            ((rows, width), BF),
            ((rows, width), F32),
            ((rows, width), BF),
            ((rows, units), BF),
            ((rows, width), BF),
            ((8, width), F32),
            ((1, units), F32),
        ],
        4 * rows * width * units,
        scratch=[pltpu.VMEM((rows, width), F32), pltpu.VMEM((rows, PAIR), F32)],
        place=place,
    )


def split_kernel(place, grad_ref, mine_ref, theirs_ref, first_ref, vec_ref, a_ref, b_ref, c_ref, d_ref, out_ref, low_ref, sums_ref, *outs_and_all):
    *outs, pairs_ref = outs_and_all
    sums_ref[...] = jnp.zeros_like(sums_ref)

    def norm(at):
        grad = grad_ref[at, :] + mine_ref[at, :].astype(F32) + theirs_ref[at, :].astype(F32)
        unit, inverse = normal(first_ref[at, :])
        out = normal_back(grad * vec_ref[1:2, :], unit, inverse)
        out_ref[at, :] = out
        low = out.astype(BF)
        low_ref[at, :] = low
        sums_ref[0:1, :] += sum_rows(grad * unit)
        sums_ref[1:2, :] += sum_rows(grad)
        sums_ref[2:3, :] += sum_rows(low.astype(F32))

    by_rows(grad_ref.shape[0], norm)
    half = a_ref.shape[0]
    per_core = len(outs) // 2
    for core, (top, bottom) in enumerate(((a_ref, b_ref), (c_ref, d_ref))):
        mixed = contract(low_ref[:, :half], top[...], 1, 0)
        mixed += contract(low_ref[:, half:], bottom[...], 1, 0)
        mixed = mixed.astype(BF)
        for p in range(per_core):
            pairs_ref[core * per_core + p] = mixed[:, p * PAIR : (p + 1) * PAIR]
    for d, piece in enumerate(outs):
        piece[...] = pairs_ref[place[2] ^ d]


def split(place, grad, mine, theirs, first, vec, weights):
    rows, width = grad.shape
    pairs = 2 * weights[0].shape[1] // PAIR
    return call(
        split_kernel,
        "split",
        (grad, mine, theirs, first, vec, *weights),
        [((rows, width), F32), ((rows, width), BF), ((8, width), F32)]
        + [((rows, PAIR), BF)] * pairs,
        2 * rows * width * pairs * PAIR,
        scratch=[pltpu.VMEM((pairs, rows, PAIR), BF)],
        place=place,
    )


def last_kernel(grad_ref, mine_ref, theirs_ref, out_ref, sums_ref):
    grad = grad_ref[...] + mine_ref[...].astype(F32) + theirs_ref[...].astype(F32)
    out_ref[...] = grad
    sums_ref[...] = jnp.broadcast_to(sum_rows(grad), sums_ref.shape)


def last(grad, mine, theirs):
    rows, width = grad.shape
    return call(
        last_kernel,
        "last",
        (grad, mine, theirs),
        [((rows, width), F32), ((8, width), F32)],
        4 * rows * width,
    )


def tally_kernel(chunks, each, place, *refs):
    two, one = refs[:chunks], refs[chunks : 2 * chunks]
    pre, qkv = refs[2 * chunks : 3 * chunks], refs[3 * chunks : 4 * chunks]
    zero, (features_ref, out_ref) = refs[4 * chunks : 5 * chunks], refs[5 * chunks :]
    core, flip, spot = place[0], place[1], place[3]
    add = lambda parts: sum(parts[1:], parts[0])
    out_ref[...] = jnp.zeros_like(out_ref)
    out_ref[0:4, :] = turned(add([ref[0:4, :] for ref in two]), flip)
    out_ref[4:7, :] = turned(add([ref[0:3, :] for ref in one]), flip)
    pre = add([ref[...] for ref in pre])
    qkv = add([ref[...] for ref in qkv])
    size = qkv.shape[1] // 2
    for slot in range(2):
        mine = core == slot
        out_ref[8 + slot : 9 + slot, :] = jnp.where(mine, pre[:, :each], pre[:, each:])
        out_ref[10 + slot : 11 + slot, :size] = jnp.where(mine, qkv[:, :size], qkv[:, size:])
    seqs = 2 * chunks
    for s in range(2 * seqs):
        here = jnp.logical_and(flip == s // seqs, core == s % seqs // chunks)
        row = turned(zero[s % chunks][0:1, :], flip)
        out_ref[12 + s : 13 + s, :] = jnp.where(here, row, 0.0)
    at = 12 + 2 * seqs
    features = features_ref[...].astype(F32)
    wide = features.shape[1]
    for s in range(2):
        here = jnp.logical_and(jnp.logical_and(core == 0, spot == 0), flip == s)
        for k in range(seqs):
            value = jnp.where(here, features[k : k + 1, :], 0.0)
            out_ref[at + s : at + s + 1, k * wide : (k + 1) * wide] = value


def tally(place, each, two, one, pre, qkv, zero, features):
    rows = -(-(14 + 2 * features.shape[0]) // 8) * 8
    return call(
        partial(tally_kernel, len(two), each),
        "tally",
        (*two, *one, *pre, *qkv, *zero, features),
        [((rows, two[0].shape[1]), F32)],
        0,
        place=place,
    )[0]


def grad_sum_kernel(pieces, cuts, *refs):
    total = refs[0][...].astype(F32)
    for ref in refs[1:pieces]:
        total = total + ref[...].astype(F32)
    for out, parts in zip(refs[pieces:], cuts):
        at = 0
        for start, size in parts:
            out[:, at : at + size] = total[:, start : start + size]
            at += size


def grad_sum(pieces, cuts):
    rows = pieces[0].shape[0]
    return call(
        partial(grad_sum_kernel, len(pieces), cuts),
        "grad_sum",
        pieces,
        [((rows, sum(size for _, size in parts)), F32) for parts in cuts],
        len(pieces) * pieces[0].size,
    )


def finish_kernel(each, size, shards, place, packed_ref, count_ref, time_ref, loss_ref, start_ref, hidden_ref, qkv_ref, *outs_and_all):
    *outs, all_ref = outs_and_all
    seqs = all_ref.shape[0]
    wide = all_ref.shape[1]
    per_row = seqs // shards
    at = 12 + seqs
    for s in range(seqs):
        k = s % per_row
        row = at + s // per_row
        all_ref[s : s + 1, :] = packed_ref[row : row + 1, k * wide : (k + 1) * wide]
    grads = packed_ref[12:at, :]
    time_ref[...] = lax.dot_general(
        all_ref[...],
        grads,
        (((0,), (0,)), ((), ())),
        precision=lax.Precision.HIGHEST,
        preferred_element_type=F32,
    )
    start_ref[...] = sum_rows(grads)
    total = jnp.sum(packed_ref[3:4, :], axis=1, keepdims=True)
    loss_ref[...] = total / (packed_ref.shape[1] * count_ref[0:1, 0:1])
    first = place[0] == 0
    hidden_ref[...] = jnp.where(first, packed_ref[8:9, :], packed_ref[9:10, :])[:, :each]
    qkv_ref[...] = jnp.where(first, packed_ref[10:11, :], packed_ref[11:12, :])[:, :size]
    for out, row in zip(outs, (0, 1, 2, 4, 5, 6)):
        out[...] = packed_ref[row : row + 1, :]


def finish(place, each, size, seqs, shards, wide, packed, count):
    width = packed.shape[1]
    return call(
        partial(finish_kernel, each, size, shards),
        "finish",
        (packed, count),
        [((wide, width), F32), ((1, 1), F32), ((1, width), F32), ((1, each), F32), ((1, size), F32)]
        + [((1, width), F32)] * 6,
        0,
        scratch=[pltpu.VMEM((seqs, wide), F32)],
        place=place,
    )


def token_sum(lefts, rights, rows, columns):
    total = None
    for left, right in zip(lefts, rights):
        term = contract(left[:, rows], right[:, columns], 0, 0)
        total = term if total is None else total + term
    return total


def grad_core_kernel(chunks, *refs):
    lefts, rights, out_ref = refs[:chunks], refs[chunks : 2 * chunks], refs[2 * chunks]
    rows, columns = out_ref.shape
    step = math.gcd(512, rows)

    def part(i, carry):
        at = pl.ds(pl.multiple_of(i * step, step), step)
        out_ref[at, :] = token_sum(lefts, rights, at, slice(columns, 2 * columns)).astype(BF)
        return carry

    lax.fori_loop(0, rows // step, part, 0)


def grad_core(lefts, rights):
    rows, columns = lefts[0].shape[1], rights[0].shape[1] // 2
    tokens = sum(a.shape[0] for a in lefts)
    return call(
        partial(grad_core_kernel, len(lefts)),
        "grad_core",
        (*lefts, *rights),
        [((rows, columns), BF)],
        2 * tokens * rows * columns,
    )[0]


def grad_shard_kernel(chunks, *refs):
    lefts, rights, (core_ref, out_ref) = refs[:chunks], refs[chunks : 2 * chunks], refs[2 * chunks :]
    half, columns = out_ref.shape
    size = math.gcd(256, half)

    def step(i, carry):
        at = pl.ds(pl.multiple_of(i * size, size), size)
        far = pl.ds(pl.multiple_of(half + i * size, size), size)
        value = token_sum(lefts, rights, far, slice(0, columns))
        out_ref[at, :] = (value + core_ref[far, :].astype(F32)).astype(BF)
        return carry

    lax.fori_loop(0, half // size, step, 0)


def grad_shard(lefts, rights, core):
    half, columns = lefts[0].shape[1] // 2, rights[0].shape[1] // 2
    tokens = sum(a.shape[0] for a in lefts)
    return call(
        partial(grad_shard_kernel, len(lefts)),
        "grad_shard",
        (*lefts, *rights, core),
        [((half, columns), BF)],
        2 * tokens * half * columns,
    )[0]


def grad_own_kernel(chunks, place, *refs):
    lefts, rights, (core_ref, shard_ref, *outs, acc) = (
        refs[:chunks],
        refs[chunks : 2 * chunks],
        refs[2 * chunks :],
    )
    half, columns = acc.shape
    size = math.gcd(256, half)

    def step(i, carry):
        at = pl.ds(pl.multiple_of(i * size, size), size)
        value = token_sum(lefts, rights, at, slice(0, columns))
        acc[at, :] = value + core_ref[at, :].astype(F32) + shard_ref[at, :].astype(F32)
        return carry

    lax.fori_loop(0, half // size, step, 0)
    rows = outs[0].shape[0]
    if len(outs) == 1:
        outs[0][...] = acc[...].astype(BF)
    else:
        for d, out in enumerate(outs):
            at = pl.multiple_of((place[2] ^ d) * rows, rows)
            out[...] = acc[pl.ds(at, rows), :].astype(out.dtype)


def grad_own(place, lefts, rights, core, shard, pieces):
    half, columns = lefts[0].shape[1] // 2, rights[0].shape[1] // 2
    tokens = sum(a.shape[0] for a in lefts)
    rows = half // pieces
    return call(
        partial(grad_own_kernel, len(lefts)),
        "grad_own",
        (*lefts, *rights, core, shard),
        [((rows, columns), F32 if pieces > 1 and d == 0 else BF) for d in range(pieces)],
        2 * tokens * half * columns,
        scratch=[pltpu.VMEM((half, columns), F32)],
        place=place,
    )


def heads_of(value):
    return value.reshape(value.shape[:-1] + (2, PAIR // 2))


def gathered_forward(qkv, scale):
    queries = heads_of(qkv[..., :PAIR])
    both = lax.all_gather(qkv[..., PAIR:], "ctx", axis=2, tiled=True)
    length = both.shape[2]
    block = math.gcd(length, 512)
    blocks = jnp.moveaxis(both.reshape(both.shape[:2] + (length // block, block, 2 * PAIR)), 2, 0)
    shape = queries.shape[:-1]

    def step(carry, piece):
        peak, total, summed = carry
        keys, values = heads_of(piece[..., :PAIR]), heads_of(piece[..., PAIR:])
        scores = jnp.einsum("gsqhd,gskhd->gsqhk", queries, keys, preferred_element_type=F32) * scale
        new_peak = jnp.maximum(peak, jnp.max(scores, axis=-1))
        fade = jnp.exp(peak - new_peak)
        weights = jnp.exp(scores - new_peak[..., None])
        total = total * fade + jnp.sum(weights, axis=-1)
        summed = summed * fade[..., None] + jnp.einsum(
            "gsqhk,gskhd->gsqhd", weights.astype(BF), values, preferred_element_type=F32
        )
        return (new_peak, total, summed), None

    first = (
        jnp.full(shape, -1e30, F32),
        jnp.zeros(shape, F32),
        jnp.zeros(queries.shape, F32),
    )
    (peak, total, summed), _ = lax.scan(step, first, blocks)
    attended = summed / total[..., None]
    mixed = attended.reshape(qkv.shape[:-1] + (PAIR,)).astype(BF)
    return mixed, (queries, blocks, peak + jnp.log(total), attended)


def gathered_backward(saved, grad, scale):
    queries, blocks, logs, attended = saved
    out_grad = heads_of(grad)
    delta = jnp.sum(out_grad.astype(F32) * attended, axis=-1)

    def step(q_grad, piece):
        keys, values = heads_of(piece[..., :PAIR]), heads_of(piece[..., PAIR:])
        scores = jnp.einsum("gsqhd,gskhd->gsqhk", queries, keys, preferred_element_type=F32) * scale
        weights = jnp.exp(scores - logs[..., None])
        weight_grad = jnp.einsum(
            "gsqhd,gskhd->gsqhk", out_grad, values, preferred_element_type=F32
        )
        score_grad = (weights * (weight_grad - delta[..., None])).astype(BF)
        v_grad = jnp.einsum(
            "gsqhk,gsqhd->gskhd", weights.astype(BF), out_grad, preferred_element_type=F32
        )
        k_grad = jnp.einsum("gsqhk,gsqhd->gskhd", score_grad, queries, preferred_element_type=F32)
        q_grad = q_grad + scale * jnp.einsum(
            "gsqhk,gskhd->gsqhd", score_grad, keys, preferred_element_type=F32
        )
        flat = lambda a: a.reshape(a.shape[:-2] + (PAIR,))
        return q_grad, jnp.concatenate([flat(k_grad) * scale, flat(v_grad)], axis=-1).astype(BF)

    q_grad, joined = lax.scan(step, jnp.zeros(queries.shape, F32), blocks)
    joined = jnp.moveaxis(joined, 0, 2)
    joined = joined.reshape(joined.shape[:2] + (-1, 2 * PAIR))
    owned = lax.psum_scatter(joined, "ctx", scatter_dimension=2, tiled=True)
    return jnp.concatenate([q_grad.reshape(grad.shape).astype(BF), owned], axis=-1)


class Order:
    def __init__(self):
        self.last = None

    def hold(self, *values):
        if self.last is None:
            return values
        return lax.optimization_barrier((*values, self.last))[: len(values)]

    def mark(self, value):
        self.last = value
        return value


def body(
    inputs,
    time_features,
    valid_mask,
    teacher,
    w_time,
    b_time,
    w_query,
    b_query,
    w_key,
    w_value,
    b_value,
    w_output,
    b_output,
    gain_one,
    shift_one,
    w_hidden,
    b_hidden,
    w_down,
    b_down,
    gain_two,
    shift_two,
):
    positions, seqs, width = inputs.shape
    half = width // 2
    chunks = seqs // 2
    columns = w_query.shape[1]
    per_core = columns // PAIR
    pairs = 2 * per_core
    each = w_hidden.shape[1]
    scale = 1.0 / math.sqrt(D // HEADS)
    ctx = lax.axis_size("ctx")
    shards = lax.axis_size("shard")
    by_units = pairs == ctx
    shard = lax.axis_index("shard")
    core = lax.axis_index("tensor") % 2
    spot = lax.axis_index("ctx")
    slot = spot if by_units else jnp.int32(0)
    place = jnp.stack([core, shard, slot, spot]).astype(jnp.int32)
    order = Order()

    def turn(value):
        return jnp.where(
            shard == 0, value, jnp.concatenate([value[..., half:], value[..., :half]], axis=-1)
        )

    def after(value, *others):
        return lax.optimization_barrier((value, *others))[0]

    qkv_mine = pack(place, w_query, w_key, w_value)
    qkv_across = swap_shard(qkv_mine)
    qkv_side = swap_core(qkv_mine)

    bias = jnp.concatenate([b_hidden, b_query, b_value]).reshape(1, -1)
    biases = (bias, swap_core(bias))
    vec = turn(
        jnp.stack([b_output, gain_one, shift_one, b_down, gain_two, shift_two, b_down, b_down])
    )
    valid = valid_mask.T.astype(F32)
    count = jnp.full((8, 128), jnp.sum(valid), F32)
    embed = jnp.dot(time_features, w_time, preferred_element_type=F32) + b_time
    place, vec, valid, embed, count = lax.optimization_barrier((place, vec, valid, embed, count))
    count = sum_ctx(count)
    count = count + swap_shard(after(count, qkv_across))
    tokens_all = positions * seqs * ctx * shards
    rows = entry(place, inputs, embed)
    low, start = rows[:chunks], rows[chunks:]
    out_mine, feed_mine = pack_feed(after(place, low[0]), w_output, w_hidden, w_down)
    out_side, feed_side = swap_core(out_mine), swap_core(feed_mine)
    teachers = own_rows(after(place, out_mine), teacher)
    order.mark(teachers[0])

    qkv_weights = (qkv_mine, qkv_across, qkv_side, swap_core(after(qkv_across, teachers[0])))
    out_across = swap_shard(after(out_mine, qkv_across))
    slots = []
    for c in range(chunks):
        (held,) = order.hold(low[c])
        slots.append(project(place, each, held, qkv_weights, biases))
        order.mark(slots[c][0])
    feed_across = swap_shard(after(feed_mine, out_across, slots[-1][0]))
    out_weights = (out_mine, out_across, out_side, swap_core(after(out_across, slots[-1][0])))
    kept, mixed = [], []
    for c in range(chunks):
        if by_units:
            sent = slots[c]
            if c > 0:
                sent = list(lax.optimization_barrier((*sent, *kept[c - 1][0]))[: len(sent)])
            pieces = swap_ctx(sent)
            *outs, logs = attend(order.hold(*pieces), scale)
            order.mark(logs)
            mixed.append(swap_ctx(outs))
            kept.append((pieces, logs))
        else:
            value, saved = gathered_forward(jnp.stack(slots[c])[:, None], scale)
            mixed.append([value[p, 0] for p in range(pairs)])
            kept.append(saved)
    firsts, norms, hiddens, slopes, feeds, flats, branches = [], [], [], [], [], [], []
    for c in range(chunks):
        held = order.hold(*mixed[c])
        flat, mine = merge(place, held, out_weights)
        order.mark(flat)
        flats.append(flat)
        branches.append((mine, swap_outer(mine)))
    feed_weights = (feed_mine, feed_across, feed_side, swap_core(after(feed_across, order.last)))
    for c in range(chunks):
        (held,) = order.hold(start[c])
        first, normed, hidden, slope, mine = feed(held, *branches[c], vec, biases, feed_weights)
        order.mark(normed)
        firsts.append(first)
        norms.append(normed)
        hiddens.append(hidden)
        slopes.append(slope)
        feeds.append((mine, swap_outer(mine)))

    results, sum_grads, feed_lows, pre_grads, backs, two_sums, pre_sums = [], [], [], [], [], [], []
    for c in range(chunks):
        (held,) = order.hold(firsts[c])
        result, sum_grad, feed_low, pre_grad, mine, two, pre_sum = feed_back(
            place, c, tokens_all, held, *feeds[c], vec, teachers[c], valid, count, slopes[c], feed_weights
        )
        order.mark(pre_sum)
        results.append(result)
        sum_grads.append(sum_grad)
        feed_lows.append(feed_low)
        pre_grads.append(pre_grad)
        backs.append((mine, swap_outer(mine)))
        two_sums.append(two)
        pre_sums.append(pre_sum)

    class Weight:
        def __init__(self, lefts, rights):
            self.lefts, self.rights = lefts, rights

        def held(self):
            first, = order.hold(self.lefts[0])
            return [first, *self.lefts[1:]]

        def core(self):
            value = order.mark(grad_core(self.held(), self.rights))
            self.from_core = swap_core(value)

        def shard(self):
            value = order.mark(grad_shard(self.held(), self.rights, self.from_core))
            self.from_shard = swap_shard(value)

        def own(self):
            count = ctx if by_units else 1
            own = grad_own(place, self.held(), self.rights, self.from_core, self.from_shard, count)
            order.mark(own[0])
            if by_units:
                self.pieces = swap_ctx(own)
            else:
                pieces = lax.all_to_all(own[0].reshape(ctx, half // ctx, -1), "ctx", 0, 0)
                self.pieces = [jnp.sum(pieces.astype(F32), axis=0)]

        def total(self, cuts):
            outs = grad_sum(order.hold(*self.pieces), cuts)
            order.mark(outs[0])
            return outs

    first_grads, branch_lows, one_sums, mixed_grads = [], [], [], []

    def run_split(c):
        (held,) = order.hold(sum_grads[c])
        first_grad, branch_low, one, *outs = split(
            place, held, *backs[c], firsts[c], vec, out_weights
        )
        order.mark(one)
        first_grads.append(first_grad)
        branch_lows.append(branch_low)
        one_sums.append(one)
        mixed_grads.append(swap_ctx(outs) if by_units else outs)

    qkv_grads = []

    def run_attend_back(c):
        if by_units:
            pieces, logs = kept[c]
            (logs,) = order.hold(logs)
            outs = attend_back(pieces, mixed_grads[c], logs, scale)
            order.mark(outs[0])
            qkv_grads.append(swap_ctx(outs))
        else:
            value = gathered_backward(kept[c], jnp.stack(mixed_grads[c])[:, None], scale)
            qkv_grads.append([value[p, 0] for p in range(pairs)])

    qkv_sums, qkv_flats, last_parts = [], [], []

    def run_project_back(c):
        held = order.hold(*qkv_grads[c])
        flat, mine, qkv_sum = project_back(place, held, qkv_weights)
        order.mark(qkv_sum)
        qkv_sums.append(qkv_sum)
        qkv_flats.append(flat)
        last_parts.append((mine, swap_outer(mine)))

    starts, zero_sums = [], []

    def run_last(c):
        (held,) = order.hold(first_grads[c])
        start_grad, zero = last(held, *last_parts[c])
        order.mark(zero)
        starts.append(start_grad)
        zero_sums.append(zero)

    down = Weight(feed_lows, hiddens)
    hidden = Weight(norms, pre_grads)
    output = Weight(branch_lows, flats)
    qkv = Weight(low, qkv_flats)
    down.core()
    run_split(0)
    hidden.core()
    down.shard()
    (held,) = order.hold(place)
    layer_out = order.mark(leave(held, results))
    run_split(1)
    hidden.shard()
    run_attend_back(0)
    output.core()
    run_attend_back(1)
    output.shard()
    run_project_back(0)
    run_project_back(1)
    qkv.core()
    down.own()
    qkv.shard()
    run_last(0)
    run_last(1)
    packed = order.mark(
        tally(place, each, two_sums, one_sums, pre_sums, qkv_sums, zero_sums, time_features)
    )
    packed = sum_tokens(packed + swap_core(packed))
    hidden.own()
    qkv.own()
    output.own()
    (held,) = order.hold(place)
    grad_inputs = order.mark(leave(held, starts))
    everything = lambda weight: [[(0, weight.rights[0].shape[1] // 2)]]
    (grad_w_down,) = down.total(everything(down))
    (grad_w_hidden,) = hidden.total(everything(hidden))
    (grad_w_output,) = output.total(everything(output))
    grad_w_query, grad_w_key, grad_w_value = qkv.total(
        [[((3 * g + j) * PAIR, PAIR) for g in range(per_core)] for j in range(3)]
    )

    (held,) = order.hold(place)
    grad_w_time, loss, start_sum, hidden_sum, qkv_sum, *rest = finish(
        held, each, 3 * columns, shards * seqs, shards, time_features.shape[1], packed, count
    )
    qkv_sum = qkv_sum.reshape(per_core, 3, PAIR)
    return (
        layer_out,
        loss.reshape(()),
        grad_inputs,
        grad_w_time,
        start_sum.reshape(-1),
        grad_w_query,
        qkv_sum[:, 0].reshape(-1),
        grad_w_key,
        grad_w_value,
        qkv_sum[:, 2].reshape(-1),
        grad_w_output,
        rest[5].reshape(-1),
        rest[3].reshape(-1),
        rest[4].reshape(-1),
        grad_w_hidden,
        hidden_sum.reshape(-1),
        grad_w_down,
        rest[2].reshape(-1),
        rest[0].reshape(-1),
        rest[1].reshape(-1),
    )


def solution(mesh):
    placed = (
        P("ctx", "shard", None),
        P("shard", None),
        P("ctx", "shard"),
        P("ctx", "shard", None),
        P(),
        P(),
        P("shard", "tensor"),
        P("tensor"),
        P("shard", "tensor"),
        P("shard", "tensor"),
        P("tensor"),
        P("shard", "tensor"),
        P(),
        P(),
        P(),
        P("shard", "tensor"),
        P("tensor"),
        P("shard", "tensor"),
        P(),
        P(),
        P(),
    )
    return jax.shard_map(
        body,
        mesh=mesh,
        in_specs=placed,
        out_specs=(
            P("ctx", "shard", None),
            P(),
            P("ctx", "shard", None),
            P(),
            P(),
            P(("shard", "ctx"), "tensor"),
            P("tensor"),
            P(("shard", "ctx"), "tensor"),
            P(("shard", "ctx"), "tensor"),
            P("tensor"),
            P(("shard", "ctx"), "tensor"),
            P(),
            P(),
            P(),
            P(("shard", "ctx"), "tensor"),
            P("tensor"),
            P(("shard", "ctx"), "tensor"),
            P(),
            P(),
            P(),
        ),
        check_vma=False,
    )
```

```python
from functools import partial
import math

import jax
import jax.numpy as jnp
from jax import lax
from jax.experimental import pallas as pl
from jax.experimental.pallas import tpu as pltpu
from jax.sharding import PartitionSpec as P

D = 1024
HEADS = 16
BF = jnp.bfloat16
F32 = jnp.float32
PAIR = 128
EPS = 1e-05


def contract(left, right, left_dim, right_dim):
    return lax.dot_general(
        left, right, (((left_dim,), (right_dim,)), ((), ())), preferred_element_type=F32
    )


PINNED = False
SCALES = {"project": 0.1, "attend": 1, "merge": 0.1, "feed": 0.1, "feed_back": 0.003, "split": 30, "attend_back": 1, "project_back": 100, "last": 10, "grad_core": 30, "grad_shard": 30, "grad_own": 30, "grad_sum": 30, "tally": 30, "leave": 30, "entry": 10, "own_rows": 1, "pack": 0.01, "pack_feed": 0.01}


def cost(name, flops, nbytes):
    scale = SCALES.get(name, 1)
    return pl.CostEstimate(
        flops=int(flops * scale), bytes_accessed=int(nbytes * scale), transcendentals=0
    )


def swap(value, axis, bit):
    size = lax.axis_size(axis)
    return lax.ppermute(value, axis, [(i, i ^ bit) for i in range(size)])


def swap_core(value):
    return swap(value, "tensor", 1)


def swap_outer(value):
    return swap(value, "tensor", 2)


def swap_shard(value):
    return swap(value, "shard", 1)


def swap_ctx(pieces):
    moved = {d: swap(pieces[d], "ctx", d) for d in reversed(range(1, len(pieces)))}
    return [pieces[0]] + [moved[d] for d in range(1, len(pieces))]


def sum_ctx(value):
    size = lax.axis_size("ctx")
    if size & (size - 1):
        return lax.psum(value, "ctx")
    bit = 1
    while bit < size:
        value = value + swap(value, "ctx", bit)
        bit *= 2
    return value


def sum_tokens(value):
    return sum_ctx(value + swap_shard(value))


def grid_call(kernel, name, grid, ins, outs, work, place, pinned=True):
    args = [a for a, _, _ in ins]
    nbytes = sum(a.size * a.dtype.itemsize for a in args)
    nbytes += sum(math.prod(s) * jnp.dtype(d).itemsize for s, d, _, _ in outs)
    without = lambda f: (lambda *i: f(*i[: len(grid)]))
    if pinned:
        args = [pltpu.with_memory_space_constraint(a, pltpu.HBM) for a in args]
    return pl.pallas_call(
        kernel,
        grid_spec=pltpu.PrefetchScalarGridSpec(
            num_scalar_prefetch=1,
            grid=grid,
            in_specs=[pl.BlockSpec(b, without(f)) for _, b, f in ins],
            out_specs=[pl.BlockSpec(b, without(f)) for _, _, b, f in outs],
        ),
        out_shape=[jax.ShapeDtypeStruct(s, d) for s, d, _, _ in outs],
        cost_estimate=cost(name, work, nbytes),
        compiler_params=pltpu.CompilerParams(vmem_limit_bytes=16 << 20),
        name=name,
    )(place, *args)


def call(kernel, name, args, outs, work, scratch=(), place=None, room=12, pinned=PINNED):
    nbytes = sum(a.size * a.dtype.itemsize for a in args)
    nbytes += sum(math.prod(s) * jnp.dtype(d).itemsize for s, d in outs)
    first = [] if place is None else [place]
    if pinned:
        args = [pltpu.with_memory_space_constraint(a, pltpu.VMEM) for a in args]
    return pl.pallas_call(
        kernel,
        in_specs=[pl.BlockSpec(memory_space=pltpu.SMEM)] * len(first)
        + [pl.BlockSpec(memory_space=pltpu.VMEM)] * len(args),
        out_specs=[pl.BlockSpec(memory_space=pltpu.VMEM)] * len(outs),
        out_shape=[jax.ShapeDtypeStruct(s, d) for s, d in outs],
        scratch_shapes=scratch,
        cost_estimate=cost(name, work, nbytes),
        compiler_params=pltpu.CompilerParams(vmem_limit_bytes=room << 20),
        name=name,
    )(*first, *args)


def whole(array):
    rank = array.ndim
    return (array, array.shape, lambda *i: (0,) * rank)


def turned(value, flip):
    half = value.shape[1] // 2
    return jnp.where(flip == 0, value, jnp.concatenate([value[:, half:], value[:, :half]], axis=1))


def entry_kernel(chunks, place, x_ref, embed_ref, *out_refs):
    core, flip = place[0], place[1]
    x = x_ref[...].astype(F32)
    rows = [x[:, s, :] + embed_ref[s : s + 1, :] for s in range(2 * chunks)]
    for c in range(chunks):
        own = turned(jnp.where(core == 0, rows[c], rows[chunks + c]), flip)
        out_refs[c][...] = own.astype(BF)
        out_refs[chunks + c][...] = own


def entry(place, x, embed):
    positions, seqs, width = x.shape
    chunks = seqs // 2
    block = math.gcd(64, positions)
    return grid_call(
        partial(entry_kernel, chunks),
        "entry",
        (positions // block,),
        [(x, (block, seqs, width), lambda i: (i, 0, 0)), whole(embed)],
        [
            ((positions, width), dtype, (block, width), lambda i: (i, 0))
            for dtype in (BF, F32)
            for _ in range(chunks)
        ],
        4 * x.size,
        place=place,
    )


def own_kernel(chunks, place, x_ref, *out_refs):
    core, flip = place[0], place[1]
    x = x_ref[...].astype(F32)
    for c in range(chunks):
        own = jnp.where(core == 0, x[:, c, :], x[:, chunks + c, :])
        out_refs[c][...] = turned(own, flip).astype(BF)


def own_rows(place, x):
    positions, seqs, width = x.shape
    chunks = seqs // 2
    block = math.gcd(64, positions)
    return grid_call(
        partial(own_kernel, chunks),
        "own_rows",
        (positions // block,),
        [(x, (block, seqs, width), lambda i: (i, 0, 0))],
        [((positions, width), BF, (block, width), lambda i: (i, 0))] * chunks,
        2 * x.size,
        place=place,
    )


def leave_kernel(chunks, dtype, place, own_ref, other_ref, out_ref):
    core, flip = place[0], place[1]
    own = [turned(own_ref[c].astype(F32), flip) for c in range(chunks)]
    other = [turned(other_ref[c].astype(F32), flip) for c in range(chunks)]
    rows = [jnp.where(core == 0, a, b) for a, b in zip(own, other)]
    rows += [jnp.where(core == 0, b, a) for a, b in zip(own, other)]
    out_ref[...] = jnp.stack(rows, axis=1).astype(dtype)


def leave(place, own, other):
    chunks, positions, width = own.shape
    block = math.gcd(64, positions)
    piece = ((chunks, block, width), lambda i: (0, i, 0))
    return grid_call(
        partial(leave_kernel, chunks, own.dtype),
        "leave",
        (positions // block,),
        [(own, *piece), (other, *piece)],
        [
            (
                (positions, 2 * chunks, width),
                own.dtype,
                (block, 2 * chunks, width),
                lambda i: (i, 0, 0),
            )
        ],
        2 * own.size,
        place=place,
        pinned=False,
    )[0]


def pack_kernel(place, q_ref, k_ref, v_ref, out_ref):
    for g in range(q_ref.shape[1] // PAIR):
        for j, ref in enumerate((q_ref, k_ref, v_ref)):
            at = (3 * g + j) * PAIR
            out_ref[:, at : at + PAIR] = ref[:, g * PAIR : (g + 1) * PAIR]


def pack(place, q, k, v):
    rows, columns = q.shape
    return grid_call(
        pack_kernel,
        "pack",
        (1,),
        [whole(q), whole(k), whole(v)],
        [((rows, 3 * columns), BF, (rows, 3 * columns), lambda i: (0, 0))],
        0,
        place,
    )[0]


def pack_feed_kernel(place, out_ref, up_ref, down_ref, copy_ref, both_ref):
    each = up_ref.shape[1]
    copy_ref[...] = out_ref[...]
    both_ref[:, :each] = up_ref[...]
    both_ref[:, each:] = down_ref[...]


def pack_feed(place, out, up, down):
    rows, each = up.shape
    block = math.gcd(128, rows)
    tall = lambda a: (a, (block, a.shape[1]), lambda i: (i, 0))
    return grid_call(
        pack_feed_kernel,
        "pack_feed",
        (rows // block,),
        [tall(out), tall(up), tall(down)],
        [
            (out.shape, BF, (block, out.shape[1]), lambda i: (i, 0)),
            ((rows, 2 * each), BF, (block, 2 * each), lambda i: (i, 0)),
        ],
        0,
        place,
    )


def project_kernel(shift, place, x_ref, a_ref, b_ref, c_ref, d_ref, bias_ref, more_ref, *outs_and_all):
    *outs, pairs_ref = outs_and_all
    half = x_ref.shape[1] // 2
    per_core = len(outs) // 2
    wide = 3 * PAIR
    for core, (top, bottom) in enumerate(((a_ref, b_ref), (c_ref, d_ref))):

        def step(g, carry, core=core, top=top, bottom=bottom):
            at = pl.ds(pl.multiple_of(g * wide, wide), wide)
            value = contract(x_ref[:, :half], top[:, at], 1, 0)
            value += contract(x_ref[:, half:], bottom[:, at], 1, 0)
            pair = core * per_core + g
            bias = (bias_ref, more_ref)[core]
            for j, first in enumerate((shift, None, shift + per_core * PAIR)):
                part = value[:, j * PAIR : (j + 1) * PAIR]
                if first is not None:
                    part += bias[:, pl.ds(pl.multiple_of(first + g * PAIR, PAIR), PAIR)]
                pairs_ref[pair, :, j * PAIR : (j + 1) * PAIR] = part.astype(BF)
            return carry

        lax.fori_loop(0, per_core, step, 0)
    for d, out in enumerate(outs):
        out[...] = pairs_ref[place[2] ^ d]


def project(place, shift, x, weights, biases):
    rows, width = x.shape
    pairs = 2 * weights[0].shape[1] // (3 * PAIR)
    return call(
        partial(project_kernel, shift),
        "project",
        (x, *weights, *biases),
        [((rows, 3 * PAIR), BF)] * pairs,
        2 * rows * width * pairs * 3 * PAIR,
        scratch=[pltpu.VMEM((pairs, rows, 3 * PAIR), BF)],
        place=place,
    )


def project_back_kernel(pairs, place, *refs):
    pieces, (a_ref, b_ref, c_ref, d_ref, flat_ref, out_ref, sums_ref, start_ref, pairs_ref) = (
        refs[:pairs],
        refs[pairs:],
    )
    for d, piece in enumerate(pieces):
        pairs_ref[place[2] ^ d] = piece[...]
    wide = 3 * PAIR
    for p in range(pairs):
        flat_ref[:, p * wide : (p + 1) * wide] = pairs_ref[p]
    half = a_ref.shape[0]
    middle = a_ref.shape[1]
    for at, first, second in ((0, a_ref, c_ref), (half, b_ref, d_ref)):
        value = contract(flat_ref[:, :middle], first[...], 1, 1)
        value += contract(flat_ref[:, middle:], second[...], 1, 1)
        out_ref[:, at : at + half] = value.astype(BF)
        start_ref[:, at : at + half] = sum_rows(value)
    sums_ref[...] = sum_rows(flat_ref[...].astype(F32))


def project_back(place, pieces, weights):
    rows, columns = pieces[0].shape
    pairs = len(pieces)
    width = 2 * weights[0].shape[0]
    return call(
        partial(project_back_kernel, pairs),
        "project_back",
        (*pieces, *weights),
        [
            ((rows, pairs * columns), BF),
            ((rows, width), BF),
            ((1, pairs * columns), F32),
            ((1, width), F32),
        ],
        2 * rows * width * pairs * columns,
        scratch=[pltpu.VMEM((pairs, rows, columns), BF)],
        place=place,
    )


def merge_kernel(pairs, place, *refs):
    pieces, (a_ref, b_ref, c_ref, d_ref, flat_ref, out_ref, pairs_ref) = refs[:pairs], refs[pairs:]
    for d, piece in enumerate(pieces):
        pairs_ref[place[2] ^ d] = piece[...]
    for p in range(pairs):
        flat_ref[:, p * PAIR : (p + 1) * PAIR] = pairs_ref[p]
    half = a_ref.shape[0]
    middle = a_ref.shape[1]
    for at, first, second in ((0, a_ref, c_ref), (half, b_ref, d_ref)):
        value = contract(flat_ref[:, :middle], first[...], 1, 1)
        value += contract(flat_ref[:, middle:], second[...], 1, 1)
        out_ref[:, at : at + half] = value.astype(BF)


def merge(place, pieces, weights):
    rows, columns = pieces[0].shape
    pairs = len(pieces)
    width = 2 * weights[0].shape[0]
    return call(
        partial(merge_kernel, pairs),
        "merge",
        (*pieces, *weights),
        [((rows, pairs * columns), BF), ((rows, width), BF)],
        2 * rows * width * pairs * columns,
        scratch=[pltpu.VMEM((pairs, rows, columns), BF)],
        place=place,
    )


def lanes_of(part):
    lane = lax.broadcasted_iota(jnp.int32, (1, PAIR), 1)
    return lane < PAIR // 2 if part == 0 else lane >= PAIR // 2


def attend_kernel(scale, pieces, *refs):
    ins, outs, (log_ref, mixed_ref) = refs[:pieces], refs[pieces : 2 * pieces], refs[2 * pieces :]
    rows = ins[0].shape[0]
    join = lambda at: jnp.concatenate([ref[:, at : at + PAIR] for ref in ins], axis=0)
    q, k, v = join(0) * BF(scale), join(PAIR), join(2 * PAIR)
    lane = lax.broadcasted_iota(jnp.int32, (1, PAIR), 1)
    mixed_ref[...] = jnp.zeros_like(mixed_ref)

    def head(part, carry):
        lanes = (lane >= PAIR // 2) == (part == 1)
        k_head, v_head = jnp.where(lanes, k, BF(0)), jnp.where(lanes, v, BF(0))
        scores = contract(k_head, q, 1, 1)
        peak = jnp.max(scores, axis=0, keepdims=True)
        weights = jnp.exp(scores - peak)
        total = jnp.sum(weights, axis=0, keepdims=True)
        mixed_ref[...] += contract(v_head, weights.astype(BF), 0, 0) * (1.0 / total)
        log_ref[pl.ds(part, 1), :] = peak + jnp.log(total)
        return carry

    lax.fori_loop(0, 2, head, 0)
    mixed = mixed_ref[...].T.astype(BF)
    for d, out in enumerate(outs):
        out[...] = mixed[d * rows : (d + 1) * rows]


def attend(pieces, scale):
    rows = pieces[0].shape[0]
    length = rows * len(pieces)
    return call(
        partial(attend_kernel, scale, len(pieces)),
        "attend",
        pieces,
        [((rows, PAIR), BF)] * len(pieces) + [((2, length), F32)],
        16 * length * length * PAIR,
        scratch=[pltpu.VMEM((PAIR, length), F32)],
        room=24,
    )


def attend_back_kernel(scale, pieces, *refs):
    ins, grads = refs[:pieces], refs[pieces : 2 * pieces]
    log_ref, outs = refs[2 * pieces], refs[2 * pieces + 1 : 3 * pieces + 1]
    k_sum, v_sum, q_sum, q_ref, grad_ref = refs[3 * pieces + 1 :]
    rows = ins[0].shape[0]
    length = rows * pieces
    join = lambda refs, at: jnp.concatenate([ref[:, at : at + PAIR] for ref in refs], axis=0)
    k, v = join(ins, PAIR), join(ins, 2 * PAIR)
    q_ref[...] = join(ins, 0) * BF(scale)
    grad_ref[...] = join(grads, 0)
    k_sum[...] = jnp.zeros_like(k_sum)
    v_sum[...] = jnp.zeros_like(v_sum)
    q_sum[...] = jnp.zeros_like(q_sum)
    lane = lax.broadcasted_iota(jnp.int32, (1, PAIR), 1)
    block = math.gcd(512, length)

    def step(i, carry):
        part = i % 2
        at = pl.ds(pl.multiple_of(i // 2 * block, block), block)
        lanes = (lane >= PAIR // 2) == (part == 1)
        q, grad = q_ref[at, :], grad_ref[at, :]
        k_head, v_head = jnp.where(lanes, k, BF(0)), jnp.where(lanes, v, BF(0))
        q_head, grad_head = jnp.where(lanes, q, BF(0)), jnp.where(lanes, grad, BF(0))
        probs = jnp.exp(contract(k_head, q, 1, 1) - log_ref[pl.ds(part, 1), at])
        probs_grad = contract(v_head, grad, 1, 1)
        delta = jnp.sum(probs * probs_grad, axis=0, keepdims=True)
        scores_grad = (probs * (probs_grad - delta)).astype(BF)
        v_sum[...] += contract(probs.astype(BF), grad_head, 1, 0)
        k_sum[...] += contract(scores_grad, q_head, 1, 0)
        q_sum[:, at] += contract(k_head, scores_grad, 0, 0)
        return carry

    lax.fori_loop(0, 2 * length // block, step, 0)
    q_grad = (q_sum[...] * scale).T.astype(BF)
    for d, out in enumerate(outs):
        at = slice(d * rows, (d + 1) * rows)
        out[:, 0:PAIR] = q_grad[at, :]
        out[:, PAIR : 2 * PAIR] = k_sum[at, :].astype(BF)
        out[:, 2 * PAIR : 3 * PAIR] = v_sum[at, :].astype(BF)


def attend_back(pieces, grads, logs, scale):
    rows = pieces[0].shape[0]
    length = rows * len(pieces)
    return call(
        partial(attend_back_kernel, scale, len(pieces)),
        "attend_back",
        (*pieces, *grads, logs),
        [((rows, 3 * PAIR), BF)] * len(pieces),
        40 * length * length * PAIR,
        scratch=[pltpu.VMEM((length, PAIR), F32)] * 2
        + [pltpu.VMEM((PAIR, length), F32)]
        + [pltpu.VMEM((length, PAIR), BF)] * 2,
        room=24,
    )


def sum_rows(value):
    return jnp.sum(value, axis=0, keepdims=True)


def normal(value):
    center = jnp.mean(value, axis=-1, keepdims=True)
    offset = value - center
    spread = jnp.mean(offset * offset, axis=-1, keepdims=True)
    inverse = lax.rsqrt(spread + EPS)
    return offset * inverse, inverse


def normal_back(grad, unit, inverse):
    return inverse * (
        grad
        - jnp.mean(grad, axis=-1, keepdims=True)
        - unit * jnp.mean(grad * unit, axis=-1, keepdims=True)
    )


def by_rows(rows, run):
    size = math.gcd(64, rows)

    def step(i, carry):
        run(pl.ds(pl.multiple_of(i * size, size), size))
        return carry

    lax.fori_loop(0, rows // size, step, 0)


def feed_kernel(
    start_ref, mine_ref, theirs_ref, vec_ref, bias_ref, more_ref, a_ref, b_ref, c_ref, d_ref,
    first_ref, low_ref, hidden_ref, slope_ref, out_ref, acc,
):
    def norm(at):
        total = start_ref[at, :] + mine_ref[at, :].astype(F32) + theirs_ref[at, :].astype(F32)
        total += vec_ref[0:1, :]
        first_ref[at, :] = total
        unit, _ = normal(total)
        low_ref[at, :] = (unit * vec_ref[1:2, :] + vec_ref[2:3, :]).astype(BF)

    by_rows(start_ref.shape[0], norm)
    half, each = a_ref.shape[0], a_ref.shape[1] // 2
    size = math.gcd(512, each)
    acc[...] = jnp.zeros_like(acc)
    for core, (top, bottom) in enumerate(((a_ref, b_ref), (c_ref, d_ref))):

        def step(i, carry, core=core, top=top, bottom=bottom):
            here = pl.ds(pl.multiple_of(i * size, size), size)
            at = pl.ds(pl.multiple_of(core * each + i * size, size), size)
            down = pl.ds(pl.multiple_of(each + i * size, size), size)
            pre = contract(low_ref[:, :half], top[:, here], 1, 0)
            pre += contract(low_ref[:, half:], bottom[:, here], 1, 0)
            pre += (bias_ref, more_ref)[core][:, here]
            phi = 0.5 + 0.5 * lax.erf(pre * math.sqrt(0.5))
            hidden = (pre * phi).astype(BF)
            hidden_ref[:, at] = hidden
            bell = jnp.exp(-0.5 * (pre * pre)) * (1.0 / math.sqrt(2.0 * math.pi))
            slope_ref[:, at] = (phi + pre * bell).astype(BF)
            for k, weight in ((0, top), (half, bottom)):
                acc[:, k : k + half] += contract(hidden, weight[:, down], 1, 1)
            return carry

        lax.fori_loop(0, each // size, step, 0)
    out_ref[...] = acc[...].astype(BF)


def feed(start, mine, theirs, vec, biases, weights):
    rows, width = start.shape
    units = weights[0].shape[1]
    return call(
        feed_kernel,
        "feed",
        (start, mine, theirs, vec, *biases, *weights),
        [
            ((rows, width), F32),
            ((rows, width), BF),
            ((rows, units), BF),
            ((rows, units), BF),
            ((rows, width), BF),
        ],
        4 * rows * width * units,
        scratch=[pltpu.VMEM((rows, width), F32)],
    )


def feed_back_kernel(
    valid_row, tokens, place, earlier_ref, first_ref, mine_ref, theirs_ref, vec_ref, teacher_ref, valid_ref, count_ref, slope_ref,
    a_ref, b_ref, c_ref, d_ref, result_ref, grad_ref, low_ref, pre_ref, out_ref, sums_ref, pre_sums_ref, acc, valid_sums,
):
    second = valid_ref.shape[0] // 2 + valid_row
    valid = jnp.where(
        place[0] == 0, valid_ref[valid_row : valid_row + 1, :], valid_ref[second : second + 1, :]
    )
    for c in range(valid_row):
        result_ref[c] = earlier_ref[c]
    valid_sums[...] = jnp.broadcast_to(valid, (PAIR, valid.shape[1])).T
    sums_ref[...] = jnp.zeros_like(sums_ref)
    factor = 2.0 * tokens / count_ref[0:1, 0:1]

    def norm(at):
        valid = valid_sums[at, 0:1]
        unit, _ = normal(first_ref[at, :])
        normed = unit * vec_ref[1:2, :] + vec_ref[2:3, :]
        total = normed + mine_ref[at, :].astype(F32) + theirs_ref[at, :].astype(F32) + vec_ref[3:4, :]
        unit, inverse = normal(total)
        result = unit * vec_ref[4:5, :] + vec_ref[5:6, :]
        result_ref[valid_row, at, :] = result.astype(BF)
        error = result - teacher_ref[at, :].astype(F32)
        result_grad = valid * factor * error
        grad = normal_back(result_grad * vec_ref[4:5, :], unit, inverse)
        grad_ref[at, :] = grad
        low = grad.astype(BF)
        low_ref[at, :] = low
        sums_ref[0:1, :] += sum_rows(result_grad * unit)
        sums_ref[1:2, :] += sum_rows(result_grad)
        sums_ref[2:3, :] += sum_rows(low.astype(F32))
        sums_ref[3:4, :] += sum_rows(valid * error * error)

    by_rows(first_ref.shape[0], norm)
    half, each = a_ref.shape[0], a_ref.shape[1] // 2
    size = math.gcd(512, each)
    acc[...] = jnp.zeros_like(acc)
    for core, (top, bottom) in enumerate(((a_ref, b_ref), (c_ref, d_ref))):

        def step(i, carry, core=core, top=top, bottom=bottom):
            here = pl.ds(pl.multiple_of(i * size, size), size)
            at = pl.ds(pl.multiple_of(core * each + i * size, size), size)
            down = pl.ds(pl.multiple_of(each + i * size, size), size)
            value = contract(low_ref[:, :half], top[:, down], 1, 0)
            value += contract(low_ref[:, half:], bottom[:, down], 1, 0)
            pre_grad = (value * slope_ref[:, at].astype(F32)).astype(BF)
            pre_ref[:, at] = pre_grad
            pre_sums_ref[:, at] = sum_rows(pre_grad.astype(F32))
            for k, weight in ((0, top), (half, bottom)):
                acc[:, k : k + half] += contract(pre_grad, weight[:, here], 1, 1)
            return carry

        lax.fori_loop(0, each // size, step, 0)
    out_ref[...] = acc[...].astype(BF)


def feed_back(place, row, tokens, earlier, first, mine, theirs, vec, teacher, valid, count, slope, weights):
    rows, width = first.shape
    units = slope.shape[1]
    return call(
        partial(feed_back_kernel, row, tokens),
        "feed_back",
        (earlier, first, mine, theirs, vec, teacher, valid, count, slope, *weights),
        [
            ((row + 1, rows, width), BF),
            ((rows, width), F32),
            ((rows, width), BF),
            ((rows, units), BF),
            ((rows, width), BF),
            ((8, width), F32),
            ((1, units), F32),
        ],
        4 * rows * width * units,
        scratch=[pltpu.VMEM((rows, width), F32), pltpu.VMEM((rows, PAIR), F32)],
        place=place,
    )


def split_kernel(place, grad_ref, mine_ref, theirs_ref, first_ref, vec_ref, a_ref, b_ref, c_ref, d_ref, out_ref, low_ref, sums_ref, *outs_and_all):
    *outs, pairs_ref = outs_and_all
    sums_ref[...] = jnp.zeros_like(sums_ref)

    def norm(at):
        grad = grad_ref[at, :] + mine_ref[at, :].astype(F32) + theirs_ref[at, :].astype(F32)
        unit, inverse = normal(first_ref[at, :])
        out = normal_back(grad * vec_ref[1:2, :], unit, inverse)
        out_ref[at, :] = out
        low = out.astype(BF)
        low_ref[at, :] = low
        sums_ref[0:1, :] += sum_rows(grad * unit)
        sums_ref[1:2, :] += sum_rows(grad)
        sums_ref[2:3, :] += sum_rows(low.astype(F32))
        sums_ref[3:4, :] += sum_rows(out)

    by_rows(grad_ref.shape[0], norm)
    half = a_ref.shape[0]
    per_core = len(outs) // 2
    for core, (top, bottom) in enumerate(((a_ref, b_ref), (c_ref, d_ref))):
        mixed = contract(low_ref[:, :half], top[...], 1, 0)
        mixed += contract(low_ref[:, half:], bottom[...], 1, 0)
        mixed = mixed.astype(BF)
        for p in range(per_core):
            pairs_ref[core * per_core + p] = mixed[:, p * PAIR : (p + 1) * PAIR]
    for d, piece in enumerate(outs):
        piece[...] = pairs_ref[place[2] ^ d]


def split(place, grad, mine, theirs, first, vec, weights):
    rows, width = grad.shape
    pairs = 2 * weights[0].shape[1] // PAIR
    return call(
        split_kernel,
        "split",
        (grad, mine, theirs, first, vec, *weights),
        [((rows, width), F32), ((rows, width), BF), ((8, width), F32)]
        + [((rows, PAIR), BF)] * pairs,
        2 * rows * width * pairs * PAIR,
        scratch=[pltpu.VMEM((pairs, rows, PAIR), BF)],
        place=place,
    )


def last_kernel(row, earlier_ref, grad_ref, mine_ref, theirs_ref, out_ref):
    for c in range(row):
        out_ref[c] = earlier_ref[c]
    out_ref[row] = grad_ref[...] + mine_ref[...].astype(F32) + theirs_ref[...].astype(F32)


def last(row, earlier, grad, mine, theirs):
    rows, width = grad.shape
    return call(
        partial(last_kernel, row),
        "last",
        (earlier, grad, mine, theirs),
        [((row + 1, rows, width), F32)],
        4 * rows * width,
    )[0]


def tally_kernel(chunks, each, place, *refs):
    two, one = refs[:chunks], refs[chunks : 2 * chunks]
    pre, qkv = refs[2 * chunks : 3 * chunks], refs[3 * chunks : 4 * chunks]
    start, (features_ref, out_ref) = refs[4 * chunks : 5 * chunks], refs[5 * chunks :]
    core, flip, spot = place[0], place[1], place[3]
    add = lambda parts: sum(parts[1:], parts[0])
    out_ref[...] = jnp.zeros_like(out_ref)
    out_ref[0:4, :] = turned(add([ref[0:4, :] for ref in two]), flip)
    out_ref[4:7, :] = turned(add([ref[0:3, :] for ref in one]), flip)
    pre = add([ref[...] for ref in pre])
    qkv = add([ref[...] for ref in qkv])
    size = qkv.shape[1] // 2
    for slot in range(2):
        mine = core == slot
        out_ref[8 + slot : 9 + slot, :] = jnp.where(mine, pre[:, :each], pre[:, each:])
        out_ref[10 + slot : 11 + slot, :size] = jnp.where(mine, qkv[:, :size], qkv[:, size:])
    seqs = 2 * chunks
    features = features_ref[...].astype(F32)
    wide = features.shape[1]
    for s in range(2):
        here = jnp.logical_and(jnp.logical_and(core == 0, spot == 0), flip == s)
        for k in range(seqs):
            value = jnp.where(here, features[k : k + 1, :], 0.0)
            out_ref[12 + s : 13 + s, k * wide : (k + 1) * wide] = value
    for s in range(2 * seqs):
        here = jnp.logical_and(flip == s // seqs, core == s % seqs // chunks)
        row = turned(0.5 * one[s % chunks][3:4, :] + start[s % chunks][...], flip)
        out_ref[16 + s : 17 + s, :] = jnp.where(here, row, 0.0)


def tally(place, each, two, one, pre, qkv, start, features):
    rows = -(-(16 + 2 * features.shape[0]) // 8) * 8
    return call(
        partial(tally_kernel, len(two), each),
        "tally",
        (*two, *one, *pre, *qkv, *start, features),
        [((rows, two[0].shape[1]), F32)],
        0,
        place=place,
    )[0]


def grad_sum_kernel(pieces, cuts, *refs):
    total = refs[0][...].astype(F32)
    for ref in refs[1:pieces]:
        total = total + ref[...].astype(F32)
    for out, parts in zip(refs[pieces:], cuts):
        at = 0
        for start, size in parts:
            out[:, at : at + size] = total[:, start : start + size]
            at += size


def grad_sum(pieces, cuts):
    rows = pieces[0].shape[0]
    return call(
        partial(grad_sum_kernel, len(pieces), cuts),
        "grad_sum",
        pieces,
        [((rows, sum(size for _, size in parts)), F32) for parts in cuts],
        len(pieces) * pieces[0].size,
    )


def finish_kernel(each, size, shards, place, packed_ref, other_ref, count_ref, time_ref, loss_ref, start_ref, hidden_ref, qkv_ref, *outs_and_all):
    *outs, all_ref = outs_and_all
    seqs = all_ref.shape[0]
    wide = all_ref.shape[1]
    per_row = seqs // shards
    for s in range(seqs):
        k = s % per_row
        row = 12 + s // per_row
        all_ref[s : s + 1, :] = packed_ref[row : row + 1, k * wide : (k + 1) * wide]
    grads = packed_ref[16 : 16 + seqs, :] + other_ref[...]
    time_ref[...] = lax.dot_general(
        all_ref[...],
        grads,
        (((0,), (0,)), ((), ())),
        precision=lax.Precision.HIGHEST,
        preferred_element_type=F32,
    )
    start_ref[...] = sum_rows(grads)
    total = jnp.sum(packed_ref[3:4, :], axis=1, keepdims=True)
    loss_ref[...] = total / (packed_ref.shape[1] * count_ref[0:1, 0:1])
    first = place[0] == 0
    hidden_ref[...] = jnp.where(first, packed_ref[8:9, :], packed_ref[9:10, :])[:, :each]
    qkv_ref[...] = jnp.where(first, packed_ref[10:11, :], packed_ref[11:12, :])[:, :size]
    for out, row in zip(outs, (0, 1, 2, 4, 5, 6)):
        out[...] = packed_ref[row : row + 1, :]


def finish(place, each, size, seqs, shards, wide, packed, other, count):
    width = packed.shape[1]
    return call(
        partial(finish_kernel, each, size, shards),
        "finish",
        (packed, other, count),
        [((wide, width), F32), ((1, 1), F32), ((1, width), F32), ((1, each), F32), ((1, size), F32)]
        + [((1, width), F32)] * 6,
        0,
        scratch=[pltpu.VMEM((seqs, wide), F32)],
        place=place,
    )


def token_sum(lefts, rights, rows, columns):
    total = None
    for left, right in zip(lefts, rights):
        term = contract(left[:, rows], right[:, columns], 0, 0)
        total = term if total is None else total + term
    return total


def each_weight(weights, refs):
    at, column, out = 0, 0, []
    for chunks, columns in weights:
        out.append((refs[at : at + chunks], refs[at + chunks : at + 2 * chunks], column, columns))
        at += 2 * chunks
        column += columns
    return out, refs[at:]


def weight_args(weights):
    args = [a for lefts, rights in weights for a in (*lefts, *rights)]
    shapes = [(len(lefts), rights[0].shape[1] // 2) for lefts, rights in weights]
    tokens = sum(a.shape[0] for a in weights[0][0])
    return args, shapes, weights[0][0][0].shape[1], sum(c for _, c in shapes), tokens


def grad_core_kernel(weights, *refs):
    weights, (out_ref,) = each_weight(weights, refs)
    rows = out_ref.shape[0]
    step = math.gcd(512, rows)

    def part(i, carry):
        at = pl.ds(pl.multiple_of(i * step, step), step)
        for lefts, rights, first, columns in weights:
            value = token_sum(lefts, rights, at, slice(columns, 2 * columns))
            out_ref[at, first : first + columns] = value.astype(BF)
        return carry

    lax.fori_loop(0, rows // step, part, 0)


def grad_core(weights):
    args, shapes, rows, columns, tokens = weight_args(weights)
    return call(
        partial(grad_core_kernel, shapes),
        "grad_core",
        args,
        [((rows, columns), BF)],
        2 * tokens * rows * columns,
    )[0]


def grad_shard_kernel(weights, *refs):
    weights, (core_ref, out_ref) = each_weight(weights, refs)
    half = out_ref.shape[0]
    size = math.gcd(256, half)

    def step(i, carry):
        at = pl.ds(pl.multiple_of(i * size, size), size)
        far = pl.ds(pl.multiple_of(half + i * size, size), size)
        for lefts, rights, first, columns in weights:
            here = slice(first, first + columns)
            value = token_sum(lefts, rights, far, slice(0, columns))
            out_ref[at, here] = (value + core_ref[far, here].astype(F32)).astype(BF)
        return carry

    lax.fori_loop(0, half // size, step, 0)


def grad_shard(weights, core):
    args, shapes, rows, columns, tokens = weight_args(weights)
    return call(
        partial(grad_shard_kernel, shapes),
        "grad_shard",
        (*args, core),
        [((rows // 2, columns), BF)],
        tokens * rows * columns,
    )[0]


def grad_own_kernel(weights, place, *refs):
    weights, (core_ref, shard_ref, *outs, acc) = each_weight(weights, refs)
    half = acc.shape[0]
    size = math.gcd(256, half)

    def step(i, carry):
        at = pl.ds(pl.multiple_of(i * size, size), size)
        for lefts, rights, first, columns in weights:
            here = slice(first, first + columns)
            value = token_sum(lefts, rights, at, slice(0, columns))
            acc[at, here] = value + core_ref[at, here].astype(F32) + shard_ref[at, here].astype(F32)
        return carry

    lax.fori_loop(0, half // size, step, 0)
    rows = outs[0].shape[0]
    if len(outs) == 1:
        outs[0][...] = acc[...].astype(BF)
    else:
        for d, out in enumerate(outs):
            at = pl.multiple_of((place[2] ^ d) * rows, rows)
            out[...] = acc[pl.ds(at, rows), :].astype(out.dtype)


def grad_own(place, weights, core, shard, pieces):
    args, shapes, rows, columns, tokens = weight_args(weights)
    half = rows // 2
    return call(
        partial(grad_own_kernel, shapes),
        "grad_own",
        (*args, core, shard),
        [
            ((half // pieces, columns), F32 if pieces > 1 and d == 0 else BF)
            for d in range(pieces)
        ],
        tokens * rows * columns,
        scratch=[pltpu.VMEM((half, columns), F32)],
        place=place,
        room=16,
    )


def heads_of(value):
    return value.reshape(value.shape[:-1] + (2, PAIR // 2))


def gathered_forward(qkv, scale):
    queries = heads_of(qkv[..., :PAIR])
    both = lax.all_gather(qkv[..., PAIR:], "ctx", axis=2, tiled=True)
    length = both.shape[2]
    block = math.gcd(length, 512)
    blocks = jnp.moveaxis(both.reshape(both.shape[:2] + (length // block, block, 2 * PAIR)), 2, 0)
    shape = queries.shape[:-1]

    def step(carry, piece):
        peak, total, summed = carry
        keys, values = heads_of(piece[..., :PAIR]), heads_of(piece[..., PAIR:])
        scores = jnp.einsum("gsqhd,gskhd->gsqhk", queries, keys, preferred_element_type=F32) * scale
        new_peak = jnp.maximum(peak, jnp.max(scores, axis=-1))
        fade = jnp.exp(peak - new_peak)
        weights = jnp.exp(scores - new_peak[..., None])
        total = total * fade + jnp.sum(weights, axis=-1)
        summed = summed * fade[..., None] + jnp.einsum(
            "gsqhk,gskhd->gsqhd", weights.astype(BF), values, preferred_element_type=F32
        )
        return (new_peak, total, summed), None

    first = (
        jnp.full(shape, -1e30, F32),
        jnp.zeros(shape, F32),
        jnp.zeros(queries.shape, F32),
    )
    (peak, total, summed), _ = lax.scan(step, first, blocks)
    attended = summed / total[..., None]
    mixed = attended.reshape(qkv.shape[:-1] + (PAIR,)).astype(BF)
    return mixed, (queries, blocks, peak + jnp.log(total), attended)


def gathered_backward(saved, grad, scale):
    queries, blocks, logs, attended = saved
    out_grad = heads_of(grad)
    delta = jnp.sum(out_grad.astype(F32) * attended, axis=-1)

    def step(q_grad, piece):
        keys, values = heads_of(piece[..., :PAIR]), heads_of(piece[..., PAIR:])
        scores = jnp.einsum("gsqhd,gskhd->gsqhk", queries, keys, preferred_element_type=F32) * scale
        weights = jnp.exp(scores - logs[..., None])
        weight_grad = jnp.einsum(
            "gsqhd,gskhd->gsqhk", out_grad, values, preferred_element_type=F32
        )
        score_grad = (weights * (weight_grad - delta[..., None])).astype(BF)
        v_grad = jnp.einsum(
            "gsqhk,gsqhd->gskhd", weights.astype(BF), out_grad, preferred_element_type=F32
        )
        k_grad = jnp.einsum("gsqhk,gsqhd->gskhd", score_grad, queries, preferred_element_type=F32)
        q_grad = q_grad + scale * jnp.einsum(
            "gsqhk,gskhd->gsqhd", score_grad, keys, preferred_element_type=F32
        )
        flat = lambda a: a.reshape(a.shape[:-2] + (PAIR,))
        return q_grad, jnp.concatenate([flat(k_grad) * scale, flat(v_grad)], axis=-1).astype(BF)

    q_grad, joined = lax.scan(step, jnp.zeros(queries.shape, F32), blocks)
    joined = jnp.moveaxis(joined, 0, 2)
    joined = joined.reshape(joined.shape[:2] + (-1, 2 * PAIR))
    owned = lax.psum_scatter(joined, "ctx", scatter_dimension=2, tiled=True)
    return jnp.concatenate([q_grad.reshape(grad.shape).astype(BF), owned], axis=-1)


GATE = 0


class Values:
    def __getattr__(self, name):
        self.__dict__[name] = made = {}
        return made


class Order:
    def __init__(self):
        self.last = None

    def hold(self, *values):
        if self.last is None:
            return values
        return lax.optimization_barrier((*values, self.last))[: len(values)]

    def mark(self, value):
        self.last = value
        return value


def body(
    inputs,
    time_features,
    valid_mask,
    teacher,
    w_time,
    b_time,
    w_query,
    b_query,
    w_key,
    w_value,
    b_value,
    w_output,
    b_output,
    gain_one,
    shift_one,
    w_hidden,
    b_hidden,
    w_down,
    b_down,
    gain_two,
    shift_two,
):
    positions, seqs, width = inputs.shape
    half = width // 2
    chunks = seqs // 2
    columns = w_query.shape[1]
    per_core = columns // PAIR
    pairs = 2 * per_core
    each = w_hidden.shape[1]
    scale = 1.0 / math.sqrt(D // HEADS)
    ctx = lax.axis_size("ctx")
    shards = lax.axis_size("shard")
    by_units = pairs == ctx
    shard = lax.axis_index("shard")
    core = lax.axis_index("tensor") % 2
    spot = lax.axis_index("ctx")
    slot = spot if by_units else jnp.int32(0)
    place = jnp.stack([core, shard, slot, spot]).astype(jnp.int32)
    order = Order()

    def turn(value):
        return jnp.where(
            shard == 0, value, jnp.concatenate([value[..., half:], value[..., :half]], axis=-1)
        )

    def after(value, *others):
        return lax.optimization_barrier((value, *others))[0]

    qkv_mine = pack(place, w_query, w_key, w_value)
    qkv_across = swap_shard(qkv_mine)
    qkv_side = swap_core(qkv_mine)

    bias = jnp.concatenate([b_hidden, b_query, b_value]).reshape(1, -1)
    biases = (bias, swap_core(bias))
    vec = turn(
        jnp.stack([b_output, gain_one, shift_one, b_down, gain_two, shift_two, b_down, b_down])
    )
    valid = valid_mask.T.astype(F32)
    count = jnp.full((8, 128), jnp.sum(valid), F32)
    embed = jnp.dot(time_features, w_time, preferred_element_type=F32) + b_time
    place, vec, valid, embed, count = lax.optimization_barrier((place, vec, valid, embed, count))
    tokens_all = positions * seqs * ctx * shards
    rows = entry(place, inputs, embed)
    low, start = rows[:chunks], rows[chunks:]
    near = sum_ctx(count)
    count = near + swap_shard(after(near, qkv_across))
    out_mine, feed_mine = pack_feed(after(place, low[0], near), w_output, w_hidden, w_down)
    out_side, feed_side = swap_core(out_mine), swap_core(feed_mine)
    order.mark(out_mine)

    qkv_weights = (qkv_mine, qkv_across, qkv_side, swap_core(after(qkv_across, feed_mine)))
    out_across = swap_shard(after(out_mine, qkv_across))
    val = Values()

    def run_project(c):
        (held,) = order.hold(low[c])
        val.slots[c] = project(place, each, held, qkv_weights, biases)
        order.mark(val.slots[c][0])
        if not val.out:
            behind = val.slots[c][0]
            val.feed_across[0] = swap_shard(after(feed_mine, out_across, behind))
            val.out[0] = (out_mine, out_across, out_side, swap_core(after(out_across, behind)))

    def run_teacher():
        (held,) = order.hold(place)
        val.teacher[0] = own_rows(held, teacher)
        order.mark(val.teacher[0][0])

    def run_attend(c):
        slots = val.slots[c]
        if by_units:
            if c > 0 and GATE:
                behind = val.kept[c - 1][0][-GATE:]
                slots = list(lax.optimization_barrier((*slots, *behind))[: len(slots)])
            pieces = swap_ctx(slots)
            *outs, logs = attend(order.hold(*pieces), scale)
            order.mark(logs)
            val.mixed[c] = swap_ctx(outs)
            val.kept[c] = (pieces, logs)
        else:
            value, saved = gathered_forward(jnp.stack(slots)[:, None], scale)
            val.mixed[c] = [value[p, 0] for p in range(pairs)]
            val.kept[c] = saved

    def run_merge(c):
        held = order.hold(*val.mixed[c])
        flat, mine = merge(place, held, val.out[0])
        order.mark(flat)
        val.flat[c] = flat
        val.branch[c] = (mine, swap_outer(mine))
        if not val.feed_weights:
            across = val.feed_across[0]
            side = swap_core(after(across, flat))
            val.feed_weights[0] = (feed_mine, across, feed_side, side)

    def run_feed(c):
        held, _ = order.hold(start[c], count)
        first, normed, hidden, slope, mine = feed(
            held, *val.branch[c], vec, biases, val.feed_weights[0]
        )
        order.mark(normed)
        val.first[c], val.norm[c], val.hidden[c], val.slope[c] = first, normed, hidden, slope
        val.feed[c] = (mine, swap_outer(mine))

    def run_feed_back(c):
        (held,) = order.hold(val.first[c])
        earlier = val.result[c - 1] if c else vec[None]
        args = (held, *val.feed[c], vec, val.teacher[0][c], valid, count, val.slope[c])
        result, grad, low_grad, pre_grad, mine, two, pre_sum = feed_back(
            place, c, tokens_all, earlier, *args, val.feed_weights[0]
        )
        order.mark(pre_sum)
        val.result[c], val.sum_grad[c], val.feed_low[c] = result, grad, low_grad
        val.pre_grad[c], val.two[c], val.pre_sum[c] = pre_grad, two, pre_sum
        val.back[c] = (mine, swap_outer(mine))
        if c == chunks - 1:
            val.result_other[0] = swap_core(result)

    def run_split(c):
        (held,) = order.hold(val.sum_grad[c])
        first_grad, branch_low, one, *outs = split(
            place, held, *val.back[c], val.first[c], vec, val.out[0]
        )
        order.mark(one)
        val.first_grad[c], val.branch_low[c], val.one[c] = first_grad, branch_low, one
        val.mixed_grad[c] = swap_ctx(outs) if by_units else outs

    def run_attend_back(c):
        if by_units:
            pieces, logs = val.kept[c]
            (logs,) = order.hold(logs)
            outs = attend_back(pieces, val.mixed_grad[c], logs, scale)
            order.mark(outs[0])
            val.qkv_grad[c] = swap_ctx(outs)
        else:
            value = gathered_backward(
                val.kept[c], jnp.stack(val.mixed_grad[c])[:, None], scale
            )
            val.qkv_grad[c] = [value[p, 0] for p in range(pairs)]

    def run_project_back(c):
        held = order.hold(*val.qkv_grad[c])
        flat, mine, qkv_sum, start_sum = project_back(place, held, qkv_weights)
        order.mark(qkv_sum)
        val.qkv_sum[c], val.qkv_flat[c], val.start_sum[c] = qkv_sum, flat, start_sum
        val.last[c] = (mine, swap_outer(mine))

    def run_last(c):
        (held,) = order.hold(val.first_grad[c])
        earlier = val.start[c - 1] if c else held[None]
        val.start[c] = order.mark(last(c, earlier, held, *val.last[c]))
        if c == chunks - 1:
            val.start_other[0] = swap_core(val.start[c])

    def every(values):
        return [values[c] for c in range(chunks)]

    def held_pairs(name):
        if name == "f":
            pairs_of = [(every(val.norm), every(val.pre_grad)), (every(val.feed_low), every(val.hidden))]
        else:
            pairs_of = [(low, every(val.qkv_flat)), (every(val.branch_low), every(val.flat))]
        (lefts, rights), *others = pairs_of
        (first,) = order.hold(lefts[0])
        return [([first, *lefts[1:]], rights), *others]

    def run_core(name):
        val.core[name] = swap_core(order.mark(grad_core(held_pairs(name))))

    def run_shard(name):
        value = order.mark(grad_shard(held_pairs(name), val.core[name]))
        val.shard[name] = swap_shard(value)

    def run_own(name):
        number = ctx if by_units else 1
        own = grad_own(place, held_pairs(name), val.core[name], val.shard[name], number)
        order.mark(own[0])
        if by_units:
            val.pieces[name] = swap_ctx(own)
        else:
            pieces = lax.all_to_all(own[0].reshape(ctx, half // ctx, -1), "ctx", 0, 0)
            val.pieces[name] = [jnp.sum(pieces.astype(F32), axis=0)]

    wide = 3 * columns
    cuts = {
        "f": [[(0, each)], [(each, each)]],
        "a": [[((3 * g + j) * PAIR, PAIR) for g in range(per_core)] for j in range(3)]
        + [[(wide, columns)]],
    }

    def run_total(name):
        val.grad[name] = grad_sum(order.hold(*val.pieces[name]), cuts[name])
        order.mark(val.grad[name][0])

    def run_leave(last):
        (held,) = order.hold(place)
        kind = val.start if last else val.result
        other = val.start_other if last else val.result_other
        val.leave[last] = order.mark(leave(held, kind[chunks - 1], other[0]))

    def run_tally():
        sums = [every(v) for v in (val.two, val.one, val.pre_sum, val.qkv_sum, val.start_sum)]
        sums[0][0] = order.hold(sums[0][0])[0]
        packed = order.mark(tally(place, each, *sums, time_features))
        packed = sum_ctx(packed)
        packed = packed + swap_core(packed)
        packed = packed + swap_shard(packed)
        val.packed[0] = (packed, swap_outer(packed[16 : 16 + shards * seqs]))

    def run_finish():
        (held,) = order.hold(place)
        sizes = (each, 3 * columns, shards * seqs, shards, time_features.shape[1])
        val.finish[0] = finish(held, *sizes, *val.packed[0], count)
        order.mark(val.finish[0][1])

    run_project(0)
    run_teacher()
    run_project(1)
    run_attend(0)
    run_attend(1)
    run_merge(0)
    run_merge(1)
    run_feed(0)
    run_feed(1)
    run_feed_back(0)
    run_feed_back(1)
    run_split(0)
    run_core("f")
    run_shard("f")
    run_split(1)
    run_attend_back(0)
    run_attend_back(1)
    run_leave(False)
    run_project_back(0)
    run_project_back(1)
    run_tally()
    run_core("a")
    run_own("f")
    run_last(0)
    run_shard("a")
    run_last(1)
    run_total("f")
    run_own("a")
    run_leave(True)
    run_finish()
    run_total("a")
    layer_out, grad_inputs = val.leave[False], val.leave[True]
    grad_w_hidden, grad_w_down = val.grad["f"]
    grad_w_query, grad_w_key, grad_w_value, grad_w_output = val.grad["a"]
    grad_w_time, loss, start_sum, hidden_sum, qkv_sum, *rest = val.finish[0]
    qkv_sum = qkv_sum.reshape(per_core, 3, PAIR)
    return (
        layer_out,
        loss.reshape(()),
        grad_inputs,
        grad_w_time,
        start_sum.reshape(-1),
        grad_w_query,
        qkv_sum[:, 0].reshape(-1),
        grad_w_key,
        grad_w_value,
        qkv_sum[:, 2].reshape(-1),
        grad_w_output,
        rest[5].reshape(-1),
        rest[3].reshape(-1),
        rest[4].reshape(-1),
        grad_w_hidden,
        hidden_sum.reshape(-1),
        grad_w_down,
        rest[2].reshape(-1),
        rest[0].reshape(-1),
        rest[1].reshape(-1),
    )


def solution(mesh):
    placed = (
        P("ctx", "shard", None),
        P("shard", None),
        P("ctx", "shard"),
        P("ctx", "shard", None),
        P(),
        P(),
        P("shard", "tensor"),
        P("tensor"),
        P("shard", "tensor"),
        P("shard", "tensor"),
        P("tensor"),
        P("shard", "tensor"),
        P(),
        P(),
        P(),
        P("shard", "tensor"),
        P("tensor"),
        P("shard", "tensor"),
        P(),
        P(),
        P(),
    )
    return jax.shard_map(
        body,
        mesh=mesh,
        in_specs=placed,
        out_specs=(
            P("ctx", "shard", None),
            P(),
            P("ctx", "shard", None),
            P(),
            P(),
            P(("shard", "ctx"), "tensor"),
            P("tensor"),
            P(("shard", "ctx"), "tensor"),
            P(("shard", "ctx"), "tensor"),
            P("tensor"),
            P(("shard", "ctx"), "tensor"),
            P(),
            P(),
            P(),
            P(("shard", "ctx"), "tensor"),
            P("tensor"),
            P(("shard", "ctx"), "tensor"),
            P(),
            P(),
            P(),
        ),
        check_vma=False,
    )
```

```python
from functools import partial
import math

import jax
import jax.numpy as jnp
from jax import lax
from jax.experimental import pallas as pl
from jax.experimental.pallas import tpu as pltpu
from jax.sharding import PartitionSpec as P

D = 1024
HEADS = 16
BF = jnp.bfloat16
F32 = jnp.float32
PAIR = 128
EPS = 1e-05


def contract(left, right, left_dim, right_dim):
    return lax.dot_general(
        left, right, (((left_dim,), (right_dim,)), ((), ())), preferred_element_type=F32
    )


PINNED = False
SCALES = {"project": 0.1, "attend": 1, "merge": 0.1, "feed": 0.1, "feed_back": 0.003, "split": 30, "attend_back": 1, "project_back": 100, "last": 10, "grad_core": 30, "grad_shard": 30, "grad_own": 100, "grad_sum": 30, "tally": 30, "leave": 30, "entry": 10, "own_rows": 10, "pack": 0.01, "pack_feed": 0.01}


def cost(name, flops, nbytes):
    scale = SCALES.get(name, 1)
    return pl.CostEstimate(
        flops=int(flops * scale), bytes_accessed=int(nbytes * scale), transcendentals=0
    )


def swap(value, axis, bit):
    size = lax.axis_size(axis)
    return lax.ppermute(value, axis, [(i, i ^ bit) for i in range(size)])


def swap_core(value):
    return swap(value, "tensor", 1)


def swap_outer(value):
    return swap(value, "tensor", 2)


def swap_shard(value):
    return swap(value, "shard", 1)


def swap_ctx(pieces):
    moved = {d: swap(pieces[d], "ctx", d) for d in reversed(range(1, len(pieces)))}
    return [pieces[0]] + [moved[d] for d in range(1, len(pieces))]


def sum_ctx(value):
    size = lax.axis_size("ctx")
    if size & (size - 1):
        return lax.psum(value, "ctx")
    bit = 1
    while bit < size:
        value = value + swap(value, "ctx", bit)
        bit *= 2
    return value


def sum_tokens(value):
    return sum_ctx(value + swap_shard(value))


def grid_call(kernel, name, grid, ins, outs, work, place, pinned=True):
    args = [a for a, _, _ in ins]
    nbytes = sum(a.size * a.dtype.itemsize for a in args)
    nbytes += sum(math.prod(s) * jnp.dtype(d).itemsize for s, d, _, _ in outs)
    without = lambda f: (lambda *i: f(*i[: len(grid)]))
    if pinned:
        args = [pltpu.with_memory_space_constraint(a, pltpu.HBM) for a in args]
    return pl.pallas_call(
        kernel,
        grid_spec=pltpu.PrefetchScalarGridSpec(
            num_scalar_prefetch=1,
            grid=grid,
            in_specs=[pl.BlockSpec(b, without(f)) for _, b, f in ins],
            out_specs=[pl.BlockSpec(b, without(f)) for _, _, b, f in outs],
        ),
        out_shape=[jax.ShapeDtypeStruct(s, d) for s, d, _, _ in outs],
        cost_estimate=cost(name, work, nbytes),
        compiler_params=pltpu.CompilerParams(vmem_limit_bytes=16 << 20),
        name=name,
    )(place, *args)


def call(kernel, name, args, outs, work, scratch=(), place=None, room=12, pinned=PINNED):
    nbytes = sum(a.size * a.dtype.itemsize for a in args)
    nbytes += sum(math.prod(s) * jnp.dtype(d).itemsize for s, d in outs)
    first = [] if place is None else [place]
    if pinned:
        args = [pltpu.with_memory_space_constraint(a, pltpu.VMEM) for a in args]
    return pl.pallas_call(
        kernel,
        in_specs=[pl.BlockSpec(memory_space=pltpu.SMEM)] * len(first)
        + [pl.BlockSpec(memory_space=pltpu.VMEM)] * len(args),
        out_specs=[pl.BlockSpec(memory_space=pltpu.VMEM)] * len(outs),
        out_shape=[jax.ShapeDtypeStruct(s, d) for s, d in outs],
        scratch_shapes=scratch,
        cost_estimate=cost(name, work, nbytes),
        compiler_params=pltpu.CompilerParams(vmem_limit_bytes=room << 20),
        name=name,
    )(*first, *args)


def whole(array):
    rank = array.ndim
    return (array, array.shape, lambda *i: (0,) * rank)


def turned(value, flip):
    half = value.shape[1] // 2
    return jnp.where(flip == 0, value, jnp.concatenate([value[:, half:], value[:, :half]], axis=1))


def entry_kernel(chunks, place, x_ref, embed_ref, *out_refs):
    core, flip = place[0], place[1]
    x = x_ref[...].astype(F32)
    rows = [x[:, s, :] + embed_ref[s : s + 1, :] for s in range(2 * chunks)]
    for c in range(chunks):
        own = turned(jnp.where(core == 0, rows[c], rows[chunks + c]), flip)
        out_refs[c][...] = own.astype(BF)
        out_refs[chunks + c][...] = own


def entry(place, x, embed):
    positions, seqs, width = x.shape
    chunks = seqs // 2
    block = math.gcd(64, positions)
    return grid_call(
        partial(entry_kernel, chunks),
        "entry",
        (positions // block,),
        [(x, (block, seqs, width), lambda i: (i, 0, 0)), whole(embed)],
        [
            ((positions, width), dtype, (block, width), lambda i: (i, 0))
            for dtype in (BF, F32)
            for _ in range(chunks)
        ],
        4 * x.size,
        place=place,
    )


def own_kernel(chunks, place, x_ref, *out_refs):
    core, flip = place[0], place[1]
    x = x_ref[...].astype(F32)
    for c in range(chunks):
        own = jnp.where(core == 0, x[:, c, :], x[:, chunks + c, :])
        out_refs[c][...] = turned(own, flip).astype(BF)


def own_rows(place, x):
    positions, seqs, width = x.shape
    chunks = seqs // 2
    block = math.gcd(64, positions)
    return grid_call(
        partial(own_kernel, chunks),
        "own_rows",
        (positions // block,),
        [(x, (block, seqs, width), lambda i: (i, 0, 0))],
        [((positions, width), BF, (block, width), lambda i: (i, 0))] * chunks,
        2 * x.size,
        place=place,
    )


def leave_kernel(chunks, dtype, place, own_ref, other_ref, out_ref):
    core, flip = place[0], place[1]
    own = [turned(own_ref[c].astype(F32), flip) for c in range(chunks)]
    other = [turned(other_ref[c].astype(F32), flip) for c in range(chunks)]
    rows = [jnp.where(core == 0, a, b) for a, b in zip(own, other)]
    rows += [jnp.where(core == 0, b, a) for a, b in zip(own, other)]
    out_ref[...] = jnp.stack(rows, axis=1).astype(dtype)


def leave(place, own, other):
    chunks, positions, width = own.shape
    block = math.gcd(64, positions)
    piece = ((chunks, block, width), lambda i: (0, i, 0))
    return grid_call(
        partial(leave_kernel, chunks, own.dtype),
        "leave",
        (positions // block,),
        [(own, *piece), (other, *piece)],
        [
            (
                (positions, 2 * chunks, width),
                own.dtype,
                (block, 2 * chunks, width),
                lambda i: (i, 0, 0),
            )
        ],
        2 * own.size,
        place=place,
        pinned=False,
    )[0]


def pack_kernel(place, q_ref, k_ref, v_ref, out_ref):
    for g in range(q_ref.shape[1] // PAIR):
        for j, ref in enumerate((q_ref, k_ref, v_ref)):
            at = (3 * g + j) * PAIR
            out_ref[:, at : at + PAIR] = ref[:, g * PAIR : (g + 1) * PAIR]


def pack(place, q, k, v):
    rows, columns = q.shape
    return grid_call(
        pack_kernel,
        "pack",
        (1,),
        [whole(q), whole(k), whole(v)],
        [((rows, 3 * columns), BF, (rows, 3 * columns), lambda i: (0, 0))],
        0,
        place,
    )[0]


def pack_feed_kernel(place, out_ref, up_ref, down_ref, copy_ref, both_ref):
    each = up_ref.shape[1]
    copy_ref[...] = out_ref[...]
    both_ref[:, :each] = up_ref[...]
    both_ref[:, each:] = down_ref[...]


def pack_feed(place, out, up, down):
    rows, each = up.shape
    block = math.gcd(128, rows)
    tall = lambda a: (a, (block, a.shape[1]), lambda i: (i, 0))
    return grid_call(
        pack_feed_kernel,
        "pack_feed",
        (rows // block,),
        [tall(out), tall(up), tall(down)],
        [
            (out.shape, BF, (block, out.shape[1]), lambda i: (i, 0)),
            ((rows, 2 * each), BF, (block, 2 * each), lambda i: (i, 0)),
        ],
        0,
        place,
    )


def project_kernel(shift, place, x_ref, a_ref, b_ref, c_ref, d_ref, bias_ref, more_ref, *outs_and_all):
    *outs, pairs_ref = outs_and_all
    half = x_ref.shape[1] // 2
    per_core = len(outs) // 2
    wide = 3 * PAIR
    for core, (top, bottom) in enumerate(((a_ref, b_ref), (c_ref, d_ref))):

        def step(g, carry, core=core, top=top, bottom=bottom):
            at = pl.ds(pl.multiple_of(g * wide, wide), wide)
            value = contract(x_ref[:, :half], top[:, at], 1, 0)
            value += contract(x_ref[:, half:], bottom[:, at], 1, 0)
            pair = core * per_core + g
            bias = (bias_ref, more_ref)[core]
            for j, first in enumerate((shift, None, shift + per_core * PAIR)):
                part = value[:, j * PAIR : (j + 1) * PAIR]
                if first is not None:
                    part += bias[:, pl.ds(pl.multiple_of(first + g * PAIR, PAIR), PAIR)]
                pairs_ref[pair, :, j * PAIR : (j + 1) * PAIR] = part.astype(BF)
            return carry

        lax.fori_loop(0, per_core, step, 0)
    for d, out in enumerate(outs):
        out[...] = pairs_ref[place[2] ^ d]


def project(place, shift, x, weights, biases):
    rows, width = x.shape
    pairs = 2 * weights[0].shape[1] // (3 * PAIR)
    return call(
        partial(project_kernel, shift),
        "project",
        (x, *weights, *biases),
        [((rows, 3 * PAIR), BF)] * pairs,
        2 * rows * width * pairs * 3 * PAIR,
        scratch=[pltpu.VMEM((pairs, rows, 3 * PAIR), BF)],
        place=place,
    )


def project_back_kernel(pairs, place, *refs):
    pieces, (a_ref, b_ref, c_ref, d_ref, flat_ref, out_ref, sums_ref, start_ref, pairs_ref) = (
        refs[:pairs],
        refs[pairs:],
    )
    for d, piece in enumerate(pieces):
        pairs_ref[place[2] ^ d] = piece[...]
    wide = 3 * PAIR
    for p in range(pairs):
        flat_ref[:, p * wide : (p + 1) * wide] = pairs_ref[p]
    half = a_ref.shape[0]
    middle = a_ref.shape[1]
    for at, first, second in ((0, a_ref, c_ref), (half, b_ref, d_ref)):
        value = contract(flat_ref[:, :middle], first[...], 1, 1)
        value += contract(flat_ref[:, middle:], second[...], 1, 1)
        out_ref[:, at : at + half] = value.astype(BF)
        start_ref[:, at : at + half] = sum_rows(value)
    sums_ref[...] = sum_rows(flat_ref[...].astype(F32))


def project_back(place, pieces, weights):
    rows, columns = pieces[0].shape
    pairs = len(pieces)
    width = 2 * weights[0].shape[0]
    return call(
        partial(project_back_kernel, pairs),
        "project_back",
        (*pieces, *weights),
        [
            ((rows, pairs * columns), BF),
            ((rows, width), BF),
            ((1, pairs * columns), F32),
            ((1, width), F32),
        ],
        2 * rows * width * pairs * columns,
        scratch=[pltpu.VMEM((pairs, rows, columns), BF)],
        place=place,
    )


def merge_kernel(pairs, place, *refs):
    pieces, (a_ref, b_ref, c_ref, d_ref, flat_ref, out_ref, pairs_ref) = refs[:pairs], refs[pairs:]
    for d, piece in enumerate(pieces):
        pairs_ref[place[2] ^ d] = piece[...]
    for p in range(pairs):
        flat_ref[:, p * PAIR : (p + 1) * PAIR] = pairs_ref[p]
    half = a_ref.shape[0]
    middle = a_ref.shape[1]
    for at, first, second in ((0, a_ref, c_ref), (half, b_ref, d_ref)):
        value = contract(flat_ref[:, :middle], first[...], 1, 1)
        value += contract(flat_ref[:, middle:], second[...], 1, 1)
        out_ref[:, at : at + half] = value.astype(BF)


def merge(place, pieces, weights):
    rows, columns = pieces[0].shape
    pairs = len(pieces)
    width = 2 * weights[0].shape[0]
    return call(
        partial(merge_kernel, pairs),
        "merge",
        (*pieces, *weights),
        [((rows, pairs * columns), BF), ((rows, width), BF)],
        2 * rows * width * pairs * columns,
        scratch=[pltpu.VMEM((pairs, rows, columns), BF)],
        place=place,
    )


def lanes_of(part):
    lane = lax.broadcasted_iota(jnp.int32, (1, PAIR), 1)
    return lane < PAIR // 2 if part == 0 else lane >= PAIR // 2


def attend_kernel(scale, pieces, *refs):
    ins, outs, (log_ref, mixed_ref) = refs[:pieces], refs[pieces : 2 * pieces], refs[2 * pieces :]
    rows = ins[0].shape[0]
    join = lambda at: jnp.concatenate([ref[:, at : at + PAIR] for ref in ins], axis=0)
    q, k, v = join(0) * BF(scale), join(PAIR), join(2 * PAIR)
    lane = lax.broadcasted_iota(jnp.int32, (1, PAIR), 1)
    mixed_ref[...] = jnp.zeros_like(mixed_ref)

    def head(part, carry):
        lanes = (lane >= PAIR // 2) == (part == 1)
        k_head, v_head = jnp.where(lanes, k, BF(0)), jnp.where(lanes, v, BF(0))
        scores = contract(k_head, q, 1, 1)
        peak = jnp.max(scores, axis=0, keepdims=True)
        weights = jnp.exp(scores - peak)
        total = jnp.sum(weights, axis=0, keepdims=True)
        mixed_ref[...] += contract(v_head, weights.astype(BF), 0, 0) * (1.0 / total)
        log_ref[pl.ds(part, 1), :] = peak + jnp.log(total)
        return carry

    lax.fori_loop(0, 2, head, 0)
    mixed = mixed_ref[...].T.astype(BF)
    for d, out in enumerate(outs):
        out[...] = mixed[d * rows : (d + 1) * rows]


def attend(pieces, scale):
    rows = pieces[0].shape[0]
    length = rows * len(pieces)
    return call(
        partial(attend_kernel, scale, len(pieces)),
        "attend",
        pieces,
        [((rows, PAIR), BF)] * len(pieces) + [((2, length), F32)],
        16 * length * length * PAIR,
        scratch=[pltpu.VMEM((PAIR, length), F32)],
        room=24,
    )


def attend_back_kernel(scale, pieces, *refs):
    ins, grads = refs[:pieces], refs[pieces : 2 * pieces]
    log_ref, outs = refs[2 * pieces], refs[2 * pieces + 1 : 3 * pieces + 1]
    k_sum, v_sum, q_sum, q_ref, grad_ref = refs[3 * pieces + 1 :]
    rows = ins[0].shape[0]
    length = rows * pieces
    join = lambda refs, at: jnp.concatenate([ref[:, at : at + PAIR] for ref in refs], axis=0)
    k, v = join(ins, PAIR), join(ins, 2 * PAIR)
    q_ref[...] = join(ins, 0) * BF(scale)
    grad_ref[...] = join(grads, 0)
    k_sum[...] = jnp.zeros_like(k_sum)
    v_sum[...] = jnp.zeros_like(v_sum)
    q_sum[...] = jnp.zeros_like(q_sum)
    lane = lax.broadcasted_iota(jnp.int32, (1, PAIR), 1)
    block = math.gcd(512, length)

    def step(i, carry):
        part = i % 2
        at = pl.ds(pl.multiple_of(i // 2 * block, block), block)
        lanes = (lane >= PAIR // 2) == (part == 1)
        q, grad = q_ref[at, :], grad_ref[at, :]
        k_head, v_head = jnp.where(lanes, k, BF(0)), jnp.where(lanes, v, BF(0))
        q_head, grad_head = jnp.where(lanes, q, BF(0)), jnp.where(lanes, grad, BF(0))
        probs = jnp.exp(contract(k_head, q, 1, 1) - log_ref[pl.ds(part, 1), at])
        probs_grad = contract(v_head, grad, 1, 1)
        delta = jnp.sum(probs * probs_grad, axis=0, keepdims=True)
        scores_grad = (probs * (probs_grad - delta)).astype(BF)
        v_sum[...] += contract(probs.astype(BF), grad_head, 1, 0)
        k_sum[...] += contract(scores_grad, q_head, 1, 0)
        q_sum[:, at] += contract(k_head, scores_grad, 0, 0)
        return carry

    lax.fori_loop(0, 2 * length // block, step, 0)
    q_grad = (q_sum[...] * scale).T.astype(BF)
    for d, out in enumerate(outs):
        at = slice(d * rows, (d + 1) * rows)
        out[:, 0:PAIR] = q_grad[at, :]
        out[:, PAIR : 2 * PAIR] = k_sum[at, :].astype(BF)
        out[:, 2 * PAIR : 3 * PAIR] = v_sum[at, :].astype(BF)


def attend_back(pieces, grads, logs, scale):
    rows = pieces[0].shape[0]
    length = rows * len(pieces)
    return call(
        partial(attend_back_kernel, scale, len(pieces)),
        "attend_back",
        (*pieces, *grads, logs),
        [((rows, 3 * PAIR), BF)] * len(pieces),
        40 * length * length * PAIR,
        scratch=[pltpu.VMEM((length, PAIR), F32)] * 2
        + [pltpu.VMEM((PAIR, length), F32)]
        + [pltpu.VMEM((length, PAIR), BF)] * 2,
        room=24,
    )


def sum_rows(value):
    return jnp.sum(value, axis=0, keepdims=True)


def normal(value):
    center = jnp.mean(value, axis=-1, keepdims=True)
    offset = value - center
    spread = jnp.mean(offset * offset, axis=-1, keepdims=True)
    inverse = lax.rsqrt(spread + EPS)
    return offset * inverse, inverse


def normal_back(grad, unit, inverse):
    return inverse * (
        grad
        - jnp.mean(grad, axis=-1, keepdims=True)
        - unit * jnp.mean(grad * unit, axis=-1, keepdims=True)
    )


def by_rows(rows, run):
    size = math.gcd(64, rows)

    def step(i, carry):
        run(pl.ds(pl.multiple_of(i * size, size), size))
        return carry

    lax.fori_loop(0, rows // size, step, 0)


def feed_kernel(
    start_ref, mine_ref, theirs_ref, vec_ref, bias_ref, more_ref, a_ref, b_ref, c_ref, d_ref,
    first_ref, low_ref, hidden_ref, slope_ref, out_ref, acc,
):
    def norm(at):
        total = start_ref[at, :] + mine_ref[at, :].astype(F32) + theirs_ref[at, :].astype(F32)
        total += vec_ref[0:1, :]
        first_ref[at, :] = total
        unit, _ = normal(total)
        low_ref[at, :] = (unit * vec_ref[1:2, :] + vec_ref[2:3, :]).astype(BF)

    by_rows(start_ref.shape[0], norm)
    half, each = a_ref.shape[0], a_ref.shape[1] // 2
    size = math.gcd(512, each)
    acc[...] = jnp.zeros_like(acc)
    for core, (top, bottom) in enumerate(((a_ref, b_ref), (c_ref, d_ref))):

        def step(i, carry, core=core, top=top, bottom=bottom):
            here = pl.ds(pl.multiple_of(i * size, size), size)
            at = pl.ds(pl.multiple_of(core * each + i * size, size), size)
            down = pl.ds(pl.multiple_of(each + i * size, size), size)
            pre = contract(low_ref[:, :half], top[:, here], 1, 0)
            pre += contract(low_ref[:, half:], bottom[:, here], 1, 0)
            pre += (bias_ref, more_ref)[core][:, here]
            phi = 0.5 + 0.5 * lax.erf(pre * math.sqrt(0.5))
            hidden = (pre * phi).astype(BF)
            hidden_ref[:, at] = hidden
            bell = jnp.exp(-0.5 * (pre * pre)) * (1.0 / math.sqrt(2.0 * math.pi))
            slope_ref[:, at] = (phi + pre * bell).astype(BF)
            for k, weight in ((0, top), (half, bottom)):
                acc[:, k : k + half] += contract(hidden, weight[:, down], 1, 1)
            return carry

        lax.fori_loop(0, each // size, step, 0)
    out_ref[...] = acc[...].astype(BF)


def feed(start, mine, theirs, vec, biases, weights):
    rows, width = start.shape
    units = weights[0].shape[1]
    return call(
        feed_kernel,
        "feed",
        (start, mine, theirs, vec, *biases, *weights),
        [
            ((rows, width), F32),
            ((rows, width), BF),
            ((rows, units), BF),
            ((rows, units), BF),
            ((rows, width), BF),
        ],
        4 * rows * width * units,
        scratch=[pltpu.VMEM((rows, width), F32)],
    )


def feed_back_kernel(
    valid_row, tokens, place, earlier_ref, first_ref, mine_ref, theirs_ref, vec_ref, teacher_ref, valid_ref, count_ref, slope_ref,
    a_ref, b_ref, c_ref, d_ref, result_ref, grad_ref, low_ref, pre_ref, out_ref, sums_ref, pre_sums_ref, acc, valid_sums,
):
    second = valid_ref.shape[0] // 2 + valid_row
    valid = jnp.where(
        place[0] == 0, valid_ref[valid_row : valid_row + 1, :], valid_ref[second : second + 1, :]
    )
    for c in range(valid_row):
        result_ref[c] = earlier_ref[c]
    valid_sums[...] = jnp.broadcast_to(valid, (PAIR, valid.shape[1])).T
    sums_ref[...] = jnp.zeros_like(sums_ref)
    factor = 2.0 * tokens / count_ref[0:1, 0:1]

    def norm(at):
        valid = valid_sums[at, 0:1]
        unit, _ = normal(first_ref[at, :])
        normed = unit * vec_ref[1:2, :] + vec_ref[2:3, :]
        total = normed + mine_ref[at, :].astype(F32) + theirs_ref[at, :].astype(F32) + vec_ref[3:4, :]
        unit, inverse = normal(total)
        result = unit * vec_ref[4:5, :] + vec_ref[5:6, :]
        result_ref[valid_row, at, :] = result.astype(BF)
        error = result - teacher_ref[at, :].astype(F32)
        result_grad = valid * factor * error
        grad = normal_back(result_grad * vec_ref[4:5, :], unit, inverse)
        grad_ref[at, :] = grad
        low = grad.astype(BF)
        low_ref[at, :] = low
        sums_ref[0:1, :] += sum_rows(result_grad * unit)
        sums_ref[1:2, :] += sum_rows(result_grad)
        sums_ref[2:3, :] += sum_rows(low.astype(F32))
        sums_ref[3:4, :] += sum_rows(valid * error * error)

    by_rows(first_ref.shape[0], norm)
    half, each = a_ref.shape[0], a_ref.shape[1] // 2
    size = math.gcd(512, each)
    acc[...] = jnp.zeros_like(acc)
    for core, (top, bottom) in enumerate(((a_ref, b_ref), (c_ref, d_ref))):

        def step(i, carry, core=core, top=top, bottom=bottom):
            here = pl.ds(pl.multiple_of(i * size, size), size)
            at = pl.ds(pl.multiple_of(core * each + i * size, size), size)
            down = pl.ds(pl.multiple_of(each + i * size, size), size)
            value = contract(low_ref[:, :half], top[:, down], 1, 0)
            value += contract(low_ref[:, half:], bottom[:, down], 1, 0)
            pre_grad = (value * slope_ref[:, at].astype(F32)).astype(BF)
            pre_ref[:, at] = pre_grad
            pre_sums_ref[:, at] = sum_rows(pre_grad.astype(F32))
            for k, weight in ((0, top), (half, bottom)):
                acc[:, k : k + half] += contract(pre_grad, weight[:, here], 1, 1)
            return carry

        lax.fori_loop(0, each // size, step, 0)
    out_ref[...] = acc[...].astype(BF)


def feed_back(place, row, tokens, earlier, first, mine, theirs, vec, teacher, valid, count, slope, weights):
    rows, width = first.shape
    units = slope.shape[1]
    return call(
        partial(feed_back_kernel, row, tokens),
        "feed_back",
        (earlier, first, mine, theirs, vec, teacher, valid, count, slope, *weights),
        [
            ((row + 1, rows, width), BF),
            ((rows, width), F32),
            ((rows, width), BF),
            ((rows, units), BF),
            ((rows, width), BF),
            ((8, width), F32),
            ((1, units), F32),
        ],
        4 * rows * width * units,
        scratch=[pltpu.VMEM((rows, width), F32), pltpu.VMEM((rows, PAIR), F32)],
        place=place,
    )


def split_kernel(place, grad_ref, mine_ref, theirs_ref, first_ref, vec_ref, a_ref, b_ref, c_ref, d_ref, out_ref, low_ref, sums_ref, *outs_and_all):
    *outs, pairs_ref = outs_and_all
    sums_ref[...] = jnp.zeros_like(sums_ref)

    def norm(at):
        grad = grad_ref[at, :] + mine_ref[at, :].astype(F32) + theirs_ref[at, :].astype(F32)
        unit, inverse = normal(first_ref[at, :])
        out = normal_back(grad * vec_ref[1:2, :], unit, inverse)
        out_ref[at, :] = out
        low = out.astype(BF)
        low_ref[at, :] = low
        sums_ref[0:1, :] += sum_rows(grad * unit)
        sums_ref[1:2, :] += sum_rows(grad)
        sums_ref[2:3, :] += sum_rows(low.astype(F32))
        sums_ref[3:4, :] += sum_rows(out)

    by_rows(grad_ref.shape[0], norm)
    half = a_ref.shape[0]
    per_core = len(outs) // 2
    for core, (top, bottom) in enumerate(((a_ref, b_ref), (c_ref, d_ref))):
        mixed = contract(low_ref[:, :half], top[...], 1, 0)
        mixed += contract(low_ref[:, half:], bottom[...], 1, 0)
        mixed = mixed.astype(BF)
        for p in range(per_core):
            pairs_ref[core * per_core + p] = mixed[:, p * PAIR : (p + 1) * PAIR]
    for d, piece in enumerate(outs):
        piece[...] = pairs_ref[place[2] ^ d]


def split(place, grad, mine, theirs, first, vec, weights):
    rows, width = grad.shape
    pairs = 2 * weights[0].shape[1] // PAIR
    return call(
        split_kernel,
        "split",
        (grad, mine, theirs, first, vec, *weights),
        [((rows, width), F32), ((rows, width), BF), ((8, width), F32)]
        + [((rows, PAIR), BF)] * pairs,
        2 * rows * width * pairs * PAIR,
        scratch=[pltpu.VMEM((pairs, rows, PAIR), BF)],
        place=place,
    )


def last_kernel(row, earlier_ref, grad_ref, mine_ref, theirs_ref, out_ref):
    for c in range(row):
        out_ref[c] = earlier_ref[c]
    out_ref[row] = grad_ref[...] + mine_ref[...].astype(F32) + theirs_ref[...].astype(F32)


def last(row, earlier, grad, mine, theirs):
    rows, width = grad.shape
    return call(
        partial(last_kernel, row),
        "last",
        (earlier, grad, mine, theirs),
        [((row + 1, rows, width), F32)],
        4 * rows * width,
    )[0]


def tally_kernel(chunks, each, place, *refs):
    two, one = refs[:chunks], refs[chunks : 2 * chunks]
    pre, qkv = refs[2 * chunks : 3 * chunks], refs[3 * chunks : 4 * chunks]
    start, (features_ref, out_ref) = refs[4 * chunks : 5 * chunks], refs[5 * chunks :]
    core, flip, spot = place[0], place[1], place[3]
    add = lambda parts: sum(parts[1:], parts[0])
    out_ref[...] = jnp.zeros_like(out_ref)
    out_ref[0:4, :] = turned(add([ref[0:4, :] for ref in two]), flip)
    out_ref[4:7, :] = turned(add([ref[0:3, :] for ref in one]), flip)
    pre = add([ref[...] for ref in pre])
    qkv = add([ref[...] for ref in qkv])
    size = qkv.shape[1] // 2
    for slot in range(2):
        mine = core == slot
        out_ref[8 + slot : 9 + slot, :] = jnp.where(mine, pre[:, :each], pre[:, each:])
        out_ref[10 + slot : 11 + slot, :size] = jnp.where(mine, qkv[:, :size], qkv[:, size:])
    seqs = 2 * chunks
    features = features_ref[...].astype(F32)
    wide = features.shape[1]
    for s in range(2):
        here = jnp.logical_and(jnp.logical_and(core == 0, spot == 0), flip == s)
        for k in range(seqs):
            value = jnp.where(here, features[k : k + 1, :], 0.0)
            out_ref[12 + s : 13 + s, k * wide : (k + 1) * wide] = value
    for s in range(2 * seqs):
        here = jnp.logical_and(flip == s // seqs, core == s % seqs // chunks)
        row = turned(0.5 * one[s % chunks][3:4, :] + start[s % chunks][...], flip)
        out_ref[16 + s : 17 + s, :] = jnp.where(here, row, 0.0)


def tally(place, each, two, one, pre, qkv, start, features):
    rows = -(-(16 + 2 * features.shape[0]) // 8) * 8
    return call(
        partial(tally_kernel, len(two), each),
        "tally",
        (*two, *one, *pre, *qkv, *start, features),
        [((rows, two[0].shape[1]), F32)],
        0,
        place=place,
    )[0]


def grad_sum_kernel(pieces, cuts, *refs):
    total = refs[0][...].astype(F32)
    for ref in refs[1:pieces]:
        total = total + ref[...].astype(F32)
    for out, parts in zip(refs[pieces:], cuts):
        at = 0
        for start, size in parts:
            out[:, at : at + size] = total[:, start : start + size]
            at += size


def grad_sum(pieces, cuts):
    rows = pieces[0].shape[0]
    return call(
        partial(grad_sum_kernel, len(pieces), cuts),
        "grad_sum",
        pieces,
        [((rows, sum(size for _, size in parts)), F32) for parts in cuts],
        len(pieces) * pieces[0].size,
    )


def finish_kernel(each, size, shards, place, packed_ref, other_ref, count_ref, time_ref, loss_ref, start_ref, hidden_ref, qkv_ref, *outs_and_all):
    *outs, all_ref = outs_and_all
    seqs = all_ref.shape[0]
    wide = all_ref.shape[1]
    per_row = seqs // shards
    for s in range(seqs):
        k = s % per_row
        row = 12 + s // per_row
        all_ref[s : s + 1, :] = packed_ref[row : row + 1, k * wide : (k + 1) * wide]
    grads = packed_ref[16 : 16 + seqs, :] + other_ref[...]
    time_ref[...] = lax.dot_general(
        all_ref[...],
        grads,
        (((0,), (0,)), ((), ())),
        precision=lax.Precision.HIGHEST,
        preferred_element_type=F32,
    )
    start_ref[...] = sum_rows(grads)
    total = jnp.sum(packed_ref[3:4, :], axis=1, keepdims=True)
    loss_ref[...] = total / (packed_ref.shape[1] * count_ref[0:1, 0:1])
    first = place[0] == 0
    hidden_ref[...] = jnp.where(first, packed_ref[8:9, :], packed_ref[9:10, :])[:, :each]
    qkv_ref[...] = jnp.where(first, packed_ref[10:11, :], packed_ref[11:12, :])[:, :size]
    for out, row in zip(outs, (0, 1, 2, 4, 5, 6)):
        out[...] = packed_ref[row : row + 1, :]


def finish(place, each, size, seqs, shards, wide, packed, other, count):
    width = packed.shape[1]
    return call(
        partial(finish_kernel, each, size, shards),
        "finish",
        (packed, other, count),
        [((wide, width), F32), ((1, 1), F32), ((1, width), F32), ((1, each), F32), ((1, size), F32)]
        + [((1, width), F32)] * 6,
        0,
        scratch=[pltpu.VMEM((seqs, wide), F32)],
        place=place,
    )


def token_sum(lefts, rights, rows, columns):
    total = None
    for left, right in zip(lefts, rights):
        term = contract(left[:, rows], right[:, columns], 0, 0)
        total = term if total is None else total + term
    return total


def each_weight(weights, refs):
    at, column, out = 0, 0, []
    for chunks, columns in weights:
        out.append((refs[at : at + chunks], refs[at + chunks : at + 2 * chunks], column, columns))
        at += 2 * chunks
        column += columns
    return out, refs[at:]


def weight_args(weights):
    args = [a for lefts, rights in weights for a in (*lefts, *rights)]
    shapes = [(len(lefts), rights[0].shape[1] // 2) for lefts, rights in weights]
    tokens = sum(a.shape[0] for a in weights[0][0])
    return args, shapes, weights[0][0][0].shape[1], sum(c for _, c in shapes), tokens


def grad_core_kernel(weights, *refs):
    weights, (out_ref,) = each_weight(weights, refs)
    rows = out_ref.shape[0]
    step = math.gcd(512, rows)

    def part(i, carry):
        at = pl.ds(pl.multiple_of(i * step, step), step)
        for lefts, rights, first, columns in weights:
            value = token_sum(lefts, rights, at, slice(columns, 2 * columns))
            out_ref[at, first : first + columns] = value.astype(BF)
        return carry

    lax.fori_loop(0, rows // step, part, 0)


def grad_core(weights):
    args, shapes, rows, columns, tokens = weight_args(weights)
    return call(
        partial(grad_core_kernel, shapes),
        "grad_core",
        args,
        [((rows, columns), BF)],
        2 * tokens * rows * columns,
    )[0]


def grad_shard_kernel(weights, *refs):
    weights, (core_ref, out_ref) = each_weight(weights, refs)
    half = out_ref.shape[0]
    size = math.gcd(256, half)

    def step(i, carry):
        at = pl.ds(pl.multiple_of(i * size, size), size)
        far = pl.ds(pl.multiple_of(half + i * size, size), size)
        for lefts, rights, first, columns in weights:
            here = slice(first, first + columns)
            value = token_sum(lefts, rights, far, slice(0, columns))
            out_ref[at, here] = (value + core_ref[far, here].astype(F32)).astype(BF)
        return carry

    lax.fori_loop(0, half // size, step, 0)


def grad_shard(weights, core):
    args, shapes, rows, columns, tokens = weight_args(weights)
    return call(
        partial(grad_shard_kernel, shapes),
        "grad_shard",
        (*args, core),
        [((rows // 2, columns), BF)],
        tokens * rows * columns,
    )[0]


def grad_own_kernel(weights, place, *refs):
    weights, (core_ref, shard_ref, *outs, acc) = each_weight(weights, refs)
    half = acc.shape[0]
    size = math.gcd(256, half)

    def step(i, carry):
        at = pl.ds(pl.multiple_of(i * size, size), size)
        for lefts, rights, first, columns in weights:
            here = slice(first, first + columns)
            value = token_sum(lefts, rights, at, slice(0, columns))
            acc[at, here] = value + core_ref[at, here].astype(F32) + shard_ref[at, here].astype(F32)
        return carry

    lax.fori_loop(0, half // size, step, 0)
    rows = outs[0].shape[0]
    if len(outs) == 1:
        outs[0][...] = acc[...].astype(BF)
    else:
        for d, out in enumerate(outs):
            at = pl.multiple_of((place[2] ^ d) * rows, rows)
            out[...] = acc[pl.ds(at, rows), :].astype(out.dtype)


def grad_own(place, weights, core, shard, pieces):
    args, shapes, rows, columns, tokens = weight_args(weights)
    half = rows // 2
    return call(
        partial(grad_own_kernel, shapes),
        "grad_own",
        (*args, core, shard),
        [
            ((half // pieces, columns), F32 if pieces > 1 and d == 0 else BF)
            for d in range(pieces)
        ],
        tokens * rows * columns,
        scratch=[pltpu.VMEM((half, columns), F32)],
        place=place,
        room=16,
    )


def heads_of(value):
    return value.reshape(value.shape[:-1] + (2, PAIR // 2))


def gathered_forward(qkv, scale):
    queries = heads_of(qkv[..., :PAIR])
    both = lax.all_gather(qkv[..., PAIR:], "ctx", axis=2, tiled=True)
    length = both.shape[2]
    block = math.gcd(length, 512)
    blocks = jnp.moveaxis(both.reshape(both.shape[:2] + (length // block, block, 2 * PAIR)), 2, 0)
    shape = queries.shape[:-1]

    def step(carry, piece):
        peak, total, summed = carry
        keys, values = heads_of(piece[..., :PAIR]), heads_of(piece[..., PAIR:])
        scores = jnp.einsum("gsqhd,gskhd->gsqhk", queries, keys, preferred_element_type=F32) * scale
        new_peak = jnp.maximum(peak, jnp.max(scores, axis=-1))
        fade = jnp.exp(peak - new_peak)
        weights = jnp.exp(scores - new_peak[..., None])
        total = total * fade + jnp.sum(weights, axis=-1)
        summed = summed * fade[..., None] + jnp.einsum(
            "gsqhk,gskhd->gsqhd", weights.astype(BF), values, preferred_element_type=F32
        )
        return (new_peak, total, summed), None

    first = (
        jnp.full(shape, -1e30, F32),
        jnp.zeros(shape, F32),
        jnp.zeros(queries.shape, F32),
    )
    (peak, total, summed), _ = lax.scan(step, first, blocks)
    attended = summed / total[..., None]
    mixed = attended.reshape(qkv.shape[:-1] + (PAIR,)).astype(BF)
    return mixed, (queries, blocks, peak + jnp.log(total), attended)


def gathered_backward(saved, grad, scale):
    queries, blocks, logs, attended = saved
    out_grad = heads_of(grad)
    delta = jnp.sum(out_grad.astype(F32) * attended, axis=-1)

    def step(q_grad, piece):
        keys, values = heads_of(piece[..., :PAIR]), heads_of(piece[..., PAIR:])
        scores = jnp.einsum("gsqhd,gskhd->gsqhk", queries, keys, preferred_element_type=F32) * scale
        weights = jnp.exp(scores - logs[..., None])
        weight_grad = jnp.einsum(
            "gsqhd,gskhd->gsqhk", out_grad, values, preferred_element_type=F32
        )
        score_grad = (weights * (weight_grad - delta[..., None])).astype(BF)
        v_grad = jnp.einsum(
            "gsqhk,gsqhd->gskhd", weights.astype(BF), out_grad, preferred_element_type=F32
        )
        k_grad = jnp.einsum("gsqhk,gsqhd->gskhd", score_grad, queries, preferred_element_type=F32)
        q_grad = q_grad + scale * jnp.einsum(
            "gsqhk,gskhd->gsqhd", score_grad, keys, preferred_element_type=F32
        )
        flat = lambda a: a.reshape(a.shape[:-2] + (PAIR,))
        return q_grad, jnp.concatenate([flat(k_grad) * scale, flat(v_grad)], axis=-1).astype(BF)

    q_grad, joined = lax.scan(step, jnp.zeros(queries.shape, F32), blocks)
    joined = jnp.moveaxis(joined, 0, 2)
    joined = joined.reshape(joined.shape[:2] + (-1, 2 * PAIR))
    owned = lax.psum_scatter(joined, "ctx", scatter_dimension=2, tiled=True)
    return jnp.concatenate([q_grad.reshape(grad.shape).astype(BF), owned], axis=-1)


GATE = 0


class Values:
    def __getattr__(self, name):
        self.__dict__[name] = made = {}
        return made


class Order:
    def __init__(self):
        self.last = None

    def hold(self, *values):
        if self.last is None:
            return values
        return lax.optimization_barrier((*values, self.last))[: len(values)]

    def mark(self, value):
        self.last = value
        return value


def body(
    inputs,
    time_features,
    valid_mask,
    teacher,
    w_time,
    b_time,
    w_query,
    b_query,
    w_key,
    w_value,
    b_value,
    w_output,
    b_output,
    gain_one,
    shift_one,
    w_hidden,
    b_hidden,
    w_down,
    b_down,
    gain_two,
    shift_two,
):
    positions, seqs, width = inputs.shape
    half = width // 2
    chunks = seqs // 2
    columns = w_query.shape[1]
    per_core = columns // PAIR
    pairs = 2 * per_core
    each = w_hidden.shape[1]
    scale = 1.0 / math.sqrt(D // HEADS)
    ctx = lax.axis_size("ctx")
    shards = lax.axis_size("shard")
    by_units = pairs == ctx
    shard = lax.axis_index("shard")
    core = lax.axis_index("tensor") % 2
    spot = lax.axis_index("ctx")
    slot = spot if by_units else jnp.int32(0)
    place = jnp.stack([core, shard, slot, spot]).astype(jnp.int32)
    order = Order()

    def turn(value):
        return jnp.where(
            shard == 0, value, jnp.concatenate([value[..., half:], value[..., :half]], axis=-1)
        )

    def after(value, *others):
        return lax.optimization_barrier((value, *others))[0]

    qkv_mine = pack(place, w_query, w_key, w_value)
    qkv_across = swap_shard(qkv_mine)
    qkv_side = swap_core(qkv_mine)

    bias = jnp.concatenate([b_hidden, b_query, b_value]).reshape(1, -1)
    biases = (bias, swap_core(bias))
    vec = turn(
        jnp.stack([b_output, gain_one, shift_one, b_down, gain_two, shift_two, b_down, b_down])
    )
    valid = valid_mask.T.astype(F32)
    count = jnp.full((8, 128), jnp.sum(valid), F32)
    embed = jnp.dot(time_features, w_time, preferred_element_type=F32) + b_time
    place, vec, valid, embed, count = lax.optimization_barrier((place, vec, valid, embed, count))
    tokens_all = positions * seqs * ctx * shards
    rows = entry(place, inputs, embed)
    low, start = rows[:chunks], rows[chunks:]
    near = sum_ctx(count)
    count = near + swap_shard(after(near, qkv_across))
    out_mine, feed_mine = pack_feed(after(place, low[0], near), w_output, w_hidden, w_down)
    out_side, feed_side = swap_core(out_mine), swap_core(feed_mine)
    order.mark(out_mine)

    qkv_weights = (qkv_mine, qkv_across, qkv_side, swap_core(after(qkv_across, feed_mine)))
    out_across = swap_shard(after(out_mine, qkv_across))
    val = Values()

    def run_project(c):
        (held,) = order.hold(low[c])
        val.slots[c] = project(place, each, held, qkv_weights, biases)
        order.mark(val.slots[c][0])
        if not val.out:
            behind = val.slots[c][0]
            val.feed_across[0] = swap_shard(after(feed_mine, out_across, behind))
            val.out[0] = (out_mine, out_across, out_side, swap_core(after(out_across, behind)))

    def run_teacher():
        (held,) = order.hold(place)
        val.teacher[0] = own_rows(held, teacher)
        order.mark(val.teacher[0][0])

    def run_attend(c):
        slots = val.slots[c]
        if by_units:
            if c > 0 and GATE:
                behind = val.kept[c - 1][0][-GATE:]
                slots = list(lax.optimization_barrier((*slots, *behind))[: len(slots)])
            pieces = swap_ctx(slots)
            *outs, logs = attend(order.hold(*pieces), scale)
            order.mark(logs)
            val.mixed[c] = swap_ctx(outs)
            val.kept[c] = (pieces, logs)
        else:
            value, saved = gathered_forward(jnp.stack(slots)[:, None], scale)
            val.mixed[c] = [value[p, 0] for p in range(pairs)]
            val.kept[c] = saved

    def run_merge(c):
        held = order.hold(*val.mixed[c])
        flat, mine = merge(place, held, val.out[0])
        order.mark(flat)
        val.flat[c] = flat
        val.branch[c] = (mine, swap_outer(mine))
        if not val.feed_weights:
            across = val.feed_across[0]
            side = swap_core(after(across, flat))
            val.feed_weights[0] = (feed_mine, across, feed_side, side)

    def run_feed(c):
        (held,) = order.hold(start[c])
        first, normed, hidden, slope, mine = feed(
            held, *val.branch[c], vec, biases, val.feed_weights[0]
        )
        order.mark(normed)
        val.first[c], val.norm[c], val.hidden[c], val.slope[c] = first, normed, hidden, slope
        val.feed[c] = (mine, swap_outer(mine))

    def run_feed_back(c):
        (held,) = order.hold(val.first[c])
        earlier = val.result[c - 1] if c else vec[None]
        args = (held, *val.feed[c], vec, val.teacher[0][c], valid, count, val.slope[c])
        result, grad, low_grad, pre_grad, mine, two, pre_sum = feed_back(
            place, c, tokens_all, earlier, *args, val.feed_weights[0]
        )
        order.mark(pre_sum)
        val.result[c], val.sum_grad[c], val.feed_low[c] = result, grad, low_grad
        val.pre_grad[c], val.two[c], val.pre_sum[c] = pre_grad, two, pre_sum
        val.back[c] = (mine, swap_outer(mine))
        if c == chunks - 1:
            val.result_other[0] = swap_core(result)

    def run_split(c):
        (held,) = order.hold(val.sum_grad[c])
        first_grad, branch_low, one, *outs = split(
            place, held, *val.back[c], val.first[c], vec, val.out[0]
        )
        order.mark(one)
        val.first_grad[c], val.branch_low[c], val.one[c] = first_grad, branch_low, one
        val.mixed_grad[c] = swap_ctx(outs) if by_units else outs

    def run_attend_back(c):
        if by_units:
            pieces, logs = val.kept[c]
            (logs,) = order.hold(logs)
            outs = attend_back(pieces, val.mixed_grad[c], logs, scale)
            order.mark(outs[0])
            val.qkv_grad[c] = swap_ctx(outs)
        else:
            value = gathered_backward(
                val.kept[c], jnp.stack(val.mixed_grad[c])[:, None], scale
            )
            val.qkv_grad[c] = [value[p, 0] for p in range(pairs)]

    def run_project_back(c):
        held = order.hold(*val.qkv_grad[c])
        flat, mine, qkv_sum, start_sum = project_back(place, held, qkv_weights)
        order.mark(qkv_sum)
        val.qkv_sum[c], val.qkv_flat[c], val.start_sum[c] = qkv_sum, flat, start_sum
        val.last[c] = (mine, swap_outer(mine))

    def run_last(c):
        (held,) = order.hold(val.first_grad[c])
        earlier = val.start[c - 1] if c else held[None]
        val.start[c] = order.mark(last(c, earlier, held, *val.last[c]))
        if c == chunks - 1:
            val.start_other[0] = swap_core(val.start[c])

    def every(values):
        return [values[c] for c in range(chunks)]

    def held_pairs(name):
        if name == "f":
            pairs_of = [(every(val.norm), every(val.pre_grad)), (every(val.feed_low), every(val.hidden))]
        else:
            pairs_of = [(low, every(val.qkv_flat)), (every(val.branch_low), every(val.flat))]
        (lefts, rights), *others = pairs_of
        (first,) = order.hold(lefts[0])
        return [([first, *lefts[1:]], rights), *others]

    def run_core(name):
        val.core[name] = swap_core(order.mark(grad_core(held_pairs(name))))

    def run_shard(name):
        value = order.mark(grad_shard(held_pairs(name), val.core[name]))
        val.shard[name] = swap_shard(value)

    def run_own(name):
        number = ctx if by_units else 1
        own = grad_own(place, held_pairs(name), val.core[name], val.shard[name], number)
        order.mark(own[0])
        if by_units:
            val.pieces[name] = swap_ctx(own)
        else:
            pieces = lax.all_to_all(own[0].reshape(ctx, half // ctx, -1), "ctx", 0, 0)
            val.pieces[name] = [jnp.sum(pieces.astype(F32), axis=0)]

    wide = 3 * columns
    cuts = {
        "f": [[(0, each)], [(each, each)]],
        "a": [[((3 * g + j) * PAIR, PAIR) for g in range(per_core)] for j in range(3)]
        + [[(wide, columns)]],
    }

    def run_total(name):
        val.grad[name] = grad_sum(order.hold(*val.pieces[name]), cuts[name])
        order.mark(val.grad[name][0])

    def run_leave(last):
        (held,) = order.hold(place)
        kind = val.start if last else val.result
        other = val.start_other if last else val.result_other
        val.leave[last] = order.mark(leave(held, kind[chunks - 1], other[0]))

    def run_tally():
        sums = [every(v) for v in (val.two, val.one, val.pre_sum, val.qkv_sum, val.start_sum)]
        sums[0][0] = order.hold(sums[0][0])[0]
        packed = order.mark(tally(place, each, *sums, time_features))
        packed = sum_ctx(packed)
        packed = packed + swap_core(packed)
        packed = packed + swap_shard(packed)
        val.packed[0] = (packed, swap_outer(packed[16 : 16 + shards * seqs]))

    def run_finish():
        (held,) = order.hold(place)
        sizes = (each, 3 * columns, shards * seqs, shards, time_features.shape[1])
        val.finish[0] = finish(held, *sizes, *val.packed[0], count)
        order.mark(val.finish[0][1])

    run_project(0)
    run_teacher()
    run_project(1)
    run_attend(0)
    run_attend(1)
    run_merge(0)
    run_merge(1)
    run_feed(0)
    run_feed(1)
    run_feed_back(0)
    run_feed_back(1)
    run_split(0)
    run_core("f")
    run_shard("f")
    run_split(1)
    run_attend_back(0)
    run_attend_back(1)
    run_leave(False)
    run_project_back(0)
    run_project_back(1)
    run_tally()
    run_core("a")
    run_own("f")
    run_last(0)
    run_shard("a")
    run_last(1)
    run_total("f")
    run_own("a")
    run_leave(True)
    run_finish()
    run_total("a")
    layer_out, grad_inputs = val.leave[False], val.leave[True]
    grad_w_hidden, grad_w_down = val.grad["f"]
    grad_w_query, grad_w_key, grad_w_value, grad_w_output = val.grad["a"]
    grad_w_time, loss, start_sum, hidden_sum, qkv_sum, *rest = val.finish[0]
    qkv_sum = qkv_sum.reshape(per_core, 3, PAIR)
    return (
        layer_out,
        loss.reshape(()),
        grad_inputs,
        grad_w_time,
        start_sum.reshape(-1),
        grad_w_query,
        qkv_sum[:, 0].reshape(-1),
        grad_w_key,
        grad_w_value,
        qkv_sum[:, 2].reshape(-1),
        grad_w_output,
        rest[5].reshape(-1),
        rest[3].reshape(-1),
        rest[4].reshape(-1),
        grad_w_hidden,
        hidden_sum.reshape(-1),
        grad_w_down,
        rest[2].reshape(-1),
        rest[0].reshape(-1),
        rest[1].reshape(-1),
    )


def solution(mesh):
    placed = (
        P("ctx", "shard", None),
        P("shard", None),
        P("ctx", "shard"),
        P("ctx", "shard", None),
        P(),
        P(),
        P("shard", "tensor"),
        P("tensor"),
        P("shard", "tensor"),
        P("shard", "tensor"),
        P("tensor"),
        P("shard", "tensor"),
        P(),
        P(),
        P(),
        P("shard", "tensor"),
        P("tensor"),
        P("shard", "tensor"),
        P(),
        P(),
        P(),
    )
    return jax.shard_map(
        body,
        mesh=mesh,
        in_specs=placed,
        out_specs=(
            P("ctx", "shard", None),
            P(),
            P("ctx", "shard", None),
            P(),
            P(),
            P(("shard", "ctx"), "tensor"),
            P("tensor"),
            P(("shard", "ctx"), "tensor"),
            P(("shard", "ctx"), "tensor"),
            P("tensor"),
            P(("shard", "ctx"), "tensor"),
            P(),
            P(),
            P(),
            P(("shard", "ctx"), "tensor"),
            P("tensor"),
            P(("shard", "ctx"), "tensor"),
            P(),
            P(),
            P(),
        ),
        check_vma=False,
    )
```

```python
from functools import partial
import math

import jax
import jax.numpy as jnp
from jax import lax
from jax.experimental import pallas as pl
from jax.experimental.pallas import tpu as pltpu
from jax.sharding import PartitionSpec as P

D = 1024
HEADS = 16
BF = jnp.bfloat16
F32 = jnp.float32
PAIR = 128
EPS = 1e-05


def contract(left, right, left_dim, right_dim):
    return lax.dot_general(
        left, right, (((left_dim,), (right_dim,)), ((), ())), preferred_element_type=F32
    )


PINNED = False
SCALES = {"project": 0.1, "attend": 1, "merge": 0.1, "feed": 0.1, "feed_back": 0.003, "split": 30, "attend_back": 1, "project_back": 100, "last": 10, "grad_core": 30, "grad_shard": 30, "grad_own": 100, "grad_sum": 30, "tally": 30, "leave": 30, "entry": 10, "own_rows": 10, "pack": 0.01, "pack_feed": 0.01}


def cost(name, flops, nbytes):
    scale = SCALES.get(name, 1)
    return pl.CostEstimate(
        flops=int(flops * scale), bytes_accessed=int(nbytes * scale), transcendentals=0
    )


def swap(value, axis, bit):
    size = lax.axis_size(axis)
    return lax.ppermute(value, axis, [(i, i ^ bit) for i in range(size)])


def swap_core(value):
    return swap(value, "tensor", 1)


def swap_outer(value):
    return swap(value, "tensor", 2)


def swap_shard(value):
    return swap(value, "shard", 1)


def swap_ctx(pieces):
    moved = {d: swap(pieces[d], "ctx", d) for d in reversed(range(1, len(pieces)))}
    return [pieces[0]] + [moved[d] for d in range(1, len(pieces))]


def sum_ctx(value):
    size = lax.axis_size("ctx")
    if size & (size - 1):
        return lax.psum(value, "ctx")
    bit = 1
    while bit < size:
        value = value + swap(value, "ctx", bit)
        bit *= 2
    return value


def sum_tokens(value):
    return sum_ctx(value + swap_shard(value))


def grid_call(kernel, name, grid, ins, outs, work, place, pinned=True):
    args = [a for a, _, _ in ins]
    nbytes = sum(a.size * a.dtype.itemsize for a in args)
    nbytes += sum(math.prod(s) * jnp.dtype(d).itemsize for s, d, _, _ in outs)
    without = lambda f: (lambda *i: f(*i[: len(grid)]))
    if pinned:
        args = [pltpu.with_memory_space_constraint(a, pltpu.HBM) for a in args]
    return pl.pallas_call(
        kernel,
        grid_spec=pltpu.PrefetchScalarGridSpec(
            num_scalar_prefetch=1,
            grid=grid,
            in_specs=[pl.BlockSpec(b, without(f)) for _, b, f in ins],
            out_specs=[pl.BlockSpec(b, without(f)) for _, _, b, f in outs],
        ),
        out_shape=[jax.ShapeDtypeStruct(s, d) for s, d, _, _ in outs],
        cost_estimate=cost(name, work, nbytes),
        compiler_params=pltpu.CompilerParams(vmem_limit_bytes=16 << 20),
        name=name,
    )(place, *args)


def call(kernel, name, args, outs, work, scratch=(), place=None, room=12, pinned=PINNED):
    nbytes = sum(a.size * a.dtype.itemsize for a in args)
    nbytes += sum(math.prod(s) * jnp.dtype(d).itemsize for s, d in outs)
    first = [] if place is None else [place]
    if pinned:
        args = [pltpu.with_memory_space_constraint(a, pltpu.VMEM) for a in args]
    return pl.pallas_call(
        kernel,
        in_specs=[pl.BlockSpec(memory_space=pltpu.SMEM)] * len(first)
        + [pl.BlockSpec(memory_space=pltpu.VMEM)] * len(args),
        out_specs=[pl.BlockSpec(memory_space=pltpu.VMEM)] * len(outs),
        out_shape=[jax.ShapeDtypeStruct(s, d) for s, d in outs],
        scratch_shapes=scratch,
        cost_estimate=cost(name, work, nbytes),
        compiler_params=pltpu.CompilerParams(vmem_limit_bytes=room << 20),
        name=name,
    )(*first, *args)


def whole(array):
    rank = array.ndim
    return (array, array.shape, lambda *i: (0,) * rank)


def turned(value, flip):
    half = value.shape[1] // 2
    return jnp.where(flip == 0, value, jnp.concatenate([value[:, half:], value[:, :half]], axis=1))


def entry_kernel(chunks, place, x_ref, embed_ref, *out_refs):
    core, flip = place[0], place[1]
    x = x_ref[...].astype(F32)
    rows = [x[:, s, :] + embed_ref[s : s + 1, :] for s in range(2 * chunks)]
    for c in range(chunks):
        own = turned(jnp.where(core == 0, rows[c], rows[chunks + c]), flip)
        out_refs[c][...] = own.astype(BF)
        out_refs[chunks + c][...] = own


def entry(place, x, embed):
    positions, seqs, width = x.shape
    chunks = seqs // 2
    block = math.gcd(64, positions)
    return grid_call(
        partial(entry_kernel, chunks),
        "entry",
        (positions // block,),
        [(x, (block, seqs, width), lambda i: (i, 0, 0)), whole(embed)],
        [
            ((positions, width), dtype, (block, width), lambda i: (i, 0))
            for dtype in (BF, F32)
            for _ in range(chunks)
        ],
        4 * x.size,
        place=place,
    )


def own_kernel(chunks, place, x_ref, *out_refs):
    core, flip = place[0], place[1]
    x = x_ref[...].astype(F32)
    for c in range(chunks):
        own = jnp.where(core == 0, x[:, c, :], x[:, chunks + c, :])
        out_refs[c][...] = turned(own, flip).astype(BF)


def own_rows(place, x):
    positions, seqs, width = x.shape
    chunks = seqs // 2
    block = math.gcd(64, positions)
    return grid_call(
        partial(own_kernel, chunks),
        "own_rows",
        (positions // block,),
        [(x, (block, seqs, width), lambda i: (i, 0, 0))],
        [((positions, width), BF, (block, width), lambda i: (i, 0))] * chunks,
        2 * x.size,
        place=place,
    )


def leave_kernel(chunks, dtype, place, own_ref, other_ref, out_ref):
    core, flip = place[0], place[1]
    own = [turned(own_ref[c].astype(F32), flip) for c in range(chunks)]
    other = [turned(other_ref[c].astype(F32), flip) for c in range(chunks)]
    rows = [jnp.where(core == 0, a, b) for a, b in zip(own, other)]
    rows += [jnp.where(core == 0, b, a) for a, b in zip(own, other)]
    out_ref[...] = jnp.stack(rows, axis=1).astype(dtype)


def leave(place, own, other):
    chunks, positions, width = own.shape
    block = math.gcd(64, positions)
    piece = ((chunks, block, width), lambda i: (0, i, 0))
    return grid_call(
        partial(leave_kernel, chunks, own.dtype),
        "leave",
        (positions // block,),
        [(own, *piece), (other, *piece)],
        [
            (
                (positions, 2 * chunks, width),
                own.dtype,
                (block, 2 * chunks, width),
                lambda i: (i, 0, 0),
            )
        ],
        2 * own.size,
        place=place,
        pinned=False,
    )[0]


def pack_kernel(place, q_ref, k_ref, v_ref, out_ref):
    for g in range(q_ref.shape[1] // PAIR):
        for j, ref in enumerate((q_ref, k_ref, v_ref)):
            at = (3 * g + j) * PAIR
            out_ref[:, at : at + PAIR] = ref[:, g * PAIR : (g + 1) * PAIR]


def pack(place, q, k, v):
    rows, columns = q.shape
    return grid_call(
        pack_kernel,
        "pack",
        (1,),
        [whole(q), whole(k), whole(v)],
        [((rows, 3 * columns), BF, (rows, 3 * columns), lambda i: (0, 0))],
        0,
        place,
    )[0]


def pack_feed_kernel(place, out_ref, up_ref, down_ref, copy_ref, both_ref):
    each = up_ref.shape[1]
    copy_ref[...] = out_ref[...]
    both_ref[:, :each] = up_ref[...]
    both_ref[:, each:] = down_ref[...]


def pack_feed(place, out, up, down):
    rows, each = up.shape
    block = math.gcd(128, rows)
    tall = lambda a: (a, (block, a.shape[1]), lambda i: (i, 0))
    return grid_call(
        pack_feed_kernel,
        "pack_feed",
        (rows // block,),
        [tall(out), tall(up), tall(down)],
        [
            (out.shape, BF, (block, out.shape[1]), lambda i: (i, 0)),
            ((rows, 2 * each), BF, (block, 2 * each), lambda i: (i, 0)),
        ],
        0,
        place,
    )


def project_kernel(shift, place, x_ref, a_ref, b_ref, c_ref, d_ref, bias_ref, more_ref, *outs_and_all):
    *outs, pairs_ref = outs_and_all
    half = x_ref.shape[1] // 2
    per_core = len(outs) // 2
    wide = 3 * PAIR
    for core, (top, bottom) in enumerate(((a_ref, b_ref), (c_ref, d_ref))):

        def step(g, carry, core=core, top=top, bottom=bottom):
            at = pl.ds(pl.multiple_of(g * wide, wide), wide)
            value = contract(x_ref[:, :half], top[:, at], 1, 0)
            value += contract(x_ref[:, half:], bottom[:, at], 1, 0)
            pair = core * per_core + g
            bias = (bias_ref, more_ref)[core]
            for j, first in enumerate((shift, None, shift + per_core * PAIR)):
                part = value[:, j * PAIR : (j + 1) * PAIR]
                if first is not None:
                    part += bias[:, pl.ds(pl.multiple_of(first + g * PAIR, PAIR), PAIR)]
                pairs_ref[pair, :, j * PAIR : (j + 1) * PAIR] = part.astype(BF)
            return carry

        lax.fori_loop(0, per_core, step, 0)
    for d, out in enumerate(outs):
        out[...] = pairs_ref[place[2] ^ d]


def project(place, shift, x, weights, biases):
    rows, width = x.shape
    pairs = 2 * weights[0].shape[1] // (3 * PAIR)
    return call(
        partial(project_kernel, shift),
        "project",
        (x, *weights, *biases),
        [((rows, 3 * PAIR), BF)] * pairs,
        2 * rows * width * pairs * 3 * PAIR,
        scratch=[pltpu.VMEM((pairs, rows, 3 * PAIR), BF)],
        place=place,
    )


def project_back_kernel(pairs, place, *refs):
    pieces, (a_ref, b_ref, c_ref, d_ref, flat_ref, out_ref, sums_ref, start_ref, pairs_ref) = (
        refs[:pairs],
        refs[pairs:],
    )
    for d, piece in enumerate(pieces):
        pairs_ref[place[2] ^ d] = piece[...]
    wide = 3 * PAIR
    for p in range(pairs):
        flat_ref[:, p * wide : (p + 1) * wide] = pairs_ref[p]
    half = a_ref.shape[0]
    middle = a_ref.shape[1]
    for at, first, second in ((0, a_ref, c_ref), (half, b_ref, d_ref)):
        value = contract(flat_ref[:, :middle], first[...], 1, 1)
        value += contract(flat_ref[:, middle:], second[...], 1, 1)
        out_ref[:, at : at + half] = value.astype(BF)
        start_ref[:, at : at + half] = sum_rows(value)
    sums_ref[...] = sum_rows(flat_ref[...].astype(F32))


def project_back(place, pieces, weights):
    rows, columns = pieces[0].shape
    pairs = len(pieces)
    width = 2 * weights[0].shape[0]
    return call(
        partial(project_back_kernel, pairs),
        "project_back",
        (*pieces, *weights),
        [
            ((rows, pairs * columns), BF),
            ((rows, width), BF),
            ((1, pairs * columns), F32),
            ((1, width), F32),
        ],
        2 * rows * width * pairs * columns,
        scratch=[pltpu.VMEM((pairs, rows, columns), BF)],
        place=place,
    )


def merge_kernel(pairs, place, *refs):
    pieces, (a_ref, b_ref, c_ref, d_ref, flat_ref, out_ref, pairs_ref) = refs[:pairs], refs[pairs:]
    for d, piece in enumerate(pieces):
        pairs_ref[place[2] ^ d] = piece[...]
    for p in range(pairs):
        flat_ref[:, p * PAIR : (p + 1) * PAIR] = pairs_ref[p]
    half = a_ref.shape[0]
    middle = a_ref.shape[1]
    for at, first, second in ((0, a_ref, c_ref), (half, b_ref, d_ref)):
        value = contract(flat_ref[:, :middle], first[...], 1, 1)
        value += contract(flat_ref[:, middle:], second[...], 1, 1)
        out_ref[:, at : at + half] = value.astype(BF)


def merge(place, pieces, weights):
    rows, columns = pieces[0].shape
    pairs = len(pieces)
    width = 2 * weights[0].shape[0]
    return call(
        partial(merge_kernel, pairs),
        "merge",
        (*pieces, *weights),
        [((rows, pairs * columns), BF), ((rows, width), BF)],
        2 * rows * width * pairs * columns,
        scratch=[pltpu.VMEM((pairs, rows, columns), BF)],
        place=place,
    )


def lanes_of(part):
    lane = lax.broadcasted_iota(jnp.int32, (1, PAIR), 1)
    return lane < PAIR // 2 if part == 0 else lane >= PAIR // 2


def attend_kernel(scale, pieces, *refs):
    ins, outs, (log_ref, mixed_ref) = refs[:pieces], refs[pieces : 2 * pieces], refs[2 * pieces :]
    rows = ins[0].shape[0]
    join = lambda at: jnp.concatenate([ref[:, at : at + PAIR] for ref in ins], axis=0)
    q, k, v = join(0) * BF(scale), join(PAIR), join(2 * PAIR)
    lane = lax.broadcasted_iota(jnp.int32, (1, PAIR), 1)
    mixed_ref[...] = jnp.zeros_like(mixed_ref)

    def head(part, carry):
        lanes = (lane >= PAIR // 2) == (part == 1)
        k_head, v_head = jnp.where(lanes, k, BF(0)), jnp.where(lanes, v, BF(0))
        scores = contract(k_head, q, 1, 1)
        peak = jnp.max(scores, axis=0, keepdims=True)
        weights = jnp.exp(scores - peak)
        total = jnp.sum(weights, axis=0, keepdims=True)
        mixed_ref[...] += contract(v_head, weights.astype(BF), 0, 0) * (1.0 / total)
        log_ref[pl.ds(part, 1), :] = peak + jnp.log(total)
        return carry

    lax.fori_loop(0, 2, head, 0)
    mixed = mixed_ref[...].T.astype(BF)
    for d, out in enumerate(outs):
        out[...] = mixed[d * rows : (d + 1) * rows]


def attend(pieces, scale):
    rows = pieces[0].shape[0]
    length = rows * len(pieces)
    return call(
        partial(attend_kernel, scale, len(pieces)),
        "attend",
        pieces,
        [((rows, PAIR), BF)] * len(pieces) + [((2, length), F32)],
        16 * length * length * PAIR,
        scratch=[pltpu.VMEM((PAIR, length), F32)],
        room=24,
    )


def attend_back_kernel(scale, pieces, *refs):
    ins, grads = refs[:pieces], refs[pieces : 2 * pieces]
    log_ref, outs = refs[2 * pieces], refs[2 * pieces + 1 : 3 * pieces + 1]
    k_sum, v_sum, q_sum, q_ref, grad_ref = refs[3 * pieces + 1 :]
    rows = ins[0].shape[0]
    length = rows * pieces
    join = lambda refs, at: jnp.concatenate([ref[:, at : at + PAIR] for ref in refs], axis=0)
    k, v = join(ins, PAIR), join(ins, 2 * PAIR)
    q_ref[...] = join(ins, 0) * BF(scale)
    grad_ref[...] = join(grads, 0)
    k_sum[...] = jnp.zeros_like(k_sum)
    v_sum[...] = jnp.zeros_like(v_sum)
    q_sum[...] = jnp.zeros_like(q_sum)
    lane = lax.broadcasted_iota(jnp.int32, (1, PAIR), 1)
    block = math.gcd(512, length)

    def step(i, carry):
        part = i % 2
        at = pl.ds(pl.multiple_of(i // 2 * block, block), block)
        lanes = (lane >= PAIR // 2) == (part == 1)
        q, grad = q_ref[at, :], grad_ref[at, :]
        k_head, v_head = jnp.where(lanes, k, BF(0)), jnp.where(lanes, v, BF(0))
        q_head, grad_head = jnp.where(lanes, q, BF(0)), jnp.where(lanes, grad, BF(0))
        probs = jnp.exp(contract(k_head, q, 1, 1) - log_ref[pl.ds(part, 1), at])
        probs_grad = contract(v_head, grad, 1, 1)
        delta = jnp.sum(probs * probs_grad, axis=0, keepdims=True)
        scores_grad = (probs * (probs_grad - delta)).astype(BF)
        v_sum[...] += contract(probs.astype(BF), grad_head, 1, 0)
        k_sum[...] += contract(scores_grad, q_head, 1, 0)
        q_sum[:, at] += contract(k_head, scores_grad, 0, 0)
        return carry

    lax.fori_loop(0, 2 * length // block, step, 0)
    q_grad = (q_sum[...] * scale).T.astype(BF)
    for d, out in enumerate(outs):
        at = slice(d * rows, (d + 1) * rows)
        out[:, 0:PAIR] = q_grad[at, :]
        out[:, PAIR : 2 * PAIR] = k_sum[at, :].astype(BF)
        out[:, 2 * PAIR : 3 * PAIR] = v_sum[at, :].astype(BF)


def attend_back(pieces, grads, logs, scale):
    rows = pieces[0].shape[0]
    length = rows * len(pieces)
    return call(
        partial(attend_back_kernel, scale, len(pieces)),
        "attend_back",
        (*pieces, *grads, logs),
        [((rows, 3 * PAIR), BF)] * len(pieces),
        40 * length * length * PAIR,
        scratch=[pltpu.VMEM((length, PAIR), F32)] * 2
        + [pltpu.VMEM((PAIR, length), F32)]
        + [pltpu.VMEM((length, PAIR), BF)] * 2,
        room=24,
    )


def sum_rows(value):
    return jnp.sum(value, axis=0, keepdims=True)


def normal(value):
    center = jnp.mean(value, axis=-1, keepdims=True)
    offset = value - center
    spread = jnp.mean(offset * offset, axis=-1, keepdims=True)
    inverse = lax.rsqrt(spread + EPS)
    return offset * inverse, inverse


def normal_back(grad, unit, inverse):
    return inverse * (
        grad
        - jnp.mean(grad, axis=-1, keepdims=True)
        - unit * jnp.mean(grad * unit, axis=-1, keepdims=True)
    )


def by_rows(rows, run):
    size = math.gcd(64, rows)

    def step(i, carry):
        run(pl.ds(pl.multiple_of(i * size, size), size))
        return carry

    lax.fori_loop(0, rows // size, step, 0)


def feed_kernel(
    start_ref, mine_ref, theirs_ref, vec_ref, bias_ref, more_ref, a_ref, b_ref, c_ref, d_ref,
    first_ref, low_ref, hidden_ref, slope_ref, out_ref, acc,
):
    def norm(at):
        total = start_ref[at, :] + mine_ref[at, :].astype(F32) + theirs_ref[at, :].astype(F32)
        total += vec_ref[0:1, :]
        first_ref[at, :] = total
        unit, _ = normal(total)
        low_ref[at, :] = (unit * vec_ref[1:2, :] + vec_ref[2:3, :]).astype(BF)

    by_rows(start_ref.shape[0], norm)
    half, each = a_ref.shape[0], a_ref.shape[1] // 2
    size = math.gcd(512, each)
    acc[...] = jnp.zeros_like(acc)
    for core, (top, bottom) in enumerate(((a_ref, b_ref), (c_ref, d_ref))):

        def step(i, carry, core=core, top=top, bottom=bottom):
            here = pl.ds(pl.multiple_of(i * size, size), size)
            at = pl.ds(pl.multiple_of(core * each + i * size, size), size)
            down = pl.ds(pl.multiple_of(each + i * size, size), size)
            pre = contract(low_ref[:, :half], top[:, here], 1, 0)
            pre += contract(low_ref[:, half:], bottom[:, here], 1, 0)
            pre += (bias_ref, more_ref)[core][:, here]
            phi = 0.5 + 0.5 * lax.erf(pre * math.sqrt(0.5))
            hidden = (pre * phi).astype(BF)
            hidden_ref[:, at] = hidden
            bell = jnp.exp(-0.5 * (pre * pre)) * (1.0 / math.sqrt(2.0 * math.pi))
            slope_ref[:, at] = (phi + pre * bell).astype(BF)
            for k, weight in ((0, top), (half, bottom)):
                acc[:, k : k + half] += contract(hidden, weight[:, down], 1, 1)
            return carry

        lax.fori_loop(0, each // size, step, 0)
    out_ref[...] = acc[...].astype(BF)


def feed(start, mine, theirs, vec, biases, weights):
    rows, width = start.shape
    units = weights[0].shape[1]
    return call(
        feed_kernel,
        "feed",
        (start, mine, theirs, vec, *biases, *weights),
        [
            ((rows, width), F32),
            ((rows, width), BF),
            ((rows, units), BF),
            ((rows, units), BF),
            ((rows, width), BF),
        ],
        4 * rows * width * units,
        scratch=[pltpu.VMEM((rows, width), F32)],
    )


def feed_back_kernel(
    valid_row, tokens, place, earlier_ref, first_ref, mine_ref, theirs_ref, vec_ref, teacher_ref, valid_ref, count_ref, slope_ref,
    a_ref, b_ref, c_ref, d_ref, result_ref, grad_ref, low_ref, pre_ref, out_ref, sums_ref, pre_sums_ref, acc, valid_sums,
):
    second = valid_ref.shape[0] // 2 + valid_row
    valid = jnp.where(
        place[0] == 0, valid_ref[valid_row : valid_row + 1, :], valid_ref[second : second + 1, :]
    )
    for c in range(valid_row):
        result_ref[c] = earlier_ref[c]
    valid_sums[...] = jnp.broadcast_to(valid, (PAIR, valid.shape[1])).T
    sums_ref[...] = jnp.zeros_like(sums_ref)
    factor = 2.0 * tokens / count_ref[0:1, 0:1]

    def norm(at):
        valid = valid_sums[at, 0:1]
        unit, _ = normal(first_ref[at, :])
        normed = unit * vec_ref[1:2, :] + vec_ref[2:3, :]
        total = normed + mine_ref[at, :].astype(F32) + theirs_ref[at, :].astype(F32) + vec_ref[3:4, :]
        unit, inverse = normal(total)
        result = unit * vec_ref[4:5, :] + vec_ref[5:6, :]
        result_ref[valid_row, at, :] = result.astype(BF)
        error = result - teacher_ref[at, :].astype(F32)
        result_grad = valid * factor * error
        grad = normal_back(result_grad * vec_ref[4:5, :], unit, inverse)
        grad_ref[at, :] = grad
        low = grad.astype(BF)
        low_ref[at, :] = low
        sums_ref[0:1, :] += sum_rows(result_grad * unit)
        sums_ref[1:2, :] += sum_rows(result_grad)
        sums_ref[2:3, :] += sum_rows(low.astype(F32))
        sums_ref[3:4, :] += sum_rows(valid * error * error)

    by_rows(first_ref.shape[0], norm)
    half, each = a_ref.shape[0], a_ref.shape[1] // 2
    size = math.gcd(512, each)
    acc[...] = jnp.zeros_like(acc)
    for core, (top, bottom) in enumerate(((a_ref, b_ref), (c_ref, d_ref))):

        def step(i, carry, core=core, top=top, bottom=bottom):
            here = pl.ds(pl.multiple_of(i * size, size), size)
            at = pl.ds(pl.multiple_of(core * each + i * size, size), size)
            down = pl.ds(pl.multiple_of(each + i * size, size), size)
            value = contract(low_ref[:, :half], top[:, down], 1, 0)
            value += contract(low_ref[:, half:], bottom[:, down], 1, 0)
            pre_grad = (value * slope_ref[:, at].astype(F32)).astype(BF)
            pre_ref[:, at] = pre_grad
            pre_sums_ref[:, at] = sum_rows(pre_grad.astype(F32))
            for k, weight in ((0, top), (half, bottom)):
                acc[:, k : k + half] += contract(pre_grad, weight[:, here], 1, 1)
            return carry

        lax.fori_loop(0, each // size, step, 0, unroll=True)
    out_ref[...] = acc[...].astype(BF)


def feed_back(place, row, tokens, earlier, first, mine, theirs, vec, teacher, valid, count, slope, weights):
    rows, width = first.shape
    units = slope.shape[1]
    return call(
        partial(feed_back_kernel, row, tokens),
        "feed_back",
        (earlier, first, mine, theirs, vec, teacher, valid, count, slope, *weights),
        [
            ((row + 1, rows, width), BF),
            ((rows, width), F32),
            ((rows, width), BF),
            ((rows, units), BF),
            ((rows, width), BF),
            ((8, width), F32),
            ((1, units), F32),
        ],
        4 * rows * width * units,
        scratch=[pltpu.VMEM((rows, width), F32), pltpu.VMEM((rows, PAIR), F32)],
        place=place,
    )


def split_kernel(place, grad_ref, mine_ref, theirs_ref, first_ref, vec_ref, a_ref, b_ref, c_ref, d_ref, out_ref, low_ref, sums_ref, *outs_and_all):
    *outs, pairs_ref = outs_and_all
    sums_ref[...] = jnp.zeros_like(sums_ref)

    def norm(at):
        grad = grad_ref[at, :] + mine_ref[at, :].astype(F32) + theirs_ref[at, :].astype(F32)
        unit, inverse = normal(first_ref[at, :])
        out = normal_back(grad * vec_ref[1:2, :], unit, inverse)
        out_ref[at, :] = out
        low = out.astype(BF)
        low_ref[at, :] = low
        sums_ref[0:1, :] += sum_rows(grad * unit)
        sums_ref[1:2, :] += sum_rows(grad)
        sums_ref[2:3, :] += sum_rows(low.astype(F32))
        sums_ref[3:4, :] += sum_rows(out)

    by_rows(grad_ref.shape[0], norm)
    half = a_ref.shape[0]
    per_core = len(outs) // 2
    for core, (top, bottom) in enumerate(((a_ref, b_ref), (c_ref, d_ref))):
        mixed = contract(low_ref[:, :half], top[...], 1, 0)
        mixed += contract(low_ref[:, half:], bottom[...], 1, 0)
        mixed = mixed.astype(BF)
        for p in range(per_core):
            pairs_ref[core * per_core + p] = mixed[:, p * PAIR : (p + 1) * PAIR]
    for d, piece in enumerate(outs):
        piece[...] = pairs_ref[place[2] ^ d]


def split(place, grad, mine, theirs, first, vec, weights):
    rows, width = grad.shape
    pairs = 2 * weights[0].shape[1] // PAIR
    return call(
        split_kernel,
        "split",
        (grad, mine, theirs, first, vec, *weights),
        [((rows, width), F32), ((rows, width), BF), ((8, width), F32)]
        + [((rows, PAIR), BF)] * pairs,
        2 * rows * width * pairs * PAIR,
        scratch=[pltpu.VMEM((pairs, rows, PAIR), BF)],
        place=place,
    )


def last_kernel(row, earlier_ref, grad_ref, mine_ref, theirs_ref, out_ref):
    for c in range(row):
        out_ref[c] = earlier_ref[c]
    out_ref[row] = grad_ref[...] + mine_ref[...].astype(F32) + theirs_ref[...].astype(F32)


def last(row, earlier, grad, mine, theirs):
    rows, width = grad.shape
    return call(
        partial(last_kernel, row),
        "last",
        (earlier, grad, mine, theirs),
        [((row + 1, rows, width), F32)],
        4 * rows * width,
    )[0]


def tally_kernel(chunks, each, place, *refs):
    two, one = refs[:chunks], refs[chunks : 2 * chunks]
    pre, qkv = refs[2 * chunks : 3 * chunks], refs[3 * chunks : 4 * chunks]
    start, (features_ref, out_ref) = refs[4 * chunks : 5 * chunks], refs[5 * chunks :]
    core, flip, spot = place[0], place[1], place[3]
    add = lambda parts: sum(parts[1:], parts[0])
    out_ref[...] = jnp.zeros_like(out_ref)
    out_ref[0:4, :] = turned(add([ref[0:4, :] for ref in two]), flip)
    out_ref[4:7, :] = turned(add([ref[0:3, :] for ref in one]), flip)
    pre = add([ref[...] for ref in pre])
    qkv = add([ref[...] for ref in qkv])
    size = qkv.shape[1] // 2
    for slot in range(2):
        mine = core == slot
        out_ref[8 + slot : 9 + slot, :] = jnp.where(mine, pre[:, :each], pre[:, each:])
        out_ref[10 + slot : 11 + slot, :size] = jnp.where(mine, qkv[:, :size], qkv[:, size:])
    seqs = 2 * chunks
    features = features_ref[...].astype(F32)
    wide = features.shape[1]
    for s in range(2):
        here = jnp.logical_and(jnp.logical_and(core == 0, spot == 0), flip == s)
        for k in range(seqs):
            value = jnp.where(here, features[k : k + 1, :], 0.0)
            out_ref[12 + s : 13 + s, k * wide : (k + 1) * wide] = value
    for s in range(2 * seqs):
        here = jnp.logical_and(flip == s // seqs, core == s % seqs // chunks)
        row = turned(0.5 * one[s % chunks][3:4, :] + start[s % chunks][...], flip)
        out_ref[16 + s : 17 + s, :] = jnp.where(here, row, 0.0)


def tally(place, each, two, one, pre, qkv, start, features):
    rows = -(-(16 + 2 * features.shape[0]) // 8) * 8
    return call(
        partial(tally_kernel, len(two), each),
        "tally",
        (*two, *one, *pre, *qkv, *start, features),
        [((rows, two[0].shape[1]), F32)],
        0,
        place=place,
    )[0]


def grad_sum_kernel(pieces, cuts, *refs):
    total = refs[0][...].astype(F32)
    for ref in refs[1:pieces]:
        total = total + ref[...].astype(F32)
    for out, parts in zip(refs[pieces:], cuts):
        at = 0
        for start, size in parts:
            out[:, at : at + size] = total[:, start : start + size]
            at += size


def grad_sum(pieces, cuts):
    rows = pieces[0].shape[0]
    return call(
        partial(grad_sum_kernel, len(pieces), cuts),
        "grad_sum",
        pieces,
        [((rows, sum(size for _, size in parts)), F32) for parts in cuts],
        len(pieces) * pieces[0].size,
    )


def finish_kernel(each, size, shards, place, packed_ref, other_ref, count_ref, time_ref, loss_ref, start_ref, hidden_ref, qkv_ref, *outs_and_all):
    *outs, all_ref = outs_and_all
    seqs = all_ref.shape[0]
    wide = all_ref.shape[1]
    per_row = seqs // shards
    for s in range(seqs):
        k = s % per_row
        row = 12 + s // per_row
        all_ref[s : s + 1, :] = packed_ref[row : row + 1, k * wide : (k + 1) * wide]
    grads = packed_ref[16 : 16 + seqs, :] + other_ref[...]
    time_ref[...] = lax.dot_general(
        all_ref[...],
        grads,
        (((0,), (0,)), ((), ())),
        precision=lax.Precision.HIGHEST,
        preferred_element_type=F32,
    )
    start_ref[...] = sum_rows(grads)
    total = jnp.sum(packed_ref[3:4, :], axis=1, keepdims=True)
    loss_ref[...] = total / (packed_ref.shape[1] * count_ref[0:1, 0:1])
    first = place[0] == 0
    hidden_ref[...] = jnp.where(first, packed_ref[8:9, :], packed_ref[9:10, :])[:, :each]
    qkv_ref[...] = jnp.where(first, packed_ref[10:11, :], packed_ref[11:12, :])[:, :size]
    for out, row in zip(outs, (0, 1, 2, 4, 5, 6)):
        out[...] = packed_ref[row : row + 1, :]


def finish(place, each, size, seqs, shards, wide, packed, other, count):
    width = packed.shape[1]
    return call(
        partial(finish_kernel, each, size, shards),
        "finish",
        (packed, other, count),
        [((wide, width), F32), ((1, 1), F32), ((1, width), F32), ((1, each), F32), ((1, size), F32)]
        + [((1, width), F32)] * 6,
        0,
        scratch=[pltpu.VMEM((seqs, wide), F32)],
        place=place,
    )


def token_sum(lefts, rights, rows, columns):
    total = None
    for left, right in zip(lefts, rights):
        term = contract(left[:, rows], right[:, columns], 0, 0)
        total = term if total is None else total + term
    return total


def each_weight(weights, refs):
    at, column, out = 0, 0, []
    for chunks, columns in weights:
        out.append((refs[at : at + chunks], refs[at + chunks : at + 2 * chunks], column, columns))
        at += 2 * chunks
        column += columns
    return out, refs[at:]


def weight_args(weights):
    args = [a for lefts, rights in weights for a in (*lefts, *rights)]
    shapes = [(len(lefts), rights[0].shape[1] // 2) for lefts, rights in weights]
    tokens = sum(a.shape[0] for a in weights[0][0])
    return args, shapes, weights[0][0][0].shape[1], sum(c for _, c in shapes), tokens


def grad_core_kernel(weights, *refs):
    weights, (out_ref,) = each_weight(weights, refs)
    rows = out_ref.shape[0]
    step = math.gcd(512, rows)

    def part(i, carry):
        at = pl.ds(pl.multiple_of(i * step, step), step)
        for lefts, rights, first, columns in weights:
            value = token_sum(lefts, rights, at, slice(columns, 2 * columns))
            out_ref[at, first : first + columns] = value.astype(BF)
        return carry

    lax.fori_loop(0, rows // step, part, 0)


def grad_core(weights):
    args, shapes, rows, columns, tokens = weight_args(weights)
    return call(
        partial(grad_core_kernel, shapes),
        "grad_core",
        args,
        [((rows, columns), BF)],
        2 * tokens * rows * columns,
    )[0]


def grad_shard_kernel(weights, *refs):
    weights, (core_ref, out_ref) = each_weight(weights, refs)
    half = out_ref.shape[0]
    size = math.gcd(256, half)

    def step(i, carry):
        at = pl.ds(pl.multiple_of(i * size, size), size)
        far = pl.ds(pl.multiple_of(half + i * size, size), size)
        for lefts, rights, first, columns in weights:
            here = slice(first, first + columns)
            value = token_sum(lefts, rights, far, slice(0, columns))
            out_ref[at, here] = (value + core_ref[far, here].astype(F32)).astype(BF)
        return carry

    lax.fori_loop(0, half // size, step, 0)


def grad_shard(weights, core):
    args, shapes, rows, columns, tokens = weight_args(weights)
    return call(
        partial(grad_shard_kernel, shapes),
        "grad_shard",
        (*args, core),
        [((rows // 2, columns), BF)],
        tokens * rows * columns,
    )[0]


def grad_own_kernel(weights, place, *refs):
    weights, (core_ref, shard_ref, *outs, acc) = each_weight(weights, refs)
    half = acc.shape[0]
    size = math.gcd(256, half)

    def step(i, carry):
        at = pl.ds(pl.multiple_of(i * size, size), size)
        for lefts, rights, first, columns in weights:
            here = slice(first, first + columns)
            value = token_sum(lefts, rights, at, slice(0, columns))
            acc[at, here] = value + core_ref[at, here].astype(F32) + shard_ref[at, here].astype(F32)
        return carry

    lax.fori_loop(0, half // size, step, 0)
    rows = outs[0].shape[0]
    if len(outs) == 1:
        outs[0][...] = acc[...].astype(BF)
    else:
        for d, out in enumerate(outs):
            at = pl.multiple_of((place[2] ^ d) * rows, rows)
            out[...] = acc[pl.ds(at, rows), :].astype(out.dtype)


def grad_own(place, weights, core, shard, pieces):
    args, shapes, rows, columns, tokens = weight_args(weights)
    half = rows // 2
    return call(
        partial(grad_own_kernel, shapes),
        "grad_own",
        (*args, core, shard),
        [
            ((half // pieces, columns), F32 if pieces > 1 and d == 0 else BF)
            for d in range(pieces)
        ],
        tokens * rows * columns,
        scratch=[pltpu.VMEM((half, columns), F32)],
        place=place,
        room=16,
    )


def heads_of(value):
    return value.reshape(value.shape[:-1] + (2, PAIR // 2))


def gathered_forward(qkv, scale):
    queries = heads_of(qkv[..., :PAIR])
    both = lax.all_gather(qkv[..., PAIR:], "ctx", axis=2, tiled=True)
    length = both.shape[2]
    block = math.gcd(length, 512)
    blocks = jnp.moveaxis(both.reshape(both.shape[:2] + (length // block, block, 2 * PAIR)), 2, 0)
    shape = queries.shape[:-1]

    def step(carry, piece):
        peak, total, summed = carry
        keys, values = heads_of(piece[..., :PAIR]), heads_of(piece[..., PAIR:])
        scores = jnp.einsum("gsqhd,gskhd->gsqhk", queries, keys, preferred_element_type=F32) * scale
        new_peak = jnp.maximum(peak, jnp.max(scores, axis=-1))
        fade = jnp.exp(peak - new_peak)
        weights = jnp.exp(scores - new_peak[..., None])
        total = total * fade + jnp.sum(weights, axis=-1)
        summed = summed * fade[..., None] + jnp.einsum(
            "gsqhk,gskhd->gsqhd", weights.astype(BF), values, preferred_element_type=F32
        )
        return (new_peak, total, summed), None

    first = (
        jnp.full(shape, -1e30, F32),
        jnp.zeros(shape, F32),
        jnp.zeros(queries.shape, F32),
    )
    (peak, total, summed), _ = lax.scan(step, first, blocks)
    attended = summed / total[..., None]
    mixed = attended.reshape(qkv.shape[:-1] + (PAIR,)).astype(BF)
    return mixed, (queries, blocks, peak + jnp.log(total), attended)


def gathered_backward(saved, grad, scale):
    queries, blocks, logs, attended = saved
    out_grad = heads_of(grad)
    delta = jnp.sum(out_grad.astype(F32) * attended, axis=-1)

    def step(q_grad, piece):
        keys, values = heads_of(piece[..., :PAIR]), heads_of(piece[..., PAIR:])
        scores = jnp.einsum("gsqhd,gskhd->gsqhk", queries, keys, preferred_element_type=F32) * scale
        weights = jnp.exp(scores - logs[..., None])
        weight_grad = jnp.einsum(
            "gsqhd,gskhd->gsqhk", out_grad, values, preferred_element_type=F32
        )
        score_grad = (weights * (weight_grad - delta[..., None])).astype(BF)
        v_grad = jnp.einsum(
            "gsqhk,gsqhd->gskhd", weights.astype(BF), out_grad, preferred_element_type=F32
        )
        k_grad = jnp.einsum("gsqhk,gsqhd->gskhd", score_grad, queries, preferred_element_type=F32)
        q_grad = q_grad + scale * jnp.einsum(
            "gsqhk,gskhd->gsqhd", score_grad, keys, preferred_element_type=F32
        )
        flat = lambda a: a.reshape(a.shape[:-2] + (PAIR,))
        return q_grad, jnp.concatenate([flat(k_grad) * scale, flat(v_grad)], axis=-1).astype(BF)

    q_grad, joined = lax.scan(step, jnp.zeros(queries.shape, F32), blocks)
    joined = jnp.moveaxis(joined, 0, 2)
    joined = joined.reshape(joined.shape[:2] + (-1, 2 * PAIR))
    owned = lax.psum_scatter(joined, "ctx", scatter_dimension=2, tiled=True)
    return jnp.concatenate([q_grad.reshape(grad.shape).astype(BF), owned], axis=-1)


GATE = 0


class Values:
    def __getattr__(self, name):
        self.__dict__[name] = made = {}
        return made


class Order:
    def __init__(self):
        self.last = None

    def hold(self, *values):
        if self.last is None:
            return values
        return lax.optimization_barrier((*values, self.last))[: len(values)]

    def mark(self, value):
        self.last = value
        return value


def body(
    inputs,
    time_features,
    valid_mask,
    teacher,
    w_time,
    b_time,
    w_query,
    b_query,
    w_key,
    w_value,
    b_value,
    w_output,
    b_output,
    gain_one,
    shift_one,
    w_hidden,
    b_hidden,
    w_down,
    b_down,
    gain_two,
    shift_two,
):
    positions, seqs, width = inputs.shape
    half = width // 2
    chunks = seqs // 2
    columns = w_query.shape[1]
    per_core = columns // PAIR
    pairs = 2 * per_core
    each = w_hidden.shape[1]
    scale = 1.0 / math.sqrt(D // HEADS)
    ctx = lax.axis_size("ctx")
    shards = lax.axis_size("shard")
    by_units = pairs == ctx
    shard = lax.axis_index("shard")
    core = lax.axis_index("tensor") % 2
    spot = lax.axis_index("ctx")
    slot = spot if by_units else jnp.int32(0)
    place = jnp.stack([core, shard, slot, spot]).astype(jnp.int32)
    order = Order()

    def turn(value):
        return jnp.where(
            shard == 0, value, jnp.concatenate([value[..., half:], value[..., :half]], axis=-1)
        )

    def after(value, *others):
        return lax.optimization_barrier((value, *others))[0]

    qkv_mine = pack(place, w_query, w_key, w_value)
    qkv_across = swap_shard(qkv_mine)
    qkv_side = swap_core(qkv_mine)

    bias = jnp.concatenate([b_hidden, b_query, b_value]).reshape(1, -1)
    biases = (bias, swap_core(bias))
    vec = turn(
        jnp.stack([b_output, gain_one, shift_one, b_down, gain_two, shift_two, b_down, b_down])
    )
    valid = valid_mask.T.astype(F32)
    count = jnp.full((8, 128), jnp.sum(valid), F32)
    embed = jnp.dot(time_features, w_time, preferred_element_type=F32) + b_time
    place, vec, valid, embed, count = lax.optimization_barrier((place, vec, valid, embed, count))
    tokens_all = positions * seqs * ctx * shards
    rows = entry(place, inputs, embed)
    low, start = rows[:chunks], rows[chunks:]
    near = sum_ctx(count)
    count = near + swap_shard(after(near, qkv_across))
    out_mine, feed_mine = pack_feed(after(place, low[0], near), w_output, w_hidden, w_down)
    out_side, feed_side = swap_core(out_mine), swap_core(feed_mine)
    order.mark(out_mine)

    qkv_weights = (qkv_mine, qkv_across, qkv_side, swap_core(after(qkv_across, feed_mine)))
    out_across = swap_shard(after(out_mine, qkv_across))
    val = Values()

    def run_project(c):
        (held,) = order.hold(low[c])
        val.slots[c] = project(place, each, held, qkv_weights, biases)
        order.mark(val.slots[c][0])
        if not val.out:
            behind = val.slots[c][0]
            val.feed_across[0] = swap_shard(after(feed_mine, out_across, behind))
            val.out[0] = (out_mine, out_across, out_side, swap_core(after(out_across, behind)))

    def run_teacher():
        (held,) = order.hold(place)
        val.teacher[0] = own_rows(held, teacher)
        order.mark(val.teacher[0][0])

    def run_attend(c):
        slots = val.slots[c]
        if by_units:
            if c > 0 and GATE:
                behind = val.kept[c - 1][0][-GATE:]
                slots = list(lax.optimization_barrier((*slots, *behind))[: len(slots)])
            pieces = swap_ctx(slots)
            *outs, logs = attend(order.hold(*pieces), scale)
            order.mark(logs)
            val.mixed[c] = swap_ctx(outs)
            val.kept[c] = (pieces, logs)
        else:
            value, saved = gathered_forward(jnp.stack(slots)[:, None], scale)
            val.mixed[c] = [value[p, 0] for p in range(pairs)]
            val.kept[c] = saved

    def run_merge(c):
        held = order.hold(*val.mixed[c])
        flat, mine = merge(place, held, val.out[0])
        order.mark(flat)
        val.flat[c] = flat
        val.branch[c] = (mine, swap_outer(mine))
        if not val.feed_weights:
            across = val.feed_across[0]
            side = swap_core(after(across, flat))
            val.feed_weights[0] = (feed_mine, across, feed_side, side)

    def run_feed(c):
        (held,) = order.hold(start[c])
        first, normed, hidden, slope, mine = feed(
            held, *val.branch[c], vec, biases, val.feed_weights[0]
        )
        order.mark(normed)
        val.first[c], val.norm[c], val.hidden[c], val.slope[c] = first, normed, hidden, slope
        val.feed[c] = (mine, swap_outer(mine))

    def run_feed_back(c):
        (held,) = order.hold(val.first[c])
        earlier = val.result[c - 1] if c else vec[None]
        args = (held, *val.feed[c], vec, val.teacher[0][c], valid, count, val.slope[c])
        result, grad, low_grad, pre_grad, mine, two, pre_sum = feed_back(
            place, c, tokens_all, earlier, *args, val.feed_weights[0]
        )
        order.mark(pre_sum)
        val.result[c], val.sum_grad[c], val.feed_low[c] = result, grad, low_grad
        val.pre_grad[c], val.two[c], val.pre_sum[c] = pre_grad, two, pre_sum
        val.back[c] = (mine, swap_outer(mine))
        if c == chunks - 1:
            val.result_other[0] = swap_core(result)

    def run_split(c):
        (held,) = order.hold(val.sum_grad[c])
        first_grad, branch_low, one, *outs = split(
            place, held, *val.back[c], val.first[c], vec, val.out[0]
        )
        order.mark(one)
        val.first_grad[c], val.branch_low[c], val.one[c] = first_grad, branch_low, one
        val.mixed_grad[c] = swap_ctx(outs) if by_units else outs

    def run_attend_back(c):
        if by_units:
            pieces, logs = val.kept[c]
            (logs,) = order.hold(logs)
            outs = attend_back(pieces, val.mixed_grad[c], logs, scale)
            order.mark(outs[0])
            val.qkv_grad[c] = swap_ctx(outs)
        else:
            value = gathered_backward(
                val.kept[c], jnp.stack(val.mixed_grad[c])[:, None], scale
            )
            val.qkv_grad[c] = [value[p, 0] for p in range(pairs)]

    def run_project_back(c):
        held = order.hold(*val.qkv_grad[c])
        flat, mine, qkv_sum, start_sum = project_back(place, held, qkv_weights)
        order.mark(qkv_sum)
        val.qkv_sum[c], val.qkv_flat[c], val.start_sum[c] = qkv_sum, flat, start_sum
        val.last[c] = (mine, swap_outer(mine))

    def run_last(c):
        (held,) = order.hold(val.first_grad[c])
        earlier = val.start[c - 1] if c else held[None]
        val.start[c] = order.mark(last(c, earlier, held, *val.last[c]))
        if c == chunks - 1:
            val.start_other[0] = swap_core(val.start[c])

    def every(values):
        return [values[c] for c in range(chunks)]

    def held_pairs(name):
        if name == "f":
            pairs_of = [(every(val.norm), every(val.pre_grad)), (every(val.feed_low), every(val.hidden))]
        else:
            pairs_of = [(low, every(val.qkv_flat)), (every(val.branch_low), every(val.flat))]
        (lefts, rights), *others = pairs_of
        (first,) = order.hold(lefts[0])
        return [([first, *lefts[1:]], rights), *others]

    def run_core(name):
        val.core[name] = swap_core(order.mark(grad_core(held_pairs(name))))

    def run_shard(name):
        value = order.mark(grad_shard(held_pairs(name), val.core[name]))
        val.shard[name] = swap_shard(value)

    def run_own(name):
        number = ctx if by_units else 1
        own = grad_own(place, held_pairs(name), val.core[name], val.shard[name], number)
        order.mark(own[0])
        if by_units:
            val.pieces[name] = swap_ctx(own)
        else:
            pieces = lax.all_to_all(own[0].reshape(ctx, half // ctx, -1), "ctx", 0, 0)
            val.pieces[name] = [jnp.sum(pieces.astype(F32), axis=0)]

    wide = 3 * columns
    cuts = {
        "f": [[(0, each)], [(each, each)]],
        "a": [[((3 * g + j) * PAIR, PAIR) for g in range(per_core)] for j in range(3)]
        + [[(wide, columns)]],
    }

    def run_total(name):
        val.grad[name] = grad_sum(order.hold(*val.pieces[name]), cuts[name])
        order.mark(val.grad[name][0])

    def run_leave(last):
        (held,) = order.hold(place)
        kind = val.start if last else val.result
        other = val.start_other if last else val.result_other
        val.leave[last] = order.mark(leave(held, kind[chunks - 1], other[0]))

    def run_tally():
        sums = [every(v) for v in (val.two, val.one, val.pre_sum, val.qkv_sum, val.start_sum)]
        sums[0][0] = order.hold(sums[0][0])[0]
        packed = order.mark(tally(place, each, *sums, time_features))
        packed = sum_ctx(packed)
        packed = packed + swap_core(packed)
        packed = packed + swap_shard(packed)
        val.packed[0] = (packed, swap_outer(packed[16 : 16 + shards * seqs]))

    def run_finish():
        (held,) = order.hold(place)
        sizes = (each, 3 * columns, shards * seqs, shards, time_features.shape[1])
        val.finish[0] = finish(held, *sizes, *val.packed[0], count)
        order.mark(val.finish[0][1])

    run_project(0)
    run_teacher()
    run_project(1)
    run_attend(0)
    run_attend(1)
    run_merge(0)
    run_merge(1)
    run_feed(0)
    run_feed(1)
    run_feed_back(0)
    run_feed_back(1)
    run_split(0)
    run_core("f")
    run_shard("f")
    run_split(1)
    run_attend_back(0)
    run_attend_back(1)
    run_leave(False)
    run_project_back(0)
    run_project_back(1)
    run_tally()
    run_core("a")
    run_own("f")
    run_last(0)
    run_shard("a")
    run_last(1)
    run_total("f")
    run_own("a")
    run_leave(True)
    run_finish()
    run_total("a")
    layer_out, grad_inputs = val.leave[False], val.leave[True]
    grad_w_hidden, grad_w_down = val.grad["f"]
    grad_w_query, grad_w_key, grad_w_value, grad_w_output = val.grad["a"]
    grad_w_time, loss, start_sum, hidden_sum, qkv_sum, *rest = val.finish[0]
    qkv_sum = qkv_sum.reshape(per_core, 3, PAIR)
    return (
        layer_out,
        loss.reshape(()),
        grad_inputs,
        grad_w_time,
        start_sum.reshape(-1),
        grad_w_query,
        qkv_sum[:, 0].reshape(-1),
        grad_w_key,
        grad_w_value,
        qkv_sum[:, 2].reshape(-1),
        grad_w_output,
        rest[5].reshape(-1),
        rest[3].reshape(-1),
        rest[4].reshape(-1),
        grad_w_hidden,
        hidden_sum.reshape(-1),
        grad_w_down,
        rest[2].reshape(-1),
        rest[0].reshape(-1),
        rest[1].reshape(-1),
    )


def solution(mesh):
    placed = (
        P("ctx", "shard", None),
        P("shard", None),
        P("ctx", "shard"),
        P("ctx", "shard", None),
        P(),
        P(),
        P("shard", "tensor"),
        P("tensor"),
        P("shard", "tensor"),
        P("shard", "tensor"),
        P("tensor"),
        P("shard", "tensor"),
        P(),
        P(),
        P(),
        P("shard", "tensor"),
        P("tensor"),
        P("shard", "tensor"),
        P(),
        P(),
        P(),
    )
    return jax.shard_map(
        body,
        mesh=mesh,
        in_specs=placed,
        out_specs=(
            P("ctx", "shard", None),
            P(),
            P("ctx", "shard", None),
            P(),
            P(),
            P(("shard", "ctx"), "tensor"),
            P("tensor"),
            P(("shard", "ctx"), "tensor"),
            P(("shard", "ctx"), "tensor"),
            P("tensor"),
            P(("shard", "ctx"), "tensor"),
            P(),
            P(),
            P(),
            P(("shard", "ctx"), "tensor"),
            P("tensor"),
            P(("shard", "ctx"), "tensor"),
            P(),
            P(),
            P(),
        ),
        check_vma=False,
    )
```
